32 devices in a mesh: replica: 4 (over y, x), shard: 8 (over z, core).
Axes of the slice: x: 2, y: 2, z: 4, core: 2. Of those that a mesh axis runs over, the one named last changes fastest.
Arguments:
- tokens: bfloat16 [4096, 2048], P(('replica', 'shard')), may hold values from -6 to 6
- ln_gain: float32 [2048], replicated, may hold values from 0.5 to 1.5
- ln_bias: float32 [2048], replicated, may hold values from -2 to 2
- w_in: bfloat16 [2048, 14336], P('shard'), may hold values from -0.125 to 0.125
- b_in: float32 [14336], replicated, may hold values from -3 to 3
- w_out: bfloat16 [10240, 2048], P('shard'), may hold values from -0.70710678 to 0.70710678
- b_out: float32 [2048], replicated, may hold values from -3 to 3
- cotangent: bfloat16 [4096, 2048], P(('replica', 'shard')), may hold values from -6 to 6
Outputs:
- block_out: bfloat16 [4096, 2048], P(('replica', 'shard'))
- grad_tokens: bfloat16 [4096, 2048], P(('replica', 'shard'))
- grad_ln_gain: float32 [2048], replicated
- grad_ln_bias: float32 [2048], replicated
- grad_w_in: float32 [2048, 14336], P('shard')
- grad_b_in: float32 [14336], replicated
- grad_w_out: float32 [10240, 2048], P('shard')
- grad_b_out: float32 [2048], replicated
The draws below stay inside these ranges and needn't reach their ends.
All inputs are finite; a program needn't handle non-finite values.
Results may differ from the reference program's by a relative error of at most 0.03.
Values may be sent and summed in bfloat16 or wider, within the bound.
A program may use at most 384 MiB of HBM per device.

```python
import math
import jax
import jax.numpy as jnp
from jax import lax

D = 2048
HEADS = 32
HEAD_DIM = 64
ROT = 32
FF = 8192
SEQ_LEN = 1024
TOKENS = 4096


def draw_w_out(key, part):
    row_index = jnp.arange(D + FF)[:, None]
    row_scale = jnp.where(row_index < D, 8.0 / math.sqrt(D), 1.0 / math.sqrt(FF))
    base = jnp.clip(jax.random.normal(key, (D + FF, D), jnp.float32), -4.0, 4.0)
    return (base * row_scale).astype(jnp.bfloat16)


def levels(own_key, shape, split, smallest, top_value):
    def one(position, parts):
        draws = jax.random.uniform(jax.random.fold_in(jax.random.fold_in(own_key, 6), position), (parts,), jnp.float32, smallest / len(split), top_value / len(split))
        return jnp.repeat(jnp.exp(draws), shape[position] // parts).reshape((-1,) + (1,) * (len(shape) - position - 1))

    gain = one(*split[0])
    for cut in split[1:]:
        gain = gain * one(*cut)
    return gain


def gaussian(stream_key, extent, spread, most, shards=(), kind=jnp.bfloat16):
    array = jax.random.normal(stream_key, extent, jnp.float32) * spread
    if len(shards) > 0:
        array = levels(stream_key, extent, shards, -0.22, 0.18) * array
    return jnp.clip(array, min=-most, max=most).astype(kind)


def setup_inputs(seed: int = 0) -> dict:
    key_list = jax.random.split(jax.random.key(seed), 9)
    return {
        "tokens": gaussian(key_list[0], (TOKENS, D), 1.0, 6.0, ((0, 32),)),
        "ln_gain": jnp.clip(1.0 + 0.1 * jax.random.normal(key_list[1], (D,), jnp.float32), 0.5, 1.5),
        "ln_bias": gaussian(key_list[2], (D,), 0.3, 2.0, (), jnp.float32),
        "w_in": gaussian(key_list[3], (D, 3 * D + FF), D ** -0.5, 0.125, ((0, 8),)),
        "b_in": gaussian(key_list[4], (3 * D + FF,), 0.5, 3.0, (), jnp.float32),
        "w_out": draw_w_out(jax.random.fold_in(key_list[8], 71), 0),
        "b_out": gaussian(key_list[6], (D,), 0.5, 3.0, (), jnp.float32),
        "cotangent": gaussian(key_list[7], (TOKENS, D), 1.0, 6.0, ((0, 32),)),
    }


@jax.custom_vjp
def low(v):
    return lax.optimization_barrier(v.astype(jnp.bfloat16)).astype(jnp.float32)

@jax.custom_vjp
def low_back(v):
    return v

def low_keep(v):
    return (low(v), None)

def low_pass(kept, grad):
    return (grad,)

def back_keep(v):
    return (v, None)

def back_low(kept, grad):
    return (low(grad),)
low.defvjp(low_keep, low_pass)
low_back.defvjp(back_keep, back_low)
highest = lax.Precision.HIGHEST
masked_score = -1e+30

def angle_tables(positions):
    steps_even = jnp.arange(0, ROT, 2).astype(jnp.float32)
    frequency = 10000.0 ** (-steps_even / ROT)
    turned = positions.astype(jnp.float32)[:, None] * frequency[None, :]
    turned = jnp.concatenate([turned, turned], axis=1)
    return (jnp.cos(turned)[:, None, :], jnp.sin(turned)[:, None, :])

def rotate(heads_in, cosine_table, sine_table):
    leading = heads_in[..., :ROT]
    halfway = ROT // 2
    swapped = jnp.concatenate([-leading[..., halfway:], leading[..., :halfway]], axis=-1)
    return jnp.concatenate([leading * cosine_table + swapped * sine_table, heads_in[..., ROT:]], axis=-1)

def attention(query_low, key_low, value_low):
    length = query_low.shape[0]
    block_rows = min(512, length)
    count_blocks = length // block_rows
    query_blocks = query_low.reshape(count_blocks, block_rows, HEADS, HEAD_DIM)
    block_starts = jnp.arange(count_blocks, dtype=jnp.int32) * block_rows
    key_places = jnp.arange(length, dtype=jnp.int32)

    def one_block(packed):
        query_block, block_start = packed
        scores = jnp.einsum('qhd,khd->hqk', query_block, key_low, precision=highest) * HEAD_DIM ** (-0.5)
        scores = low_back(scores)
        query_places = block_start + jnp.arange(block_rows, dtype=jnp.int32)
        visible = key_places[None, :] <= query_places[:, None]
        scores = jnp.where(visible[None], scores, masked_score)
        chances_low = low(jax.nn.softmax(scores, axis=-1))
        return jnp.einsum('hqk,khd->qhd', chances_low, value_low, precision=highest)
    attended = lax.map(jax.checkpoint(one_block), (query_blocks, block_starts))
    return attended.reshape(length, D)

def forward(seq_tokens, norm_gain, norm_shift, w_in, b_in, w_out, b_out):
    length = seq_tokens.shape[0]
    row_mean = lax.optimization_barrier(jnp.mean(seq_tokens, axis=-1, keepdims=True))
    centred = seq_tokens - row_mean
    variance = lax.optimization_barrier(jnp.mean(centred * centred, axis=-1, keepdims=True))
    normed = centred * lax.rsqrt(variance + 1e-05)
    normed_low = low(normed * norm_gain + norm_shift)
    projected = low_back(jnp.dot(normed_low, w_in, precision=highest) + b_in)
    cosine_table, sine_table = angle_tables(jnp.arange(length))
    query_low = low(rotate(projected[:, :D].reshape(length, HEADS, HEAD_DIM), cosine_table, sine_table))
    key_low = low(rotate(projected[:, D:2 * D].reshape(length, HEADS, HEAD_DIM), cosine_table, sine_table))
    value_low = low(projected[:, 2 * D:3 * D]).reshape(length, HEADS, HEAD_DIM)
    attended = low_back(attention(query_low, key_low, value_low))
    hidden = jax.nn.gelu(projected[:, 3 * D:], approximate=True)
    joined = low(jnp.concatenate([attended, hidden], axis=1))
    return seq_tokens + jnp.dot(joined, w_out, precision=highest) + b_out

def reference(tokens, ln_gain, ln_bias, w_in, b_in, w_out, b_out, cotangent):
    parameters = (ln_gain.astype(jnp.float32), ln_bias.astype(jnp.float32), w_in.astype(jnp.float32), b_in.astype(jnp.float32), w_out.astype(jnp.float32), b_out.astype(jnp.float32))
    count_seqs = TOKENS // SEQ_LEN
    inputs = tokens.astype(jnp.float32).reshape(count_seqs, SEQ_LEN, D)
    seeds = cotangent.astype(jnp.float32).reshape(count_seqs, SEQ_LEN, D)

    def one_sequence(totals, seq_pair):
        seq_tokens, seq_cot = seq_pair
        result, pullback = jax.vjp(forward, seq_tokens, *parameters)
        gradients = pullback(seq_cot)
        totals = tuple((first_sum + second_sum for first_sum, second_sum in zip(totals, gradients[1:])))
        return (totals, (result, gradients[0]))
    zero_grads = tuple((jnp.zeros_like(entry) for entry in parameters))
    totals, (results, input_grads) = lax.scan(one_sequence, zero_grads, (inputs, seeds))
    return (results.reshape(TOKENS, D).astype(jnp.bfloat16), input_grads.reshape(TOKENS, D).astype(jnp.bfloat16), totals[0], totals[1], totals[2], totals[3], totals[4], totals[5])
```

```python
import functools
import jax
import jax.numpy as jnp
from jax import lax
from jax.experimental import pallas as pl
from jax.experimental.pallas import tpu as pltpu
from jax.sharding import PartitionSpec as P

D = 2048
HEADS = 32
HEAD_DIM = 64
ROT = 32
FF = 8192
SEQ_LEN = 1024
SLOTS = 5

epsilon = 1e-05
masked_score = -1e30
MESH = pl.DeviceIdType.MESH
f32 = jnp.float32
bf16 = jnp.bfloat16


class Place:
    def __init__(self, n, replicas):
        self.n, self.R = n, replicas
        self.X = max(replicas // 2, 1)
        self.Y = replicas // self.X
        self.L = n // 2
        self.r, self.s = lax.axis_index("replica"), lax.axis_index("shard")
        self.x, self.y = self.r % self.X, self.r // self.X
        self.z, self.c = self.s // 2, self.s % 2
        self.sibling = (self.r, self.s + 1 - 2 * self.c)
        self.pending = []

    def x_peer(self, dx):
        return self.y * self.X + (self.x + dx) % self.X

    def y_peer(self, dy):
        return ((self.y + dy) % self.Y) * self.X + self.x

    def send(self, src, dst, send_sem, recv_sem, device, when=None):
        copy = pltpu.make_async_remote_copy(
            src_ref=src, dst_ref=dst, send_sem=send_sem, recv_sem=recv_sem,
            device_id=device, device_id_type=MESH,
        )
        guarded(when, copy.start)
        self.pending.append((when, copy.wait_send))

    def local(self, src, dst, sem, when=None):
        guarded(when, pltpu.make_async_copy(src, dst, sem).start)

    def arrived(self, ref, sem, when=None):
        guarded(when, pltpu.make_async_copy(ref, ref, sem).wait)

    def drain(self):
        for when, wait in self.pending:
            guarded(when, wait)

    def meet(self, line=True, square=True, whole=False):
        barrier = pltpu.get_barrier_semaphore()
        peers = []
        if line:
            peers += [(self.r, (self.s + k) % self.n) for k in range(1, self.n)]
        if whole:
            peers += [((self.r + k) % self.R, self.s) for k in range(1, self.R)]
        elif square:
            peers += [(self.x_peer(dx), self.s) for dx in range(1, self.X)]
            peers += [(self.y_peer(dy), self.s) for dy in range(1, self.Y)]
        for peer in peers:
            pl.semaphore_signal(barrier, inc=1, device_id=peer, device_id_type=MESH)
        pl.semaphore_wait(barrier, len(peers))


def guarded(when, act):
    if when is None:
        act()
    else:
        pl.when(when)(act)


def both(a, b):
    return b if a is None else a if b is None else jnp.logical_and(a, b)


def rows_at(start, size, multiple=16):
    return pl.ds(pl.multiple_of(start, multiple), size)


def half_of(width):
    return -(-width // 256) * 128


def slot_of(block, n):
    past = jnp.maximum(block - n, 0)
    first = block < n
    return jnp.where(first, block, past // 4), jnp.where(first, 0, 1 + past % 4)


def block_of(device, slot, n):
    return device if slot == 0 else n + 4 * device + slot - 1


def gather_kernel(
    n, replicas, nl, cot, wi, wo, all_nl, all_cot, cols, rows_out,
    ag_send, ag_recv, sib_send, sib_recv, own_sem, wz_send, wz_recv, ws_send, ws_recv,
    dx_send, dx_recv, dy_send, dy_recv, fa_send, fa_recv, fb_send, fb_recv,
    oz_send, oz_recv, ox_send, ox_recv, oy_send, oy_recv, oa_send, oa_recv, ob_send, ob_recv,
):
    me = Place(n, replicas)
    X, Y, L, r, s, z = me.X, me.Y, me.L, me.r, me.s, me.z
    rows = nl.shape[0]
    depth = wi.shape[0]
    q = depth // replicas
    head = D // n
    fc = FF // n
    width = 3 * head + fc
    me.meet()

    def chunk(ref, owner):
        return ref.at[rows_at(owner * rows, rows)]

    pairs = ((nl, all_nl), (cot, all_cot))
    has_left, has_right = z > 0, z < L - 1
    left, right = (r, jnp.maximum(s - 2, 0)), (r, jnp.minimum(s + 2, n - 1))
    for a, (own, every) in enumerate(pairs):
        me.send(own, chunk(every, s), ag_send.at[a, 0, 0], ag_recv.at[a, 0, 1], right, has_right)
        me.send(own, chunk(every, s), ag_send.at[a, 1, 0], ag_recv.at[a, 1, 1], left, has_left)

    def ranges(device):
        return [(part * D + head * device, part * head, head) for part in range(3)] + [
            (3 * D + fc * device, 3 * head, fc)
        ]

    def far(t):
        return (2 * z + 2 + t) % n

    for t in range(n - 2):
        device = far(t)
        back = (s - 2 * (device // 2) - 2) % n
        for part, (src, dst, size) in enumerate(ranges(device)):
            me.send(
                wi.at[rows_at(r * q, q), rows_at(src, size, 128)],
                cols.at[rows_at(s * depth + r * q, q), pl.ds(dst, size)],
                wz_send.at[t, part], wz_recv.at[back, part // 3], (r, device),
            )

    blk = wo.shape[0] // SLOTS
    oq = blk // replicas
    for i in range(SLOTS):
        device, slot = slot_of(SLOTS * s + i, n)
        mine = device == s
        near = jnp.logical_and(device // 2 == z, device != s)
        away = device // 2 != z
        me.local(wo.at[pl.ds(i * blk, blk)], rows_out.at[rows_at(slot * blk, blk)], oz_recv.at[slot], mine)
        me.send(
            wo.at[pl.ds(i * blk, blk)], rows_out.at[rows_at(slot * blk, blk)],
            oz_send.at[i], oz_recv.at[slot], me.sibling, near,
        )
        target = jnp.where(away, device, (s + 2) % n)
        me.send(
            wo.at[rows_at(i * blk + r * oq, oq)], rows_out.at[rows_at(slot * blk + r * oq, oq)],
            oz_send.at[i], oz_recv.at[slot], (r, target), away,
        )

    for a, (own, every) in enumerate(pairs):
        me.local(own, chunk(every, s), own_sem.at[a])
        me.send(own, chunk(every, s), sib_send.at[a, 0], sib_recv.at[a, 0], me.sibling)
    for part, (src, dst, size) in enumerate(ranges(s)):
        me.local(
            wi.at[:, rows_at(src, size, 128)],
            cols.at[rows_at(s * depth, depth), pl.ds(dst, size)], own_sem.at[2 + part],
        )
    for part, (src, dst, size) in enumerate(ranges(me.sibling[1])):
        me.send(
            wi.at[:, rows_at(src, size, 128)],
            cols.at[rows_at(s * depth, depth), pl.ds(dst, size)],
            ws_send.at[part], ws_recv.at[part], me.sibling,
        )

    def share(ref_of, halves, index, sx, rx, sy, ry, sa, ra, sb, rb, when=None):
        def direct():
            for h, (start, size) in enumerate(halves):
                ref = ref_of(r, start, size)
                for dx in range(1, X):
                    me.send(ref, ref, sx.at[index, dx - 1, h], rx.at[index, X - dx - 1, h], (me.x_peer(dx), s), when)
                for dy in range(1, Y):
                    me.send(ref, ref, sy.at[index, dy - 1, h], ry.at[index, Y - dy - 1, h], (me.y_peer(dy), s), when)

        def forward():
            for h, (start, size) in enumerate(halves):
                if h % 2 == 0:
                    for dx in range(1, X):
                        ref = ref_of(me.x_peer(dx), start, size)
                        me.arrived(ref, rx.at[index, dx - 1, h], when)
                        for dy in range(1, Y):
                            me.send(
                                ref, ref, sa.at[index, dy - 1, dx - 1, h // 2],
                                ra.at[index, Y - dy - 1, dx - 1, h // 2], (me.y_peer(dy), s), when,
                            )
                else:
                    for dy in range(1, Y):
                        ref = ref_of(me.y_peer(dy), start, size)
                        me.arrived(ref, ry.at[index, dy - 1, h], when)
                        for dx in range(1, X):
                            me.send(
                                ref, ref, sb.at[index, dx - 1, dy - 1, h // 2],
                                rb.at[index, X - dx - 1, dy - 1, h // 2], (me.x_peer(dx), s), when,
                            )

        def finish():
            for h, (start, size) in enumerate(halves):
                if h % 2 == 0:
                    for dy in range(1, Y):
                        me.arrived(ref_of(me.y_peer(dy), start, size), ry.at[index, dy - 1, h], when)
                else:
                    for dx in range(1, X):
                        me.arrived(ref_of(me.x_peer(dx), start, size), rx.at[index, dx - 1, h], when)
                for dy in range(1, Y):
                    for dx in range(1, X):
                        corner = ((me.y + dy) % Y) * X + (me.x + dx) % X
                        ref = ref_of(corner, start, size)
                        sem = ra.at[index, dy - 1, dx - 1, h // 2] if h % 2 == 0 else rb.at[index, dx - 1, dy - 1, h // 2]
                        me.arrived(ref, sem, when)

        return direct, forward, finish

    fc_half, qkv_half = half_of(fc), half_of(3 * head)
    halves_in = (
        (3 * head, fc_half), (3 * head + fc_half, fc - fc_half),
        (0, qkv_half), (qkv_half, 3 * head - qkv_half),
    )

    def in_piece(t):
        def ref_of(replica, start, size):
            return cols.at[rows_at(far(t) * depth + replica * q, q), pl.ds(start, size)]

        return share(ref_of, halves_in, t, dx_send, dx_recv, dy_send, dy_recv, fa_send, fa_recv, fb_send, fb_recv)

    def in_arrived(t):
        base = rows_at(far(t) * depth + r * q, q)
        me.arrived(cols.at[base, pl.ds(3 * head, fc)], wz_recv.at[t, 1])
        me.arrived(cols.at[base, pl.ds(0, 3 * head)], wz_recv.at[t, 0])

    out_half = half_of(D)
    halves_out = ((0, out_half), (out_half, D - out_half))

    def out_piece(j):
        source = block_of(s, j, n) // SLOTS

        def ref_of(replica, start, size):
            return rows_out.at[rows_at(j * blk + replica * oq, oq), pl.ds(start, size)]

        return share(
            ref_of, halves_out, j, ox_send, ox_recv, oy_send, oy_recv, oa_send, oa_recv, ob_send, ob_recv,
            source // 2 != z,
        )

    def out_arrived(j):
        source = block_of(s, j, n) // SLOTS
        me.arrived(rows_out.at[rows_at(j * blk + r * oq, oq)], oz_recv.at[j], source // 2 != z)
        me.arrived(rows_out.at[pl.ds(j * blk, blk)], oz_recv.at[j], source // 2 == z)

    def pass_on(k):
        for a, (_, every) in enumerate(pairs):
            for side, (source, there, onward) in enumerate(
                ((s - 2 * k, right, has_right), (s + 2 * k, left, has_left))
            ):
                known = (z - k >= 0) if side == 0 else (z + k < L)
                ref = chunk(every, jnp.clip(source, 0, n - 1))
                me.arrived(ref, ag_recv.at[a, side, k], known)
                if k < L - 1:
                    me.send(
                        ref, ref, ag_send.at[a, side, k], ag_recv.at[a, side, k + 1], there, both(known, onward)
                    )
                me.send(
                    ref, ref, sib_send.at[a, 2 * k - 1 + side], sib_recv.at[a, 2 * k - 1 + side], me.sibling, known
                )

    stages = [in_piece(t) for t in range(n - 2)] + [out_piece(j) for j in range(SLOTS)]
    ready = [functools.partial(in_arrived, t) for t in range(n - 2)] + [
        functools.partial(out_arrived, j) for j in range(SLOTS)
    ]
    count = len(stages)
    lag = 2
    for u in range(count + lag):
        if u % 2 == 1 and (u + 1) // 2 < L:
            pass_on((u + 1) // 2)
        if u < count:
            ready[u]()
            stages[u][0]()
        if u >= lag:
            stages[u - lag][1]()
    for k in range((count + lag) // 2 + 1, L):
        pass_on(k)
    for stage in stages:
        stage[2]()
    other = me.sibling[1]
    for a, (own, every) in enumerate(pairs):
        me.arrived(chunk(every, s), own_sem.at[a])
        me.arrived(chunk(every, other), sib_recv.at[a, 0])
        for k in range(1, L):
            for side in range(2):
                source = other - 2 * k if side == 0 else other + 2 * k
                known = (z - k >= 0) if side == 0 else (z + k < L)
                me.arrived(chunk(every, jnp.clip(source, 0, n - 1)), sib_recv.at[a, 2 * k - 1 + side], known)
    for part, (_, dst, size) in enumerate(ranges(s)):
        me.arrived(cols.at[rows_at(s * depth, depth), pl.ds(dst, size)], own_sem.at[2 + part])
        me.arrived(cols.at[rows_at(other * depth, depth), pl.ds(dst, size)], ws_recv.at[part])
    me.drain()


def gather_all(normed_low, cotangent, w_in, w_out):
    n, replicas = lax.axis_size("shard"), lax.axis_size("replica")
    X = max(replicas // 2, 1)
    Y = replicas // X
    L = n // 2
    rows = normed_low.shape[0]
    dma = pltpu.SemaphoreType.DMA
    t = n - 2
    sems = [
        (2, 2, L), (2, 2, L), (2, 2 * L), (2, 2 * L), (6,), (t, 4), (t, 2), (4,), (4,),
        (t, X - 1, 4), (t, X - 1, 4), (t, Y - 1, 4), (t, Y - 1, 4),
        (t, Y - 1, X - 1, 2), (t, Y - 1, X - 1, 2), (t, X - 1, Y - 1, 2), (t, X - 1, Y - 1, 2),
        (SLOTS,), (SLOTS,), (SLOTS, X - 1, 2), (SLOTS, X - 1, 2), (SLOTS, Y - 1, 2), (SLOTS, Y - 1, 2),
        (SLOTS, Y - 1, X - 1, 1), (SLOTS, Y - 1, X - 1, 1), (SLOTS, X - 1, Y - 1, 1), (SLOTS, X - 1, Y - 1, 1),
    ]
    any_space = pl.BlockSpec(memory_space=pl.ANY)
    return pl.pallas_call(
        functools.partial(gather_kernel, n, replicas),
        out_shape=(
            jax.ShapeDtypeStruct((rows * n, D), bf16),
            jax.ShapeDtypeStruct((rows * n, D), bf16),
            jax.ShapeDtypeStruct((D, (3 * D + FF) // n), bf16),
            jax.ShapeDtypeStruct((w_out.shape[0], D), bf16),
        ),
        in_specs=[any_space] * 4,
        out_specs=[any_space] * 4,
        scratch_shapes=[dma(shape) for shape in sems],
        compiler_params=pltpu.CompilerParams(collective_id=0, has_side_effects=True),
        name="gather_all",
    )(normed_low, cotangent, w_in, w_out)


def add_rows(store, loads, rows, strip=16):
    def step(i, carry):
        at = rows_at(i * strip, strip)
        total = loads[0](at).astype(f32)
        for load in loads[1:]:
            total = total + load(at).astype(f32)
        store(at, total)
        return carry

    lax.fori_loop(0, rows // strip, step, 0)


def reduce_kernel(
    n, replicas, gi, go, pm, pd, fi, fo, mixed, d_normed,
    r1ia, r1ib, r2ia, r2ib, r1oa, r1ob, r2oa, r2ob, sb, zb,
    s1_send, s1_recv, s2_send, s2_recv, z_send, z_recv,
    ax_send, ax_recv, ay_send, ay_recv, fa_send, fa_recv, fb_send, fb_recv,
    sib_send, sib_recv, zr_send, zr_recv,
):
    me = Place(n, replicas)
    X, Y, L, r, s, z, c = me.X, me.Y, me.L, me.r, me.s, me.z, me.c
    depth = gi.shape[0] // n
    q = depth // replicas
    width = gi.shape[1]
    me.meet()
    def quarter(half, replica):
        x, y = replica % X, replica // X
        return x * Y + y if half == 0 else y * X + x

    outs = SLOTS
    units = [("out", j) for j in range(outs)] + [("in", k) for k in range(n)]
    aw = {"in": half_of(width), "out": half_of(D)}
    full = {"in": width, "out": D}

    def columns(kind, half):
        return pl.ds(0, aw[kind]) if half == 0 else pl.ds(aw[kind], full[kind] - aw[kind])

    def grad_rows(unit, start, size):
        kind, k = unit
        if kind == "in":
            return rows_at(((s + k) % n) * depth + start, size)
        return rows_at(k * depth + start, size)

    def source(unit):
        return gi if unit[0] == "in" else go

    first = {("in", 0): r1ia, ("in", 1): r1ib, ("out", 0): r1oa, ("out", 1): r1ob}
    second = {("in", 0): r2ia, ("in", 1): r2ib, ("out", 0): r2oa, ("out", 1): r2ob}

    def step_one(u):
        unit = units[u]
        kind, k = unit
        for half in range(2):
            run = (Y if half == 0 else X) * q
            span = X if half == 0 else Y
            for d in range(1, span):
                peer = me.x_peer(d) if half == 0 else me.y_peer(d)
                place = (me.x + d) % X if half == 0 else (me.y + d) % Y
                me.send(
                    source(unit).at[grad_rows(unit, place * run, run), columns(kind, half)],
                    first[kind, half].at[k, span - d - 1],
                    s1_send.at[u, half, d - 1], s1_recv.at[u, half, span - d - 1], (peer, s),
                )

    def step_two(u):
        unit = units[u]
        kind, k = unit
        for half in range(2):
            run = (Y if half == 0 else X) * q
            span = X if half == 0 else Y
            place = me.x if half == 0 else me.y
            buf = first[kind, half]
            for d in range(1, span):
                me.arrived(buf.at[k, d - 1], s1_recv.at[u, half, d - 1])
            cols = columns(kind, half)

            def own(at, unit=unit, start=place * run, cols=cols):
                return source(unit)[pl.ds(pl.multiple_of(grad_rows(unit, start, 16).start + at.start, 16), at.size), cols]

            def store(at, total, buf=buf, k=k):
                buf[k, 0, at, :] = total.astype(bf16)

            add_rows(store, [own] + [lambda at, d=d, buf=buf, k=k: buf[k, d - 1, at, :] for d in range(1, span)], run)
            span2 = Y if half == 0 else X
            for d in range(1, span2):
                peer = me.y_peer(d) if half == 0 else me.x_peer(d)
                place2 = (me.y + d) % Y if half == 0 else (me.x + d) % X
                me.send(
                    buf.at[k, 0, rows_at(place2 * q, q)], second[kind, half].at[k, span2 - d - 1],
                    s2_send.at[u, half, d - 1], s2_recv.at[u, half, span2 - d - 1], (peer, s),
                )

    def step_three(u):
        unit = units[u]
        kind, k = unit
        for half in range(2):
            span2 = Y if half == 0 else X
            place2 = me.y if half == 0 else me.x
            buf, got = first[kind, half], second[kind, half]
            for d in range(1, span2):
                me.arrived(got.at[k, d - 1], s2_recv.at[u, half, d - 1])

            def own(at, buf=buf, k=k, start=place2 * q):
                return buf[k, 0, pl.ds(pl.multiple_of(start + at.start, 16), at.size), :]

            def store(at, total, got=got, k=k):
                got[k, 0, at, :] = total.astype(bf16)

            add_rows(store, [own] + [lambda at, d=d, got=got, k=k: got[k, d - 1, at, :] for d in range(1, span2)], q)
            at = rows_at(quarter(half, r) * q, q)
            cols = columns(kind, half)
            if kind == "in":
                dst = fi.at[s, at, cols]
                if k == 0:
                    me.local(got.at[k, 0], dst, z_recv.at[u, half])
                else:
                    me.send(got.at[k, 0], dst, z_send.at[u, half], z_recv.at[u, half], (r, (s + k) % n))
            else:
                block = block_of(s, k, n)
                device, i = block // SLOTS, block % SLOTS
                dst = fo.at[i, at, cols]
                me.local(got.at[k, 0], dst, z_recv.at[i, half], device == s)
                target = jnp.where(device == s, (s + 1) % n, device)
                me.send(got.at[k, 0], dst, z_send.at[u, half], z_recv.at[i, half], (r, target), device != s)

    def landed(u, half, replica):
        kind, k = units[u]
        at = rows_at(quarter(half, replica) * q, q)
        cols = columns(kind, half)
        if kind == "in":
            return fi.at[(s - k) % n, at, cols]
        return fo.at[k, at, cols]

    def step_four(u):
        for half in range(2):
            ref = landed(u, half, r)
            me.arrived(ref, z_recv.at[u, half])
            for d in range(1, X):
                me.send(ref, ref, ax_send.at[u, half, d - 1], ax_recv.at[u, half, X - d - 1], (me.x_peer(d), s))
            for d in range(1, Y):
                me.send(ref, ref, ay_send.at[u, half, d - 1], ay_recv.at[u, half, Y - d - 1], (me.y_peer(d), s))

    def step_five(u):
        for dx in range(1, X):
            ref = landed(u, 0, me.x_peer(dx))
            me.arrived(ref, ax_recv.at[u, 0, dx - 1])
            for dy in range(1, Y):
                me.send(ref, ref, fa_send.at[u, dy - 1, dx - 1], fa_recv.at[u, Y - dy - 1, dx - 1], (me.y_peer(dy), s))
        for dy in range(1, Y):
            ref = landed(u, 1, me.y_peer(dy))
            me.arrived(ref, ay_recv.at[u, 1, dy - 1])
            for dx in range(1, X):
                me.send(ref, ref, fb_send.at[u, dx - 1, dy - 1], fb_recv.at[u, X - dx - 1, dy - 1], (me.x_peer(dx), s))

    def step_six(u):
        for dy in range(1, Y):
            me.arrived(landed(u, 0, me.y_peer(dy)), ay_recv.at[u, 0, dy - 1])
        for dx in range(1, X):
            me.arrived(landed(u, 1, me.x_peer(dx)), ax_recv.at[u, 1, dx - 1])
        for dy in range(1, Y):
            for dx in range(1, X):
                corner = ((me.y + dy) % Y) * X + (me.x + dx) % X
                me.arrived(landed(u, 0, corner), fa_recv.at[u, dy - 1, dx - 1])
                me.arrived(landed(u, 1, corner), fb_recv.at[u, dx - 1, dy - 1])

    rows = mixed.shape[0]
    sums = ((pm, mixed), (pd, d_normed))

    def part_rows(device):
        return rows_at(device * rows, rows)

    def line_begin():
        for a, (part, _) in enumerate(sums):
            for line in range(L):
                me.send(
                    part.at[part_rows(2 * line + 1 - c)], sb.at[a, line],
                    sib_send.at[a, line], sib_recv.at[a, line], me.sibling,
                )

    def line_send(a, m):
        part = sums[a][0]
        line = (z + m) % L
        me.arrived(sb.at[a, line], sib_recv.at[a, line])
        start = (2 * line + c) * rows

        def store(at, total):
            sb[a, line, at, :] = total.astype(bf16)

        add_rows(
            store,
            [lambda at: part[pl.ds(pl.multiple_of(start + at.start, 16), at.size), :], lambda at: sb[a, line, at, :]],
            rows,
        )
        me.send(sb.at[a, line], zb.at[a, L - m - 1], zr_send.at[a, m - 1], zr_recv.at[a, L - m - 1], (r, 2 * line + c))

    def line_end(a):
        part, total_ref = sums[a]
        me.arrived(sb.at[a, z], sib_recv.at[a, z])
        for m in range(1, L):
            me.arrived(zb.at[a, m - 1], zr_recv.at[a, m - 1])

        def store(at, total):
            total_ref[at, :] = total

        add_rows(
            store,
            [lambda at: part[pl.ds(pl.multiple_of(s * rows + at.start, 16), at.size), :], lambda at: sb[a, z, at, :]]
            + [lambda at, m=m: zb[a, m - 1, at, :] for m in range(1, L)],
            rows,
        )

    ahead = 2
    for u in range(ahead):
        step_one(u)
    line_begin()
    for a in range(2):
        for m in range(1, L):
            line_send(a, m)
    count = len(units)
    for u in range(count + 6):
        if u + ahead < count:
            step_one(u + ahead)
        if u < count:
            step_two(u)
        if 0 <= u - 1 < count:
            step_three(u - 1)
        if 0 <= u - 3 < count:
            step_four(u - 3)
        if 0 <= u - 5 < count:
            step_five(u - 5)
    for a in range(2):
        line_end(a)
    for u in range(count):
        step_six(u)
    me.drain()


def reduce_all(grad_in, grad_out, part_mixed, part_normed, rows):
    n, replicas = lax.axis_size("shard"), lax.axis_size("replica")
    X = max(replicas // 2, 1)
    Y = replicas // X
    L = n // 2
    dma = pltpu.SemaphoreType.DMA
    width = grad_in.shape[1]
    depth = D // n
    q = depth // replicas
    wa, wb = half_of(width), width - half_of(width)
    oa, ob = half_of(D), D - half_of(D)
    units = n + SLOTS
    vmem = pltpu.VMEM
    scratch = [
        vmem((n, X - 1, Y * q, wa), bf16), vmem((n, Y - 1, X * q, wb), bf16),
        vmem((n, Y - 1, q, wa), bf16), vmem((n, X - 1, q, wb), bf16),
        vmem((SLOTS, X - 1, Y * q, oa), bf16), vmem((SLOTS, Y - 1, X * q, ob), bf16),
        vmem((SLOTS, Y - 1, q, oa), bf16), vmem((SLOTS, X - 1, q, ob), bf16),
        vmem((2, L, rows, D), bf16), vmem((2, L - 1, rows, D), bf16),
    ]
    most = max(X, Y) - 1
    sems = [
        (units, 2, most), (units, 2, most), (units, 2, most), (units, 2, most), (units, 2), (units, 2),
        (units, 2, X - 1), (units, 2, X - 1), (units, 2, Y - 1), (units, 2, Y - 1),
        (units, Y - 1, X - 1), (units, Y - 1, X - 1), (units, X - 1, Y - 1), (units, X - 1, Y - 1),
        (2, L), (2, L), (2, L - 1), (2, L - 1),
    ]
    any_space = pl.BlockSpec(memory_space=pl.ANY)
    in_vmem = pl.BlockSpec(memory_space=pltpu.VMEM)
    return pl.pallas_call(
        functools.partial(reduce_kernel, n, replicas),
        out_shape=(
            jax.ShapeDtypeStruct((n, depth, width), bf16),
            jax.ShapeDtypeStruct((SLOTS, depth, D), bf16),
            jax.ShapeDtypeStruct((rows, D), f32),
            jax.ShapeDtypeStruct((rows, D), f32),
        ),
        in_specs=[in_vmem] * 4,
        out_specs=[any_space, any_space, in_vmem, in_vmem],
        scratch_shapes=scratch + [dma(shape) for shape in sems],
        compiler_params=pltpu.CompilerParams(collective_id=1, has_side_effects=True, vmem_limit_bytes=60 << 20),
        name="reduce_all",
    )(grad_in, grad_out, part_mixed, part_normed)


def small_kernel(n, replicas, v, every, got, a_send, a_recv, b_send, b_recv):
    me = Place(n, replicas)
    me.meet(whole=True)
    for k in range(1, replicas):
        me.send(v, got.at[replicas - k - 1], a_send.at[k - 1], a_recv.at[replicas - k - 1], ((me.r + k) % replicas, me.s))
    for k in range(1, replicas):
        me.arrived(got.at[k - 1], a_recv.at[k - 1])
    total = v[...]
    for k in range(1, replicas):
        total = total + got[k - 1]
    every[me.s] = total
    mine = every.at[me.s]
    for k in range(1, n):
        me.send(mine, mine, b_send.at[k - 1], b_recv.at[n - k - 1], (me.r, (me.s + k) % n))
    for k in range(1, n):
        me.arrived(every.at[(me.s + k) % n], b_recv.at[k - 1])
    me.drain()


def small_all(v):
    n, replicas = lax.axis_size("shard"), lax.axis_size("replica")
    dma = pltpu.SemaphoreType.DMA
    in_vmem = pl.BlockSpec(memory_space=pltpu.VMEM)
    return pl.pallas_call(
        functools.partial(small_kernel, n, replicas),
        out_shape=jax.ShapeDtypeStruct((n,) + v.shape, f32),
        in_specs=[in_vmem],
        out_specs=in_vmem,
        scratch_shapes=[
            pltpu.VMEM((replicas - 1,) + v.shape, f32),
            dma((replicas - 1,)), dma((replicas - 1,)), dma((n - 1,)), dma((n - 1,)),
        ],
        compiler_params=pltpu.CompilerParams(collective_id=2, has_side_effects=True),
        name="small_all",
    )(v)


def angle_tables(positions):
    steps_even = jnp.arange(0, ROT, 2).astype(f32)
    frequency = 10000.0 ** (-steps_even / ROT)
    turned = positions.astype(f32)[:, None] * frequency[None, :]
    turned = jnp.concatenate([turned, turned], axis=1)
    return (jnp.cos(turned)[:, None, :], jnp.sin(turned)[:, None, :])


def rotate(heads_in, cosine_table, sine_table):
    leading = heads_in[..., :ROT]
    halfway = ROT // 2
    swapped = jnp.concatenate([-leading[..., halfway:], leading[..., :halfway]], axis=-1)
    return jnp.concatenate([leading * cosine_table + swapped * sine_table, heads_in[..., ROT:]], axis=-1)


def gelu_tanh(values_in):
    return jax.nn.gelu(values_in, approximate=True)


def own_columns(vector, s, n):
    head, fc = D // n, FF // n
    parts = [lax.dynamic_slice_in_dim(vector, part * D + s * head, head) for part in range(3)]
    return jnp.concatenate(parts + [lax.dynamic_slice_in_dim(vector, 3 * D + s * fc, fc)])


def local(tokens, ln_gain, ln_bias, w_in, b_in, w_out, b_out, cotangent):
    n = lax.axis_size("shard")
    s = lax.axis_index("shard")
    rows = tokens.shape[0]
    group = rows * n
    head, fc = D // n, FF // n
    heads = HEADS // n
    width = 3 * head + fc
    sequences = group // SEQ_LEN
    tokens_wide = tokens.astype(f32)
    row_mean = jnp.mean(tokens_wide, axis=-1, keepdims=True)
    centred = tokens_wide - row_mean
    variance = jnp.mean(centred * centred, axis=-1, keepdims=True)
    row_rstd = lax.rsqrt(variance + epsilon)
    normed = centred * row_rstd
    normed_low = (normed * ln_gain + ln_bias).astype(bf16)

    all_normed, all_cot, cols_in, rows_out = gather_all(normed_low, cotangent, w_in, w_out)

    projected = jnp.dot(all_normed, cols_in, preferred_element_type=f32) + own_columns(b_in, s, n)
    cosine_table, sine_table = angle_tables(jnp.arange(group, dtype=jnp.int32) % SEQ_LEN)

    def heads_of(block):
        return block.reshape(sequences, SEQ_LEN, heads, HEAD_DIM)

    def turn(block, sine):
        return rotate(block.reshape(group, heads, HEAD_DIM), cosine_table, sine).reshape(group, head)

    query = heads_of(turn(projected[:, :head], sine_table).astype(bf16))
    key = heads_of(turn(projected[:, head : 2 * head], sine_table).astype(bf16))
    value = heads_of(projected[:, 2 * head : 3 * head].astype(bf16))
    fc_pre = projected[:, 3 * head :]
    hidden = gelu_tanh(fc_pre)
    d_joined = lax.dot_general(all_cot, rows_out, (((1,), (1,)), ((), ())), preferred_element_type=f32)
    d_attended = heads_of(d_joined[:, :head].astype(bf16))

    scale = HEAD_DIM ** (-0.5)
    scores = jnp.einsum("bqhd,bkhd->bhqk", query, key, preferred_element_type=f32) * scale
    place = jnp.arange(SEQ_LEN)
    visible = (place[None, :] <= place[:, None])[None, None]
    chances = jax.nn.softmax(jnp.where(visible, scores, masked_score), axis=-1)
    chances_low = chances.astype(bf16)
    attended = jnp.einsum("bhqk,bkhd->bqhd", chances_low, value, preferred_element_type=f32)
    row_delta = jnp.einsum("bqhd,bqhd->bhq", d_attended.astype(f32), attended)
    d_chances = jnp.einsum("bqhd,bkhd->bhqk", d_attended, value, preferred_element_type=f32)
    d_scores = (chances * (d_chances - row_delta[..., None])).astype(bf16)
    d_query = jnp.einsum("bhqk,bkhd->bqhd", d_scores, key, preferred_element_type=f32) * scale
    d_key = jnp.einsum("bhqk,bqhd->bkhd", d_scores, query, preferred_element_type=f32) * scale
    d_value = jnp.einsum("bhqk,bqhd->bkhd", chances_low, d_attended, preferred_element_type=f32)

    joined = jnp.concatenate([attended.reshape(group, head), hidden], axis=1).astype(bf16)
    part_mixed = jnp.dot(joined, rows_out, preferred_element_type=f32).astype(bf16)
    d_fc = jax.vjp(gelu_tanh, fc_pre)[1](d_joined[:, head:])[0]
    d_projected = jnp.concatenate(
        [turn(d_query, -sine_table), turn(d_key, -sine_table), d_value.reshape(group, head), d_fc], axis=1
    ).astype(bf16)
    part_normed = lax.dot_general(
        d_projected, cols_in, (((1,), (1,)), ((), ())), preferred_element_type=f32
    ).astype(bf16)
    across = (((0,), (0,)), ((), ()))
    grad_in_part = lax.dot_general(all_normed, d_projected, across, preferred_element_type=f32).astype(bf16)
    grad_out_part = lax.dot_general(joined, all_cot, across, preferred_element_type=f32).astype(bf16)
    b_in_part = jnp.sum(d_projected.astype(f32), axis=0)
    b_out_part = jnp.sum(all_cot.astype(f32), axis=0)

    grad_in, grad_out, mixed, d_normed = reduce_all(grad_in_part, grad_out_part, part_mixed, part_normed, rows)

    block_out = (tokens_wide + mixed + b_out).astype(bf16)
    scaled_back = d_normed * ln_gain
    input_part = row_rstd * (
        scaled_back
        - jnp.mean(scaled_back, axis=-1, keepdims=True)
        - normed * jnp.mean(scaled_back * normed, axis=-1, keepdims=True)
    )
    grad_tokens = (cotangent.astype(f32) + input_part).astype(bf16)
    small = jnp.concatenate([b_in_part, b_out_part, jnp.sum(d_normed * normed, axis=0), jnp.sum(d_normed, axis=0)])
    lines = -(-small.shape[0] // 1024) * 8
    small = jnp.pad(small, (0, lines * 128 - small.shape[0])).reshape(lines, 128)
    every = small_all(small).reshape(n, lines * 128)
    grad_b_in = jnp.concatenate(
        [every[:, part * head : (part + 1) * head].reshape(D) for part in range(3)]
        + [every[:, 3 * head : width].reshape(FF)]
    )
    grad_b_out = every[0, width : width + D]
    grad_ln_gain = jnp.sum(every[:, width + D : width + 2 * D], axis=0)
    grad_ln_bias = jnp.sum(every[:, width + 2 * D : width + 3 * D], axis=0)
    depth = D // n
    grad_w_in = jnp.concatenate(
        [
            grad_in[:, :, part * head : (part + 1) * head].transpose(1, 0, 2).reshape(depth, D)
            for part in range(3)
        ]
        + [grad_in[:, :, 3 * head :].transpose(1, 0, 2).reshape(depth, FF)],
        axis=1,
    ).astype(f32)
    grad_w_out = grad_out.reshape(SLOTS * depth, D).astype(f32)
    return (block_out, grad_tokens, grad_ln_gain, grad_ln_bias, grad_w_in, grad_b_in, grad_w_out, grad_b_out)


def solution(mesh):
    both_axes = P(("replica", "shard"), None)
    return jax.shard_map(
        local,
        mesh=mesh,
        in_specs=(both_axes, P(), P(), P("shard", None), P(), P("shard", None), P(), both_axes),
        out_specs=(both_axes, both_axes, P(), P(), P("shard", None), P(), P("shard", None), P()),
        check_vma=False,
    )
```

```python
import functools
import jax
import jax.numpy as jnp
from jax import lax
from jax.experimental import pallas as pl
from jax.experimental.pallas import tpu as pltpu
from jax.sharding import PartitionSpec as P

D = 2048
HEADS = 32
HEAD_DIM = 64
ROT = 32
FF = 8192
SEQ_LEN = 1024
SLOTS = 5

epsilon = 1e-05
masked_score = -1e30
MESH = pl.DeviceIdType.MESH
f32 = jnp.float32
bf16 = jnp.bfloat16


class Place:
    def __init__(self, n, replicas):
        self.n, self.R = n, replicas
        self.X = max(replicas // 2, 1)
        self.Y = replicas // self.X
        self.L = n // 2
        self.r, self.s = lax.axis_index("replica"), lax.axis_index("shard")
        self.x, self.y = self.r % self.X, self.r // self.X
        self.z, self.c = self.s // 2, self.s % 2
        self.sibling = (self.r, self.s + 1 - 2 * self.c)
        self.pending = []

    def x_peer(self, dx):
        return self.y * self.X + (self.x + dx) % self.X

    def y_peer(self, dy):
        return ((self.y + dy) % self.Y) * self.X + self.x

    def send(self, src, dst, send_sem, recv_sem, device, when=None):
        copy = pltpu.make_async_remote_copy(
            src_ref=src, dst_ref=dst, send_sem=send_sem, recv_sem=recv_sem,
            device_id=device, device_id_type=MESH,
        )
        guarded(when, copy.start)
        self.pending.append((when, copy.wait_send))

    def local(self, src, dst, sem, when=None):
        guarded(when, pltpu.make_async_copy(src, dst, sem).start)

    def arrived(self, ref, sem, when=None):
        guarded(when, pltpu.make_async_copy(ref, ref, sem).wait)

    def drain(self):
        for when, wait in self.pending:
            guarded(when, wait)

    def meet(self, line=True, square=True, whole=False):
        barrier = pltpu.get_barrier_semaphore()
        peers = []
        if line:
            peers += [(self.r, (self.s + k) % self.n) for k in range(1, self.n)]
        if whole:
            peers += [((self.r + k) % self.R, self.s) for k in range(1, self.R)]
        elif square:
            peers += [(self.x_peer(dx), self.s) for dx in range(1, self.X)]
            peers += [(self.y_peer(dy), self.s) for dy in range(1, self.Y)]
        for peer in peers:
            pl.semaphore_signal(barrier, inc=1, device_id=peer, device_id_type=MESH)
        pl.semaphore_wait(barrier, len(peers))


def guarded(when, act):
    if when is None:
        act()
    else:
        pl.when(when)(act)


def both(a, b):
    return b if a is None else a if b is None else jnp.logical_and(a, b)


def rows_at(start, size, multiple=16):
    return pl.ds(pl.multiple_of(start, multiple), size)


def half_of(width):
    return -(-width // 256) * 128


def slot_of(block, n):
    past = jnp.maximum(block - n, 0)
    first = block < n
    return jnp.where(first, block, past // 4), jnp.where(first, 0, 1 + past % 4)


def block_of(device, slot, n):
    return device if slot == 0 else n + 4 * device + slot - 1


UP = 0.7978845608028654
NT = (((1,), (1,)), ((), ()))
TALL = 512


class Names:
    def __init__(self, names, refs):
        for name, ref in zip(names, refs, strict=True):
            setattr(self, name, ref)


class Unit:
    def __init__(self, kind, k, buf, width, col0, one, two):
        self.kind, self.k, self.buf, self.width, self.col0 = kind, k, buf, width, col0
        cut = half_of(width)
        self.halves = ((0, cut), (cut, width - cut))
        self.one, self.two = one, two
        self.sent = []


def loop(count, body):
    def step(i, carry):
        body(i)
        return carry

    lax.fori_loop(0, count, step, 0)


def add_rows(store, loads, rows, strip=16):
    def step(i):
        at = rows_at(i * strip, strip)
        total = loads[0](at).astype(f32)
        for load in loads[1:]:
            total = total + load(at).astype(f32)
        store(at, total)

    loop(rows // strip, step)


def shifted(start, at):
    return pl.ds(pl.multiple_of(start + at.start, 16), at.size)


def fused_kernel(n, replicas, names, *refs):
    v = Names(names, refs)
    me = Place(n, replicas)
    X, Y, L, r, s, z, c = me.X, me.Y, me.L, me.r, me.s, me.z, me.c
    rows = v.tok.shape[0]
    group = rows * n
    depth = D // n
    q = depth // replicas
    head, fc = D // n, FF // n
    heads = head // HEAD_DIM
    sequences = group // SEQ_LEN
    head3 = 3 * head
    width = head3 + fc
    tall = group // TALL
    me.meet(whole=True)

    def chunk(ref, owner):
        return ref.at[rows_at(owner * rows, rows)]

    def ranges(device):
        return [(part * D + head * device, part * head, head) for part in range(3)] + [
            (3 * D + fc * device, head3, fc)
        ]

    def far(t):
        return (2 * z + 2 + t) % n

    pairs = (v.nl, v.ct)
    has_left, has_right = z > 0, z < L - 1
    left, right = (r, jnp.maximum(s - 2, 0)), (r, jnp.minimum(s + 2, n - 1))

    def spread_own(a, own):
        every = pairs[a]
        me.send(own, chunk(every, s), v.ag_send.at[a, 0, 0], v.ag_recv.at[a, 0, 1], right, has_right)
        me.send(own, chunk(every, s), v.ag_send.at[a, 1, 0], v.ag_recv.at[a, 1, 1], left, has_left)
        me.send(own, chunk(every, s), v.sib_send.at[a, 0], v.sib_recv.at[a, 0], me.sibling)

    spread_own(1, v.cot)
    me.local(v.cot, chunk(v.ct, s), v.own_sem.at[0])

    def send_far(t, which):
        device = far(t)
        back = (s - 2 * (device // 2) - 2) % n
        for part, (src, dst, size) in enumerate(ranges(device)):
            if (part == 3) == (which == "fc"):
                me.send(
                    v.w_in.at[rows_at(r * q, q), rows_at(src, size, 128)],
                    v.wi.at[rows_at(s * depth + r * q, q), pl.ds(dst, size)],
                    v.wz_send.at[t, part], v.wz_recv.at[back, part // 3], (r, device),
                )

    for t in range(n - 2):
        send_far(t, "fc")

    def normalise(at):
        wide = v.tok[at, :].astype(f32)
        centred = wide - jnp.mean(wide, axis=-1, keepdims=True)
        rstd = lax.rsqrt(jnp.mean(centred * centred, axis=-1, keepdims=True) + epsilon)
        return centred * rstd, rstd

    def norm_strip(i):
        at = rows_at(i * 16, 16)
        normed, _ = normalise(at)
        v.nl[rows_at(s * rows + i * 16, 16), :] = (normed * v.gain[...] + v.bias[...]).astype(bf16)

    loop(rows // 16, norm_strip)
    spread_own(0, chunk(v.nl, s))

    for i in range(SLOTS):
        device, slot = slot_of(SLOTS * s + i, n)
        mine = device == s
        near = jnp.logical_and(device // 2 == z, device != s)
        away = device // 2 != z
        full = v.wo.at[rows_at(slot * depth, depth)]
        me.local(v.w_out.at[pl.ds(i * depth, depth)], full, v.oz_recv.at[slot], mine)
        me.send(v.w_out.at[pl.ds(i * depth, depth)], full, v.oz_send.at[i], v.oz_recv.at[slot], me.sibling, near)
        target = jnp.where(away, device, (s + 2) % n)
        me.send(
            v.w_out.at[rows_at(i * depth + r * q, q)], v.wo.at[rows_at(slot * depth + r * q, q)],
            v.oz_send.at[i], v.oz_recv.at[slot], (r, target), away,
        )
    for t in range(n - 2):
        send_far(t, "qkv")
    for part, (src, dst, size) in enumerate(ranges(s)):
        me.local(
            v.w_in.at[:, rows_at(src, size, 128)], v.wi.at[rows_at(s * depth, depth), pl.ds(dst, size)],
            v.own_sem.at[1 + part],
        )
    for part, (src, dst, size) in enumerate(ranges(me.sibling[1])):
        me.send(
            v.w_in.at[:, rows_at(src, size, 128)], v.wi.at[rows_at(s * depth, depth), pl.ds(dst, size)],
            v.ws_send.at[part], v.ws_recv.at[part], me.sibling,
        )

    def share(ref_of, halves, index, tag, when=None):
        sx, rx, sy, ry, sa, ra, sb, rb = [
            getattr(v, tag + end)
            for end in ("x_send", "x_recv", "y_send", "y_recv", "a_send", "a_recv", "b_send", "b_recv")
        ]

        def direct(picked):
            for h in picked:
                ref = ref_of(r, *halves[h])
                for dx in range(1, X):
                    me.send(ref, ref, sx.at[index, dx - 1, h], rx.at[index, X - dx - 1, h], (me.x_peer(dx), s), when)
                for dy in range(1, Y):
                    me.send(ref, ref, sy.at[index, dy - 1, h], ry.at[index, Y - dy - 1, h], (me.y_peer(dy), s), when)

        def forward(picked):
            for h in picked:
                if h % 2 == 0:
                    for dx in range(1, X):
                        ref = ref_of(me.x_peer(dx), *halves[h])
                        me.arrived(ref, rx.at[index, dx - 1, h], when)
                        for dy in range(1, Y):
                            me.send(
                                ref, ref, sa.at[index, dy - 1, dx - 1, h // 2],
                                ra.at[index, Y - dy - 1, dx - 1, h // 2], (me.y_peer(dy), s), when,
                            )
                else:
                    for dy in range(1, Y):
                        ref = ref_of(me.y_peer(dy), *halves[h])
                        me.arrived(ref, ry.at[index, dy - 1, h], when)
                        for dx in range(1, X):
                            me.send(
                                ref, ref, sb.at[index, dx - 1, dy - 1, h // 2],
                                rb.at[index, X - dx - 1, dy - 1, h // 2], (me.x_peer(dx), s), when,
                            )

        def finish(picked):
            for h in picked:
                if h % 2 == 0:
                    for dy in range(1, Y):
                        me.arrived(ref_of(me.y_peer(dy), *halves[h]), ry.at[index, dy - 1, h], when)
                else:
                    for dx in range(1, X):
                        me.arrived(ref_of(me.x_peer(dx), *halves[h]), rx.at[index, dx - 1, h], when)
                for dy in range(1, Y):
                    for dx in range(1, X):
                        corner = ((me.y + dy) % Y) * X + (me.x + dx) % X
                        sem = ra.at[index, dy - 1, dx - 1, h // 2] if h % 2 == 0 else rb.at[index, dx - 1, dy - 1, h // 2]
                        me.arrived(ref_of(corner, *halves[h]), sem, when)

        return direct, forward, finish

    fc_half, qkv_half = half_of(fc), half_of(head3)
    halves_in = (
        (head3, fc_half), (head3 + fc_half, fc - fc_half), (0, qkv_half), (qkv_half, head3 - qkv_half),
    )

    def in_piece(t):
        def ref_of(replica, start, size):
            return v.wi.at[rows_at(far(t) * depth + replica * q, q), pl.ds(start, size)]

        return share(ref_of, halves_in, t, "i")

    def in_arrived(t, part):
        base = rows_at(far(t) * depth + r * q, q)
        if part == "fc":
            me.arrived(v.wi.at[base, pl.ds(head3, fc)], v.wz_recv.at[t, 1])
        else:
            me.arrived(v.wi.at[base, pl.ds(0, head3)], v.wz_recv.at[t, 0])

    out_half = half_of(D)
    halves_out = ((0, out_half), (out_half, D - out_half))

    def out_piece(j):
        source = block_of(s, j, n) // SLOTS

        def ref_of(replica, start, size):
            return v.wo.at[rows_at(j * depth + replica * q, q), pl.ds(start, size)]

        return share(ref_of, halves_out, j, "o", source // 2 != z)

    def out_arrived(j):
        source = block_of(s, j, n) // SLOTS
        me.arrived(v.wo.at[rows_at(j * depth + r * q, q)], v.oz_recv.at[j], source // 2 != z)
        me.arrived(v.wo.at[pl.ds(j * depth, depth)], v.oz_recv.at[j], source // 2 == z)

    def pass_on(k, a):
        every = pairs[a]
        for side, (source, there, onward) in enumerate(((s - 2 * k, right, has_right), (s + 2 * k, left, has_left))):
            known = (z - k >= 0) if side == 0 else (z + k < L)
            ref = chunk(every, jnp.clip(source, 0, n - 1))
            me.arrived(ref, v.ag_recv.at[a, side, k], known)
            if k < L - 1:
                me.send(ref, ref, v.ag_send.at[a, side, k], v.ag_recv.at[a, side, k + 1], there, both(known, onward))
            me.send(
                ref, ref, v.sib_send.at[a, 2 * k - 1 + side], v.sib_recv.at[a, 2 * k - 1 + side], me.sibling, known
            )

    ins = [in_piece(t) for t in range(n - 2)]
    outs = [out_piece(j) for j in range(SLOTS)]
    fc_h, qkv_h = (0, 1), (2, 3)
    steps = []
    for t in range(n - 2):
        steps.append((t, lambda t=t: (in_arrived(t, "fc"), ins[t][0](fc_h))))
        steps.append((t + 2.5, lambda t=t: ins[t][1](fc_h)))
        steps.append((t + n + 4, lambda t=t: (in_arrived(t, "qkv"), ins[t][0](qkv_h))))
        steps.append((t + n + 6.5, lambda t=t: ins[t][1](qkv_h)))
    for j in range(SLOTS):
        steps.append((n - 2 + j, lambda j=j: (out_arrived(j), outs[j][0](fc_h))))
        steps.append((n + 0.5 + j, lambda j=j: outs[j][1](fc_h)))
    for k in range(1, L):
        steps.append((2 * k - 0.6, lambda k=k: pass_on(k, 1)))
        steps.append((2 * k + 0.4, lambda k=k: pass_on(k, 0)))
    for _, step in sorted(steps, key=lambda pair: pair[0]):
        step()
    for piece in ins:
        piece[2](fc_h + qkv_h)
    for piece in outs:
        piece[2](fc_h)
    other = me.sibling[1]
    me.arrived(chunk(v.ct, s), v.own_sem.at[0])
    for a, every in enumerate(pairs):
        me.arrived(chunk(every, other), v.sib_recv.at[a, 0])
        for k in range(1, L):
            for side in range(2):
                source = other - 2 * k if side == 0 else other + 2 * k
                known = (z - k >= 0) if side == 0 else (z + k < L)
                me.arrived(chunk(every, jnp.clip(source, 0, n - 1)), v.sib_recv.at[a, 2 * k - 1 + side], known)
    for part, (_, dst, size) in enumerate(ranges(s)):
        me.arrived(v.wi.at[rows_at(s * depth, depth), pl.ds(dst, size)], v.own_sem.at[1 + part])
        me.arrived(v.wi.at[rows_at(other * depth, depth), pl.ds(dst, size)], v.ws_recv.at[part])
    me.drain()
    me.pending.clear()

    def tile(i, size=TALL):
        return rows_at(i * size, size)

    def hidden_tile(j):
        cols = pl.ds(head3 + 256 * j, 256)

        def body(m):
            x = jnp.dot(v.nl[tile(m), :], v.wi[:, cols], preferred_element_type=f32) + v.b_own[:, cols]
            square = x * x
            t = jnp.tanh(UP * (x + 0.044715 * (square * x)))
            v.joined[tile(m), pl.ds(head + 256 * j, 256)] = (0.5 * x * (1.0 + t)).astype(bf16)
            slope = 0.5 * (1.0 + t) + 0.5 * x * (1.0 - t * t) * (UP * (1.0 + (3 * 0.044715) * square))
            v.dproj[tile(m), cols] = slope.astype(bf16)

        loop(tall, body)

    def back_hidden_tile(j):
        cols = pl.ds(head3 + 256 * j, 256)

        def body(m):
            d_hidden = lax.dot_general(
                v.ct[tile(m), :], v.wo[pl.ds(depth + 256 * j, 256), :], NT, preferred_element_type=f32
            )
            v.dproj[tile(m), cols] = (d_hidden * v.dproj[tile(m), cols].astype(f32)).astype(bf16)

        loop(tall, body)

    def turned_columns(ref, start, size):
        def body(m):
            v.flip[:size, rows_at(m * 256, 256, 256)] = jnp.transpose(ref[tile(m, 256), pl.ds(start, size)])

        loop(group // 256, body)

    def turned_rows(start):
        def body(m):
            v.flip[:depth, rows_at(m * 256, 256, 256)] = jnp.transpose(v.nl[tile(m, 256), rows_at(start, depth, 128)])

        loop(group // 256, body)

    def grad_out(unit):
        turned_columns(v.joined, depth * unit.k, depth)

        def body(m):
            cols = rows_at(m * 512, 512, 512)
            unit.buf[:, cols] = jnp.dot(v.flip[:depth, :], v.ct[:, cols], preferred_element_type=f32).astype(bf16)

        loop(D // 512, body)

    def grad_in(unit):
        turned_rows(((s + unit.k) % n) * depth)
        for start in range(0, unit.width, 256):
            size = min(256, unit.width - start)
            unit.buf[:, pl.ds(start, size)] = jnp.dot(
                v.flip[:depth, :], v.dproj[:, pl.ds(unit.col0 + start, size)], preferred_element_type=f32
            ).astype(bf16)

    def lanes_turn(x, at, sign):
        lane = lax.broadcasted_iota(jnp.int32, x.shape, 1) % HEAD_DIM
        sine = v.sine[at, :] * sign
        swapped = jnp.where(lane < ROT // 2, -pltpu.roll(x, 128 - ROT // 2, 1), pltpu.roll(x, ROT // 2, 1))
        return x * v.cosine[at, :] + swapped * sine

    def project_heads():
        def body(m):
            at = rows_at((m % (SEQ_LEN // TALL)) * TALL, TALL)
            for slab in range(head3 // 128):
                cols = pl.ds(128 * slab, 128)
                x = jnp.dot(v.nl[tile(m), :], v.wi[:, cols], preferred_element_type=f32) + v.b_own[:, cols]
                part, first = slab // (head // 128), 2 * (slab % (head // 128))
                if part < 2:
                    x = lanes_turn(x, at, 1.0)
                x = x.astype(bf16)
                to = (v.qh, v.kh, v.vh)[part]
                base = (m // (SEQ_LEN // TALL)) * heads + first
                to[base, at, :] = x[:, :HEAD_DIM]
                to[base + 1, at, :] = x[:, HEAD_DIM:]
            for slab in range(head // 128):
                x = lax.dot_general(
                    v.ct[tile(m), :], v.wo[pl.ds(128 * slab, 128), :], NT, preferred_element_type=f32
                ).astype(bf16)
                base = (m // (SEQ_LEN // TALL)) * heads + 2 * slab
                v.doh[base, at, :] = x[:, :HEAD_DIM]
                v.doh[base + 1, at, :] = x[:, HEAD_DIM:]

        loop(tall, body)

    scale = HEAD_DIM ** (-0.5)
    block = 256

    def attend_pair(b, pair):
        def one(side):
            hb = b * heads + 2 * pair + side
            key_turned = jnp.transpose(v.kh[hb])
            value_turned = jnp.transpose(v.vh[hb])
            v.dk[side] = jnp.zeros((SEQ_LEN, HEAD_DIM), f32)
            v.dv[side] = jnp.zeros((SEQ_LEN, HEAD_DIM), f32)
            for i in range(SEQ_LEN // block):
                at, past = pl.ds(i * block, block), (i + 1) * block
                query, d_out = v.qh[hb, at, :], v.doh[hb, at, :]
                scores = lax.dot_general(v.kh[hb, :past, :], query, NT, preferred_element_type=f32) * scale
                key_place = lax.broadcasted_iota(jnp.int32, (past, block), 0)
                query_place = lax.broadcasted_iota(jnp.int32, (past, block), 1) + i * block
                scores = jnp.where(key_place <= query_place, scores, masked_score)
                raised = jnp.exp(scores - jnp.max(scores, axis=0, keepdims=True))
                chances = raised * (1.0 / jnp.sum(raised, axis=0, keepdims=True))
                low = chances.astype(bf16)
                out_turned = jnp.dot(value_turned[:, :past], low, preferred_element_type=f32)
                d_out_turned = jnp.transpose(d_out.astype(f32))
                delta = jnp.sum(d_out_turned * out_turned, axis=0, keepdims=True)
                d_chances = lax.dot_general(v.vh[hb, :past, :], d_out, NT, preferred_element_type=f32)
                d_scores = (chances * (d_chances - delta)).astype(bf16)
                v.oh[side, at, :] = jnp.transpose(out_turned)
                d_query_turned = jnp.dot(key_turned[:, :past], d_scores, preferred_element_type=f32) * scale
                v.dq[side, at, :] = jnp.transpose(d_query_turned)
                v.dk[side, :past, :] += jnp.dot(d_scores, query, preferred_element_type=f32) * scale
                v.dv[side, :past, :] += jnp.dot(low, d_out, preferred_element_type=f32)

        loop(2, one)

        def settle(m):
            at = tile(m, 256)
            put = rows_at(b * SEQ_LEN + m * 256, 256)

            def slab(ref):
                return jnp.concatenate([ref[0, at, :], ref[1, at, :]], axis=1)

            v.joined[put, pl.ds(128 * pair, 128)] = slab(v.oh).astype(bf16)
            v.dproj[put, pl.ds(128 * pair, 128)] = lanes_turn(slab(v.dq), at, -1.0).astype(bf16)
            v.dproj[put, pl.ds(head + 128 * pair, 128)] = lanes_turn(slab(v.dk), at, -1.0).astype(bf16)
            v.dproj[put, pl.ds(2 * head + 128 * pair, 128)] = slab(v.dv).astype(bf16)

        loop(SEQ_LEN // 256, settle)

    def mixed_tiles():
        def body(i):
            m, cols = i % tall, rows_at((i // tall) * 256, 256, 256)
            v.nl[tile(m), cols] = jnp.dot(v.joined[tile(m), :], v.wo[:, cols], preferred_element_type=f32).astype(bf16)

        loop(tall * (D // 256), body)

    def d_normed_tiles():
        def body(i):
            m, at = i % tall, (i // tall) * 256
            v.ct[tile(m), rows_at(at, 256, 256)] = lax.dot_general(
                v.dproj[tile(m), :], v.wi[rows_at(at, 256, 256), :], NT, preferred_element_type=f32
            ).astype(bf16)

        loop(tall * (D // 256), body)

    def quarter(half, replica):
        x, y = replica % X, replica // X
        return x * Y + y if half == 0 else y * X + x

    units_hidden_out = [
        Unit("out", j, v.g_out.at[j - 1], D, 0, (v.r1oa, v.r1ob), (v.r2oa, v.r2ob)) for j in range(1, SLOTS)
    ]
    units_hidden_in = [
        Unit("in", k, v.g_in.at[k], fc, head3, (v.r1fa, v.r1fb), (v.r2fa, v.r2fb)) for k in range(n)
    ]
    unit_attention = Unit("out", 0, v.g_out.at[0], D, 0, (v.r1oa, v.r1ob), (v.r2oa, v.r2ob))
    units_heads = [
        Unit("in", k, v.g_in.at[k, :, pl.ds(0, head3)], head3, 0, (v.r1qa, v.r1qb), (v.r2qa, v.r2qb)) for k in range(n)
    ]
    units = units_hidden_out + units_hidden_in + [unit_attention] + units_heads
    for u, unit in enumerate(units):
        unit.u = u

    def step_one(unit):
        before = len(me.pending)
        for half, (start, size) in enumerate(unit.halves):
            run = (Y if half == 0 else X) * q
            span = X if half == 0 else Y
            for d in range(1, span):
                peer = me.x_peer(d) if half == 0 else me.y_peer(d)
                place = (me.x + d) % X if half == 0 else (me.y + d) % Y
                me.send(
                    unit.buf.at[rows_at(place * run, run), pl.ds(start, size)],
                    unit.one[half].at[unit.k, span - d - 1],
                    v.s1_send.at[unit.u, half, d - 1], v.s1_recv.at[unit.u, half, span - d - 1], (peer, s),
                )
        unit.sent = me.pending[before:]
        del me.pending[before:]

    def drain_unit(unit):
        for when, wait in unit.sent:
            guarded(when, wait)
        unit.sent = []

    def step_two(unit):
        for half, (start, size) in enumerate(unit.halves):
            run = (Y if half == 0 else X) * q
            span = X if half == 0 else Y
            place = me.x if half == 0 else me.y
            got, k = unit.one[half], unit.k
            for d in range(1, span):
                me.arrived(got.at[k, d - 1], v.s1_recv.at[unit.u, half, d - 1])

            def own(at):
                return unit.buf[shifted(place * run, at), pl.ds(start, size)]

            def store(at, total):
                got[k, 0, at, :] = total.astype(bf16)

            add_rows(store, [own] + [lambda at, d=d: got[k, d - 1, at, :] for d in range(1, span)], run)
            span2 = Y if half == 0 else X
            for d in range(1, span2):
                peer = me.y_peer(d) if half == 0 else me.x_peer(d)
                place2 = (me.y + d) % Y if half == 0 else (me.x + d) % X
                me.send(
                    got.at[k, 0, rows_at(place2 * q, q)], unit.two[half].at[k, span2 - d - 1],
                    v.s2_send.at[unit.u, half, d - 1], v.s2_recv.at[unit.u, half, span2 - d - 1], (peer, s),
                )

    def arrive_sems(unit):
        return unit.u

    def step_three(unit):
        for half, (start, size) in enumerate(unit.halves):
            span2 = Y if half == 0 else X
            place2 = me.y if half == 0 else me.x
            kept, got, k = unit.one[half], unit.two[half], unit.k
            for d in range(1, span2):
                me.arrived(got.at[k, d - 1], v.s2_recv.at[unit.u, half, d - 1])

            def own(at):
                return kept[k, 0, shifted(place2 * q, at), :]

            def store(at, total):
                got[k, 0, at, :] = total.astype(bf16)

            add_rows(store, [own] + [lambda at, d=d: got[k, d - 1, at, :] for d in range(1, span2)], q)
            at = rows_at(quarter(half, r) * q, q)
            cols = pl.ds(unit.col0 + start, size)
            if unit.kind == "in":
                dst = v.fi.at[s, at, cols]
                if k == 0:
                    me.local(got.at[k, 0], dst, v.zi_recv.at[unit.u, half])
                else:
                    me.send(
                        got.at[k, 0], dst, v.zi_send.at[unit.u, half], v.zi_recv.at[unit.u, half], (r, (s + k) % n)
                    )
            else:
                natural = block_of(s, k, n)
                device, i = natural // SLOTS, natural % SLOTS
                dst = v.fo.at[i, at, cols]
                me.local(got.at[k, 0], dst, v.zo_recv.at[i, half], device == s)
                target = jnp.where(device == s, (s + 1) % n, device)
                me.send(got.at[k, 0], dst, v.zo_send.at[k, half], v.zo_recv.at[i, half], (r, target), device != s)

    class Landing:
        def __init__(self, kind, k, index, unit):
            self.kind, self.k, self.index, self.unit = kind, k, index, unit

        def ref(self, half, replica):
            at = rows_at(quarter(half, replica) * q, q)
            start, size = self.unit.halves[half]
            cols = pl.ds(self.unit.col0 + start, size)
            if self.kind == "in":
                return v.fi.at[(s - self.k) % n, at, cols]
            return v.fo.at[self.k, at, cols]

        def spread(self):
            u = self.index
            for half in range(2):
                ref = self.ref(half, r)
                sem = v.zi_recv.at[self.unit.u, half] if self.kind == "in" else v.zo_recv.at[self.k, half]
                me.arrived(ref, sem)
                for d in range(1, X):
                    me.send(ref, ref, v.ax_send.at[u, half, d - 1], v.ax_recv.at[u, half, X - d - 1], (me.x_peer(d), s))
                for d in range(1, Y):
                    me.send(ref, ref, v.ay_send.at[u, half, d - 1], v.ay_recv.at[u, half, Y - d - 1], (me.y_peer(d), s))

        def forward(self):
            u = self.index
            for dx in range(1, X):
                ref = self.ref(0, me.x_peer(dx))
                me.arrived(ref, v.ax_recv.at[u, 0, dx - 1])
                for dy in range(1, Y):
                    me.send(
                        ref, ref, v.af_send.at[u, dy - 1, dx - 1], v.af_recv.at[u, Y - dy - 1, dx - 1], (me.y_peer(dy), s)
                    )
            for dy in range(1, Y):
                ref = self.ref(1, me.y_peer(dy))
                me.arrived(ref, v.ay_recv.at[u, 1, dy - 1])
                for dx in range(1, X):
                    me.send(
                        ref, ref, v.bf_send.at[u, dx - 1, dy - 1], v.bf_recv.at[u, X - dx - 1, dy - 1], (me.x_peer(dx), s)
                    )

        def finish(self):
            u = self.index
            for dy in range(1, Y):
                me.arrived(self.ref(0, me.y_peer(dy)), v.ay_recv.at[u, 0, dy - 1])
            for dx in range(1, X):
                me.arrived(self.ref(1, me.x_peer(dx)), v.ax_recv.at[u, 1, dx - 1])
            for dy in range(1, Y):
                for dx in range(1, X):
                    corner = ((me.y + dy) % Y) * X + (me.x + dx) % X
                    me.arrived(self.ref(0, corner), v.af_recv.at[u, dy - 1, dx - 1])
                    me.arrived(self.ref(1, corner), v.bf_recv.at[u, dx - 1, dy - 1])

    landings_in = [Landing("in", k, k, unit) for k, unit in enumerate(units_hidden_in)]
    landings_out = [Landing("out", i, n + i, unit_attention) for i in range(SLOTS)]
    landings_heads = [Landing("in", k, n + SLOTS + k, unit) for k, unit in enumerate(units_heads)]
    landings = landings_in + landings_out + landings_heads

    def line_begin(a):
        part = pairs[a]
        for line in range(L):
            me.send(
                chunk(part, 2 * line + 1 - c), v.sbx.at[a, line], v.ls_send.at[a, line], v.ls_recv.at[a, line], me.sibling
            )

    def fetch(src, slot):
        copy = pltpu.make_async_copy(src, v.tmp.at[slot], v.tmp_sem.at[slot])
        copy.start()
        return copy

    def line_send(a, m):
        part = pairs[a]
        line = (z + m) % L
        me.arrived(v.sbx.at[a, line], v.ls_recv.at[a, line])
        fetch(v.sbx.at[a, line], m).wait()
        start = (2 * line + c) * rows

        def store(at, total):
            part[shifted(start, at), :] = total.astype(bf16)

        add_rows(store, [lambda at: part[shifted(start, at), :], lambda at: v.tmp[m, at, :]], rows)
        me.send(
            chunk(part, 2 * line + c), v.zbx.at[a, L - m - 1], v.lz_send.at[a, m - 1], v.lz_recv.at[a, L - m - 1],
            (r, 2 * line + c),
        )

    def line_sum(a):
        part = pairs[a]
        me.arrived(v.sbx.at[a, z], v.ls_recv.at[a, z])
        copies = [fetch(v.sbx.at[a, z], 0)]
        for m in range(1, L):
            me.arrived(v.zbx.at[a, m - 1], v.lz_recv.at[a, m - 1])
            copies.append(fetch(v.zbx.at[a, m - 1], m))
        for copy in copies:
            copy.wait()

        def strip(at):
            total = part[shifted(s * rows, at), :].astype(f32)
            for m in range(L):
                total = total + v.tmp[m, at, :].astype(f32)
            return total

        return strip

    def finish_mixed():
        strip = line_sum(0)

        def body(i):
            at = rows_at(i * 16, 16)
            v.block_out[at, :] = (v.tok[at, :].astype(f32) + strip(at) + v.b_out[...]).astype(bf16)

        loop(rows // 16, body)

    def finish_normed():
        strip = line_sum(1)
        v.acc[...] = jnp.zeros(v.acc.shape, f32)

        def body(i):
            at = rows_at(i * 16, 16)
            d_normed = strip(at)
            normed, rstd = normalise(at)
            e = d_normed * v.gain[...]
            back = rstd * (
                e - jnp.mean(e, axis=-1, keepdims=True) - normed * jnp.mean(e * normed, axis=-1, keepdims=True)
            )
            v.grad_tokens[at, :] = (v.cot[at, :].astype(f32) + back).astype(bf16)
            product = d_normed * normed
            v.acc[0] += product[:8] + product[8:]
            v.acc[1] += d_normed[:8] + d_normed[8:]

        loop(rows // 16, body)
        v.v2[:, pl.ds(0, D)] = jnp.sum(v.acc[0], axis=0, keepdims=True)
        v.v2[:, pl.ds(D, D)] = jnp.sum(v.acc[1], axis=0, keepdims=True)

    def to_replicas(vec, got, index):
        for k in range(1, replicas):
            me.send(
                vec, got.at[replicas - k - 1], v.vr_send.at[index, k - 1], v.vr_recv.at[index, replicas - k - 1],
                ((r + k) % replicas, s),
            )

    def from_replicas(vec, got, index):
        for k in range(1, replicas):
            me.arrived(got.at[k - 1], v.vr_recv.at[index, k - 1])
        total = vec[...]
        for k in range(1, replicas):
            total = total + got[k - 1]
        return total

    def biases_begin():
        ones = jnp.ones((8, group), bf16)
        for start in range(0, width, 256):
            size = min(256, width - start)
            v.v1[:, pl.ds(start, size)] = jnp.dot(ones, v.dproj[:, pl.ds(start, size)], preferred_element_type=f32)[:1]
        to_replicas(v.v1, v.got1, 0)

    def bias_out_begin():
        ones = jnp.ones((8, group), bf16)

        def body(i):
            cols = rows_at(i * 256, 256, 256)
            v.v1[:, rows_at(width + i * 256, 256, 256)] = jnp.dot(ones, v.ct[:, cols], preferred_element_type=f32)[:1]

        loop(D // 256, body)

    def biases_share():
        v.v1s[...] = from_replicas(v.v1, v.got1, 0)
        v.gb_out[...] = v.v1s[:, pl.ds(width, D)]
        for part, (src, dst, size) in enumerate(ranges(s)):
            at = rows_at(src, size, 128)
            v.gb_in[:, at] = v.v1s[:, pl.ds(dst, size)]
            for k in range(1, n):
                me.send(
                    v.v1s.at[:, pl.ds(dst, size)], v.gb_in.at[:, at], v.vl_send.at[k - 1, part],
                    v.vl_recv.at[n - k - 1, part], (r, (s + k) % n),
                )

    def biases_end():
        for k in range(1, n):
            for part, (src, _, size) in enumerate(ranges((s + k) % n)):
                me.arrived(v.gb_in.at[:, rows_at(src, size, 128)], v.vl_recv.at[k - 1, part])

    def norms_share():
        v.v2s[...] = from_replicas(v.v2, v.got2, 1)
        for k in range(1, n):
            me.send(v.v2s, v.got3.at[n - k - 1], v.vn_send.at[k - 1], v.vn_recv.at[n - k - 1], (r, (s + k) % n))
        for k in range(1, n):
            me.arrived(v.got3.at[k - 1], v.vn_recv.at[k - 1])
        total = v.v2s[...]
        for k in range(1, n):
            total = total + v.got3[k - 1]
        v.g_gain[...] = total[:, :D]
        v.g_bias[...] = total[:, D:]

    events = []
    for unit in units:
        events.append((unit.u, "two", unit, lambda unit=unit: step_two(unit)))
        events.append((unit.u + 1.1, "three", unit, lambda unit=unit: step_three(unit)))
    for landing in landings_in + landings_heads:
        u = landing.unit.u
        events.append((u + 3.2, "four", None, landing.spread))
        events.append((u + 5.3, "five", None, landing.forward))
    for i, landing in enumerate(landings_out):
        u = unit_attention.u + 0.9 * i
        events.append((u + 3.4, "four", None, landing.spread))
        events.append((u + 5.5, "five", None, landing.forward))
    events.sort(key=lambda event: event[0])
    started, doubled = set(), set()

    def begin(unit):
        step_one(unit)
        started.add(unit.u)

    def advance(until):
        while events and events[0][0] <= until:
            _, name, unit, act = events[0]
            if name == "two" and unit.u not in started:
                return
            events.pop(0)
            if name == "two":
                doubled.add(unit.u)
            act()

    for j in range(fc // 256):
        hidden_tile(j)
    for unit in units_hidden_out:
        grad_out(unit)
        begin(unit)
    for j in range(fc // 256):
        back_hidden_tile(j)
    advance(0)
    for k, unit in enumerate(units_hidden_in):
        grad_in(unit)
        begin(unit)
        if k % 4 == 3:
            advance(k // 4 + 1.5)
    project_heads()
    advance(4)
    pair_list = [(b, pair) for b in range(sequences) for pair in range(heads // 2)]
    for i, (b, pair) in enumerate(pair_list):
        attend_pair(b, pair)
        advance(4 + 4 * (i + 1))
    advance(units_hidden_in[-1].u)
    assert all(unit.u in doubled for unit in units_hidden_out + units_hidden_in)
    drain_unit(units_hidden_out[0])
    grad_out(unit_attention)
    begin(unit_attention)
    bias_out_begin()
    biases_begin()
    for unit, past in zip(units_heads, units_hidden_in, strict=True):
        drain_unit(past)
        grad_in(unit)
        begin(unit)
    advance(unit_attention.u)
    mixed_tiles()
    line_begin(0)
    advance(unit_attention.u + 2)
    d_normed_tiles()
    line_begin(1)
    biases_share()
    advance(unit_attention.u + 3)
    for m in range(1, L):
        line_send(0, m)
    advance(unit_attention.u + 4)
    for m in range(1, L):
        line_send(1, m)
    advance(unit_attention.u + 7)
    finish_mixed()
    advance(unit_attention.u + 8)
    finish_normed()
    to_replicas(v.v2, v.got2, 1)
    advance(1000)
    norms_share()
    biases_end()
    for landing in landings:
        landing.finish()
    for unit in units:
        drain_unit(unit)
    me.drain()


def fused(tokens, ln_gain, ln_bias, w_in, b_own, w_out, b_out, cotangent, cosine, sine):
    n, replicas = lax.axis_size("shard"), lax.axis_size("replica")
    X = max(replicas // 2, 1)
    Y = replicas // X
    L = n // 2
    rows = tokens.shape[0]
    group = rows * n
    depth = D // n
    q = depth // replicas
    head, fc = D // n, FF // n
    head3 = 3 * head
    width = head3 + fc
    both_heads = (group // SEQ_LEN) * (head // HEAD_DIM)
    vmem, dma = pltpu.VMEM, pltpu.SemaphoreType.DMA
    t = n - 2
    most = max(X, Y) - 1
    units = 2 * n + SLOTS
    scratch = {
        "nl": vmem((group, D), bf16), "ct": vmem((group, D), bf16),
        "wi": vmem((D, width), bf16), "wo": vmem((SLOTS * depth, D), bf16),
        "joined": vmem((group, head + fc), bf16), "dproj": vmem((group, width), bf16),
        "flip": vmem((depth, group), bf16),
        "oh": vmem((2, SEQ_LEN, HEAD_DIM), f32), "dq": vmem((2, SEQ_LEN, HEAD_DIM), f32),
        "dk": vmem((2, SEQ_LEN, HEAD_DIM), f32), "dv": vmem((2, SEQ_LEN, HEAD_DIM), f32),
        "g_out": vmem((SLOTS - 1, depth, D), bf16), "g_in": vmem((n, depth, fc), bf16),
        "tmp": vmem((L, rows, D), bf16), "acc": vmem((2, 8, D), f32),
        "v1": vmem((1, width + D), f32), "v1s": vmem((1, width + D), f32), "got1": vmem((replicas - 1, 1, width + D), f32),
        "v2": vmem((1, 2 * D), f32), "v2s": vmem((1, 2 * D), f32), "got2": vmem((replicas - 1, 1, 2 * D), f32),
        "got3": vmem((n - 1, 1, 2 * D), f32),
    }
    for name in ("qh", "kh", "vh", "doh"):
        scratch[name] = vmem((both_heads, SEQ_LEN, HEAD_DIM), bf16)
    for tag, count, wide in (("o", SLOTS, D), ("f", n, fc), ("q", n, head3)):
        a, b = half_of(wide), wide - half_of(wide)
        scratch["r1" + tag + "a"] = vmem((count, X - 1, Y * q, a), bf16)
        scratch["r1" + tag + "b"] = vmem((count, Y - 1, X * q, b), bf16)
        scratch["r2" + tag + "a"] = vmem((count, Y - 1, q, a), bf16)
        scratch["r2" + tag + "b"] = vmem((count, X - 1, q, b), bf16)
    sems = {
        "ag": (2, 2, L), "sib": (2, 2 * L), "ws": (4,), "oz": (SLOTS,),
        "ix": (t, X - 1, 4), "iy": (t, Y - 1, 4), "ia": (t, Y - 1, X - 1, 2), "ib": (t, X - 1, Y - 1, 2),
        "ox": (SLOTS, X - 1, 2), "oy": (SLOTS, Y - 1, 2), "oa": (SLOTS, Y - 1, X - 1, 1), "ob": (SLOTS, X - 1, Y - 1, 1),
        "s1": (units, 2, most), "s2": (units, 2, most), "zi": (units, 2), "zo": (SLOTS, 2),
        "ax": (units, 2, X - 1), "ay": (units, 2, Y - 1),
        "af": (units, Y - 1, X - 1), "bf": (units, X - 1, Y - 1),
        "ls": (2, L), "lz": (2, L - 1), "vr": (2, replicas - 1), "vl": (n - 1, 4), "vn": (n - 1,),
    }
    for name, shape in sems.items():
        scratch[name + "_send"] = dma(shape)
        scratch[name + "_recv"] = dma(shape)
    scratch["wz_send"], scratch["wz_recv"] = dma((t, 4)), dma((t, 2))
    scratch["own_sem"], scratch["tmp_sem"] = dma((5,)), dma((L,))
    any_space, in_vmem = pl.BlockSpec(memory_space=pl.ANY), pl.BlockSpec(memory_space=pltpu.VMEM)
    inputs = {
        "tok": (tokens, in_vmem), "cot": (cotangent, in_vmem), "gain": (ln_gain.reshape(1, D), in_vmem),
        "bias": (ln_bias.reshape(1, D), in_vmem), "b_own": (b_own.reshape(1, width), in_vmem),
        "b_out": (b_out.reshape(1, D), in_vmem), "cosine": (cosine, in_vmem), "sine": (sine, in_vmem),
        "w_in": (w_in, any_space), "w_out": (w_out, any_space),
    }
    shape = jax.ShapeDtypeStruct
    outputs = {
        "fi": (shape((n, depth, width), bf16), any_space), "fo": (shape((SLOTS, depth, D), bf16), any_space),
        "block_out": (shape((rows, D), bf16), in_vmem), "grad_tokens": (shape((rows, D), bf16), in_vmem),
        "gb_in": (shape((1, 3 * D + FF), f32), in_vmem), "gb_out": (shape((1, D), f32), in_vmem),
        "g_gain": (shape((1, D), f32), in_vmem), "g_bias": (shape((1, D), f32), in_vmem),
        "sbx": (shape((2, L, rows, D), bf16), any_space), "zbx": (shape((2, L - 1, rows, D), bf16), any_space),
    }
    return pl.pallas_call(
        functools.partial(fused_kernel, n, replicas, list(inputs) + list(outputs) + list(scratch)),
        out_shape=tuple(out for out, _ in outputs.values()),
        in_specs=[spec for _, spec in inputs.values()],
        out_specs=tuple(spec for _, spec in outputs.values()),
        scratch_shapes=list(scratch.values()),
        compiler_params=pltpu.CompilerParams(collective_id=0, has_side_effects=True, vmem_limit_bytes=63 << 20),
        name="fused",
    )(*[value for value, _ in inputs.values()])


def widen_kernel(n, fi, fo, gi, go, low, wide, in_sem, out_sem):
    depth, width = fi.shape[1], fi.shape[2]
    head, fc = D // n, FF // n
    jobs = [("in", d) for d in range(n)] + [("out", i) for i in range(SLOTS)]

    def load(j):
        kind, i = jobs[j]
        src = fi.at[i] if kind == "in" else fo.at[i]
        return pltpu.make_async_copy(src, low.at[j % 2, :, pl.ds(0, src.shape[1])], in_sem.at[j % 2])

    def stores(j):
        kind, i = jobs[j]
        slot = j % 2
        if kind == "out":
            return [pltpu.make_async_copy(wide.at[slot], go.at[pl.ds(i * depth, depth)], out_sem.at[slot, 0])]
        places = [(part * D + head * i, part * head, head) for part in range(3)] + [(3 * D + fc * i, 3 * head, fc)]
        return [
            pltpu.make_async_copy(wide.at[slot, :, pl.ds(src, size)], gi.at[:, pl.ds(dst, size)], out_sem.at[slot, p])
            for p, (dst, src, size) in enumerate(places)
        ]

    load(0).start()
    for j, (kind, _) in enumerate(jobs):
        if j + 1 < len(jobs):
            load(j + 1).start()
        load(j).wait()
        if j >= 2:
            for copy in stores(j - 2):
                copy.wait()
        size = width if kind == "in" else D

        def body(i, j=j, size=size):
            at = rows_at(i * 16, 16)
            wide[j % 2, at, pl.ds(0, size)] = low[j % 2, at, pl.ds(0, size)].astype(f32)

        loop(depth // 16, body)
        for copy in stores(j):
            copy.start()
    for j in (len(jobs) - 2, len(jobs) - 1):
        for copy in stores(j):
            copy.wait()


def widen(fi, fo):
    n = lax.axis_size("shard")
    depth = fi.shape[1]
    dma = pltpu.SemaphoreType.DMA
    any_space = pl.BlockSpec(memory_space=pl.ANY)
    return pl.pallas_call(
        functools.partial(widen_kernel, n),
        out_shape=(
            jax.ShapeDtypeStruct((depth, 3 * D + FF), f32),
            jax.ShapeDtypeStruct((SLOTS * depth, D), f32),
        ),
        in_specs=[any_space] * 2,
        out_specs=(any_space,) * 2,
        scratch_shapes=[
            pltpu.VMEM((2, depth, D), bf16), pltpu.VMEM((2, depth, D), f32), dma((2,)), dma((2, 4)),
        ],
        compiler_params=pltpu.CompilerParams(vmem_limit_bytes=20 << 20),
        name="widen",
    )(fi, fo)


def own_columns(vector, s, n):
    head, fc = D // n, FF // n
    parts = [lax.dynamic_slice_in_dim(vector, part * D + s * head, head) for part in range(3)]
    return jnp.concatenate(parts + [lax.dynamic_slice_in_dim(vector, 3 * D + s * fc, fc)])


def local(tokens, ln_gain, ln_bias, w_in, b_in, w_out, b_out, cotangent):
    n = lax.axis_size("shard")
    s = lax.axis_index("shard")
    lane = jnp.arange(128) % HEAD_DIM
    frequency = 10000.0 ** (-(2.0 * (lane % (ROT // 2))).astype(f32) / ROT)
    angle = jnp.arange(SEQ_LEN).astype(f32)[:, None] * frequency[None, :]
    rotary = (lane < ROT)[None, :]
    cosine = jnp.where(rotary, jnp.cos(angle), 1.0)
    sine = jnp.where(rotary, jnp.sin(angle), 0.0)
    fi, fo, block_out, grad_tokens, gb_in, gb_out, g_gain, g_bias, _, _ = fused(
        tokens, ln_gain, ln_bias, w_in, own_columns(b_in, s, n), w_out, b_out, cotangent, cosine, sine
    )
    grad_w_in, grad_w_out = widen(fi, fo)
    return (
        block_out, grad_tokens, g_gain.reshape(D), g_bias.reshape(D),
        grad_w_in, gb_in.reshape(3 * D + FF), grad_w_out, gb_out.reshape(D),
    )


def solution(mesh):
    both_axes = P(("replica", "shard"), None)
    return jax.shard_map(
        local,
        mesh=mesh,
        in_specs=(both_axes, P(), P(), P("shard", None), P(), P("shard", None), P(), both_axes),
        out_specs=(both_axes, both_axes, P(), P(), P("shard", None), P(), P("shard", None), P()),
        check_vma=False,
    )
```

```python
import functools
import jax
import jax.numpy as jnp
from jax import lax
from jax.experimental import pallas as pl
from jax.experimental.pallas import tpu as pltpu
from jax.sharding import PartitionSpec as P

D = 2048
HEADS = 32
HEAD_DIM = 64
ROT = 32
FF = 8192
SEQ_LEN = 1024
SLOTS = 5

epsilon = 1e-05
masked_score = -1e30
MESH = pl.DeviceIdType.MESH
f32 = jnp.float32
bf16 = jnp.bfloat16


class Place:
    def __init__(self, n, replicas):
        self.n, self.R = n, replicas
        self.X = max(replicas // 2, 1)
        self.Y = replicas // self.X
        self.L = n // 2
        self.r, self.s = lax.axis_index("replica"), lax.axis_index("shard")
        self.x, self.y = self.r % self.X, self.r // self.X
        self.z, self.c = self.s // 2, self.s % 2
        self.sibling = (self.r, self.s + 1 - 2 * self.c)
        self.pending = []

    def x_peer(self, dx):
        return self.y * self.X + (self.x + dx) % self.X

    def y_peer(self, dy):
        return ((self.y + dy) % self.Y) * self.X + self.x

    def send(self, src, dst, send_sem, recv_sem, device, when=None):
        copy = pltpu.make_async_remote_copy(
            src_ref=src, dst_ref=dst, send_sem=send_sem, recv_sem=recv_sem,
            device_id=device, device_id_type=MESH,
        )
        guarded(when, copy.start)
        self.pending.append((when, copy.wait_send))

    def local(self, src, dst, sem, when=None):
        guarded(when, pltpu.make_async_copy(src, dst, sem).start)

    def arrived(self, ref, sem, when=None):
        guarded(when, pltpu.make_async_copy(ref, ref, sem).wait)

    def drain(self):
        for when, wait in self.pending:
            guarded(when, wait)

    def meet(self, line=True, square=True, whole=False):
        barrier = pltpu.get_barrier_semaphore()
        peers = []
        if line:
            peers += [(self.r, (self.s + k) % self.n) for k in range(1, self.n)]
        if whole:
            peers += [((self.r + k) % self.R, self.s) for k in range(1, self.R)]
        elif square:
            peers += [(self.x_peer(dx), self.s) for dx in range(1, self.X)]
            peers += [(self.y_peer(dy), self.s) for dy in range(1, self.Y)]
        for peer in peers:
            pl.semaphore_signal(barrier, inc=1, device_id=peer, device_id_type=MESH)
        pl.semaphore_wait(barrier, len(peers))


def guarded(when, act):
    if when is None:
        act()
    else:
        pl.when(when)(act)


def both(a, b):
    return b if a is None else a if b is None else jnp.logical_and(a, b)


def rows_at(start, size, multiple=16):
    return pl.ds(pl.multiple_of(start, multiple), size)


def half_of(width):
    return -(-width // 256) * 128


def slot_of(block, n):
    past = jnp.maximum(block - n, 0)
    first = block < n
    return jnp.where(first, block, past // 4), jnp.where(first, 0, 1 + past % 4)


def block_of(device, slot, n):
    return device if slot == 0 else n + 4 * device + slot - 1


UP = 0.7978845608028654
NT = (((1,), (1,)), ((), ()))
TALL = 512
EAGER = (1.0, 2.0, 1.0, 4.0, 1.5)
HOP = 2.5


class Names:
    def __init__(self, names, refs):
        for name, ref in zip(names, refs, strict=True):
            setattr(self, name, ref)


class Unit:
    def __init__(self, kind, k, buf, width, col0, one, two):
        self.kind, self.k, self.buf, self.width, self.col0 = kind, k, buf, width, col0
        cut = half_of(width)
        self.halves = ((0, cut), (cut, width - cut))
        self.one, self.two = one, two
        self.sent = []


def loop(count, body):
    def step(i, carry):
        body(i)
        return carry

    lax.fori_loop(0, count, step, 0)


def add_rows(store, loads, rows, strip=16):
    def step(i):
        at = rows_at(i * strip, strip)
        total = loads[0](at).astype(f32)
        for load in loads[1:]:
            total = total + load(at).astype(f32)
        store(at, total)

    loop(rows // strip, step)


def shifted(start, at):
    return pl.ds(pl.multiple_of(start + at.start, 16), at.size)


def fused_kernel(n, replicas, names, *refs):
    v = Names(names, refs)
    me = Place(n, replicas)
    X, Y, L, r, s, z, c = me.X, me.Y, me.L, me.r, me.s, me.z, me.c
    rows = v.tok.shape[0]
    group = rows * n
    depth = D // n
    q = depth // replicas
    head, fc = D // n, FF // n
    heads = head // HEAD_DIM
    sequences = group // SEQ_LEN
    head3 = 3 * head
    width = head3 + fc
    tall = group // TALL
    me.meet(whole=True)

    def chunk(ref, owner):
        return ref.at[rows_at(owner * rows, rows)]

    def ranges(device):
        return [(part * D + head * device, part * head, head) for part in range(3)] + [
            (3 * D + fc * device, head3, fc)
        ]

    order = list(range(L // 2, L)) + list(range(1, L // 2))

    def far(t):
        chip, m, bit = 0, order[t // 2], 1
        while bit < L:
            chip = chip + ((z // bit + m // bit) % 2) * bit
            bit *= 2
        return 2 * chip + t % 2

    pairs = (v.nl, v.ct)
    has_left, has_right = z > 0, z < L - 1
    left, right = (r, jnp.maximum(s - 2, 0)), (r, jnp.minimum(s + 2, n - 1))

    def spread_own(a, own):
        every = pairs[a]
        me.send(own, chunk(every, s), v.ag_send.at[a, 0, 0], v.ag_recv.at[a, 0, 1], right, has_right)
        me.send(own, chunk(every, s), v.ag_send.at[a, 1, 0], v.ag_recv.at[a, 1, 1], left, has_left)
        me.send(own, chunk(every, s), v.sib_send.at[a, 0], v.sib_recv.at[a, 0], me.sibling)

    me.local(v.cot, chunk(v.ct, s), v.own_sem.at[0])

    def send_far(t, which):
        device = far(t)
        back = 2 * (t // 2) + c
        for part, (src, dst, size) in enumerate(ranges(device)):
            if (part == 3) == (which == "fc"):
                me.send(
                    v.w_in.at[rows_at(r * q, q), rows_at(src, size, 128)],
                    v.wi.at[rows_at(s * depth + r * q, q), pl.ds(dst, size)],
                    v.wz_send.at[t, part], v.wz_recv.at[back, part // 3], (r, device),
                )

    for t in range(n - 2):
        send_far(t, "fc")

    def normalise(at):
        wide = v.tok[at, :].astype(f32)
        centred = wide - jnp.mean(wide, axis=-1, keepdims=True)
        rstd = lax.rsqrt(jnp.mean(centred * centred, axis=-1, keepdims=True) + epsilon)
        return centred * rstd, rstd

    def norm_strip(i):
        at = rows_at(i * 16, 16)
        normed, _ = normalise(at)
        v.nl[rows_at(s * rows + i * 16, 16), :] = (normed * v.gain[...] + v.bias[...]).astype(bf16)

    loop(rows // 16, norm_strip)

    for i in range(SLOTS):
        device, slot = slot_of(SLOTS * s + i, n)
        mine = device == s
        near = jnp.logical_and(device // 2 == z, device != s)
        away = device // 2 != z
        full = v.wo.at[rows_at(slot * depth, depth)]
        me.local(v.w_out.at[pl.ds(i * depth, depth)], full, v.oz_recv.at[slot], mine)
        me.send(v.w_out.at[pl.ds(i * depth, depth)], full, v.oz_send.at[i], v.oz_recv.at[slot], me.sibling, near)
        target = jnp.where(away, device, (s + 2) % n)
        me.send(
            v.w_out.at[rows_at(i * depth + r * q, q)], v.wo.at[rows_at(slot * depth + r * q, q)],
            v.oz_send.at[i], v.oz_recv.at[slot], (r, target), away,
        )
    for t in range(n - 2):
        send_far(t, "qkv")
    for part, (src, dst, size) in enumerate(ranges(s)):
        me.local(
            v.w_in.at[:, rows_at(src, size, 128)], v.wi.at[rows_at(s * depth, depth), pl.ds(dst, size)],
            v.own_sem.at[1 + part],
        )
    for part, (src, dst, size) in enumerate(ranges(me.sibling[1])):
        me.send(
            v.w_in.at[:, rows_at(src, size, 128)], v.wi.at[rows_at(s * depth, depth), pl.ds(dst, size)],
            v.ws_send.at[part], v.ws_recv.at[part], me.sibling,
        )

    def share(ref_of, halves, index, tag, when=None):
        sx, rx, sy, ry, sa, ra, sb, rb = [
            getattr(v, tag + end)
            for end in ("x_send", "x_recv", "y_send", "y_recv", "a_send", "a_recv", "b_send", "b_recv")
        ]

        def direct(picked):
            for h in picked:
                ref = ref_of(r, *halves[h])
                for dx in range(1, X):
                    me.send(ref, ref, sx.at[index, dx - 1, h], rx.at[index, X - dx - 1, h], (me.x_peer(dx), s), when)
                for dy in range(1, Y):
                    me.send(ref, ref, sy.at[index, dy - 1, h], ry.at[index, Y - dy - 1, h], (me.y_peer(dy), s), when)

        def forward(picked):
            for h in picked:
                if h % 2 == 0:
                    for dx in range(1, X):
                        ref = ref_of(me.x_peer(dx), *halves[h])
                        me.arrived(ref, rx.at[index, dx - 1, h], when)
                        for dy in range(1, Y):
                            me.send(
                                ref, ref, sa.at[index, dy - 1, dx - 1, h // 2],
                                ra.at[index, Y - dy - 1, dx - 1, h // 2], (me.y_peer(dy), s), when,
                            )
                else:
                    for dy in range(1, Y):
                        ref = ref_of(me.y_peer(dy), *halves[h])
                        me.arrived(ref, ry.at[index, dy - 1, h], when)
                        for dx in range(1, X):
                            me.send(
                                ref, ref, sb.at[index, dx - 1, dy - 1, h // 2],
                                rb.at[index, X - dx - 1, dy - 1, h // 2], (me.x_peer(dx), s), when,
                            )

        def finish(picked):
            for h in picked:
                if h % 2 == 0:
                    for dy in range(1, Y):
                        me.arrived(ref_of(me.y_peer(dy), *halves[h]), ry.at[index, dy - 1, h], when)
                else:
                    for dx in range(1, X):
                        me.arrived(ref_of(me.x_peer(dx), *halves[h]), rx.at[index, dx - 1, h], when)
                for dy in range(1, Y):
                    for dx in range(1, X):
                        corner = ((me.y + dy) % Y) * X + (me.x + dx) % X
                        sem = ra.at[index, dy - 1, dx - 1, h // 2] if h % 2 == 0 else rb.at[index, dx - 1, dy - 1, h // 2]
                        me.arrived(ref_of(corner, *halves[h]), sem, when)

        return direct, forward, finish

    fc_half, qkv_half = half_of(fc), half_of(head3)
    halves_in = (
        (head3, fc_half), (head3 + fc_half, fc - fc_half), (0, qkv_half), (qkv_half, head3 - qkv_half),
    )

    def in_piece(t):
        def ref_of(replica, start, size):
            return v.wi.at[rows_at(far(t) * depth + replica * q, q), pl.ds(start, size)]

        return share(ref_of, halves_in, t, "i")

    def in_arrived(t, part):
        base = rows_at(far(t) * depth + r * q, q)
        if part == "fc":
            me.arrived(v.wi.at[base, pl.ds(head3, fc)], v.wz_recv.at[t, 1])
        else:
            me.arrived(v.wi.at[base, pl.ds(0, head3)], v.wz_recv.at[t, 0])

    out_half = half_of(D)
    halves_out = ((0, out_half), (out_half, D - out_half))

    def out_piece(j):
        source = block_of(s, j, n) // SLOTS

        def ref_of(replica, start, size):
            return v.wo.at[rows_at(j * depth + replica * q, q), pl.ds(start, size)]

        return share(ref_of, halves_out, j, "o", source // 2 != z)

    def out_arrived(j):
        source = block_of(s, j, n) // SLOTS
        me.arrived(v.wo.at[rows_at(j * depth + r * q, q)], v.oz_recv.at[j], source // 2 != z)
        me.arrived(v.wo.at[pl.ds(j * depth, depth)], v.oz_recv.at[j], source // 2 == z)

    def pass_on(k, a):
        every = pairs[a]
        for side, (source, there, onward) in enumerate(((s - 2 * k, right, has_right), (s + 2 * k, left, has_left))):
            known = (z - k >= 0) if side == 0 else (z + k < L)
            ref = chunk(every, jnp.clip(source, 0, n - 1))
            me.arrived(ref, v.ag_recv.at[a, side, k], known)
            if k < L - 1:
                me.send(ref, ref, v.ag_send.at[a, side, k], v.ag_recv.at[a, side, k + 1], there, both(known, onward))
            me.send(
                ref, ref, v.sib_send.at[a, 2 * k - 1 + side], v.sib_recv.at[a, 2 * k - 1 + side], me.sibling, known
            )

    def hidden_rows(chip, when=None):
        at = rows_at(jnp.clip(chip, 0, L - 1) * (2 * rows), 2 * rows)

        def body(j):
            cols = rows_at(head3 + 256 * j, 256, 128)
            x = jnp.dot(v.nl[at, :], v.wi[:, cols], preferred_element_type=f32) + v.b_own[:, cols]
            square = x * x
            t = jnp.tanh(UP * (x + 0.044715 * (square * x)))
            v.joined[at, rows_at(head + 256 * j, 256, 128)] = (0.5 * x * (1.0 + t)).astype(bf16)
            slope = 0.5 * (1.0 + t) + 0.5 * x * (1.0 - t * t) * (UP * (1.0 + (3 * 0.044715) * square))
            d_hidden = lax.dot_general(
                v.ct[at, :], v.wo[rows_at(depth + 256 * j, 256, 128), :], NT, preferred_element_type=f32
            )
            v.dproj[at, cols] = (d_hidden * slope).astype(bf16)

        guarded(when, lambda: loop(fc // 256, body))

    ins = [in_piece(t) for t in range(n - 2)]
    outs = [out_piece(j) for j in range(SLOTS)]
    fc_h, qkv_h = (0, 1), (2, 3)
    arrivals, steps = [], []
    for t in range(n - 2):
        arrivals.append((lambda t=t: (in_arrived(t, "fc"), ins[t][0](fc_h)), lambda t=t: ins[t][1](fc_h)))
    for j in range(SLOTS):
        arrivals.append((lambda j=j: (out_arrived(j), outs[j][0](fc_h)), lambda j=j: outs[j][1](fc_h)))
    for t in range(n - 2):
        arrivals.append((lambda t=t: (in_arrived(t, "qkv"), ins[t][0](qkv_h)), lambda t=t: ins[t][1](qkv_h)))
    for i, (first, then) in enumerate(arrivals):
        steps.append((i, first))
        steps.append((i + 2.5, then))
    steps.append((8.2, lambda: (spread_own(1, v.cot), spread_own(0, chunk(v.nl, s)))))
    for k in range(1, L - 1):
        steps.append((8.1 + 4 * k, lambda k=k: pass_on(k, 1)))
        steps.append((8.2 + 4 * k, lambda k=k: pass_on(k, 0)))
    for _, step in sorted(steps, key=lambda pair: pair[0]):
        step()
    other = me.sibling[1]

    def rows_there(k):
        for every in (v.nl, v.ct):
            a = 0 if every is v.nl else 1
            if k == 0:
                me.arrived(chunk(every, other), v.sib_recv.at[a, 0])
                continue
            for side in range(2):
                source = other - 2 * k if side == 0 else other + 2 * k
                known = (z - k >= 0) if side == 0 else (z + k < L)
                me.arrived(chunk(every, jnp.clip(source, 0, n - 1)), v.sib_recv.at[a, 2 * k - 1 + side], known)

    me.arrived(chunk(v.ct, s), v.own_sem.at[0])
    for piece in ins:
        piece[2](fc_h)
    for piece in outs:
        piece[2](fc_h)
    for part, (_, dst, size) in enumerate(ranges(s)):
        me.arrived(v.wi.at[rows_at(s * depth, depth), pl.ds(dst, size)], v.own_sem.at[1 + part])
        me.arrived(v.wi.at[rows_at(other * depth, depth), pl.ds(dst, size)], v.ws_recv.at[part])
    for k in range(L):
        if k == L - 1:
            pass_on(k, 1)
            pass_on(k, 0)
        rows_there(k)
        if k == 0:
            hidden_rows(z)
        else:
            hidden_rows(z - k, z - k >= 0)
            hidden_rows(z + k, z + k < L)
    for piece in ins:
        piece[2](qkv_h)
    me.drain()
    me.pending.clear()

    def tile(i, size=TALL):
        return rows_at(i * size, size)

    def turned_columns(ref, start, size):
        def body(m):
            v.flip[:size, rows_at(m * 256, 256, 256)] = jnp.transpose(ref[tile(m, 256), pl.ds(start, size)])

        loop(group // 256, body)

    def turned_rows(start):
        def body(m):
            v.flip[:depth, rows_at(m * 256, 256, 256)] = jnp.transpose(v.nl[tile(m, 256), rows_at(start, depth, 128)])

        loop(group // 256, body)

    def grad_out(unit):
        turned_columns(v.joined, depth * unit.k, depth)

        def body(m):
            cols = rows_at(m * 512, 512, 512)
            unit.buf[:, cols] = jnp.dot(v.flip[:depth, :], v.ct[:, cols], preferred_element_type=f32).astype(bf16)

        loop(D // 512, body)

    def grad_in(unit):
        turned_rows(((s + unit.k) % n) * depth)
        for start in range(0, unit.width, 256):
            size = min(256, unit.width - start)
            unit.buf[:, pl.ds(start, size)] = jnp.dot(
                v.flip[:depth, :], v.dproj[:, pl.ds(unit.col0 + start, size)], preferred_element_type=f32
            ).astype(bf16)

    def lanes_turn(x, at, sign):
        lane = lax.broadcasted_iota(jnp.int32, x.shape, 1) % HEAD_DIM
        sine = v.sine[at, :] * sign
        swapped = jnp.where(lane < ROT // 2, -pltpu.roll(x, 128 - ROT // 2, 1), pltpu.roll(x, ROT // 2, 1))
        return x * v.cosine[at, :] + swapped * sine

    def project_heads(m):
        at = pl.ds((m % (SEQ_LEN // TALL)) * TALL, TALL)
        for slab in range(head3 // 128):
            cols = pl.ds(128 * slab, 128)
            x = jnp.dot(v.nl[tile(m), :], v.wi[:, cols], preferred_element_type=f32) + v.b_own[:, cols]
            part, first = slab // (head // 128), 2 * (slab % (head // 128))
            if part < 2:
                x = lanes_turn(x, at, 1.0)
            x = x.astype(bf16)
            to = (v.qh, v.kh, v.vh)[part]
            base = (m // (SEQ_LEN // TALL)) * heads + first
            to[base, at, :] = x[:, :HEAD_DIM]
            to[base + 1, at, :] = x[:, HEAD_DIM:]
        for slab in range(head // 128):
            x = lax.dot_general(
                v.ct[tile(m), :], v.wo[pl.ds(128 * slab, 128), :], NT, preferred_element_type=f32
            ).astype(bf16)
            base = (m // (SEQ_LEN // TALL)) * heads + 2 * slab
            v.doh[base, at, :] = x[:, :HEAD_DIM]
            v.doh[base + 1, at, :] = x[:, HEAD_DIM:]

    scale = HEAD_DIM ** (-0.5)
    block = 256

    def attend(b, pair, side):
        hb = b * heads + 2 * pair + side
        key_turned = jnp.transpose(v.kh[hb])
        value_turned = jnp.transpose(v.vh[hb])
        v.dk[side] = jnp.zeros((SEQ_LEN, HEAD_DIM), f32)
        v.dv[side] = jnp.zeros((SEQ_LEN, HEAD_DIM), f32)
        for i in range(SEQ_LEN // block):
            at, past = pl.ds(i * block, block), (i + 1) * block
            query, d_out = v.qh[hb, at, :], v.doh[hb, at, :]
            scores = lax.dot_general(v.kh[hb, :past, :], query, NT, preferred_element_type=f32) * scale
            key_place = lax.broadcasted_iota(jnp.int32, (past, block), 0)
            query_place = lax.broadcasted_iota(jnp.int32, (past, block), 1) + i * block
            scores = jnp.where(key_place <= query_place, scores, masked_score)
            raised = jnp.exp(scores - jnp.max(scores, axis=0, keepdims=True))
            chances = raised * (1.0 / jnp.sum(raised, axis=0, keepdims=True))
            low = chances.astype(bf16)
            out_turned = jnp.dot(value_turned[:, :past], low, preferred_element_type=f32)
            d_out_turned = jnp.transpose(d_out.astype(f32))
            delta = jnp.sum(d_out_turned * out_turned, axis=0, keepdims=True)
            d_chances = lax.dot_general(v.vh[hb, :past, :], d_out, NT, preferred_element_type=f32)
            d_scores = (chances * (d_chances - delta)).astype(bf16)
            v.oh[side, at, :] = jnp.transpose(out_turned)
            d_query_turned = jnp.dot(key_turned[:, :past], d_scores, preferred_element_type=f32) * scale
            v.dq[side, at, :] = jnp.transpose(d_query_turned)
            v.dk[side, :past, :] += jnp.dot(d_scores, query, preferred_element_type=f32) * scale
            v.dv[side, :past, :] += jnp.dot(low, d_out, preferred_element_type=f32)

    def settle_pair(b, pair):
        def settle(m):
            at = tile(m, 256)
            put = rows_at(b * SEQ_LEN + m * 256, 256)

            def slab(ref):
                return jnp.concatenate([ref[0, at, :], ref[1, at, :]], axis=1)

            v.joined[put, pl.ds(128 * pair, 128)] = slab(v.oh).astype(bf16)
            v.dproj[put, pl.ds(128 * pair, 128)] = lanes_turn(slab(v.dq), at, -1.0).astype(bf16)
            v.dproj[put, pl.ds(head + 128 * pair, 128)] = lanes_turn(slab(v.dk), at, -1.0).astype(bf16)
            v.dproj[put, pl.ds(2 * head + 128 * pair, 128)] = slab(v.dv).astype(bf16)

        loop(SEQ_LEN // 256, settle)

    def mixed_tiles():
        def body(i):
            m, cols = i % tall, rows_at((i // tall) * 256, 256, 256)
            v.ct[tile(m), cols] = jnp.dot(v.joined[tile(m), :], v.wo[:, cols], preferred_element_type=f32).astype(bf16)

        loop(tall * (D // 256), body)

    def d_normed_tiles():
        def body(i):
            m, at = i % tall, (i // tall) * 256
            v.nl[tile(m), rows_at(at, 256, 256)] = lax.dot_general(
                v.dproj[tile(m), :], v.wi[rows_at(at, 256, 256), :], NT, preferred_element_type=f32
            ).astype(bf16)

        loop(tall * (D // 256), body)

    def quarter(half, replica):
        x, y = replica % X, replica // X
        return x * Y + y if half == 0 else y * X + x

    units_hidden_out = [
        Unit("out", j, v.g_out.at[j - 1], D, 0, (v.r1oa, v.r1ob), (v.r2oa, v.r2ob)) for j in range(1, SLOTS)
    ]
    units_hidden_in = [
        Unit("in", k, v.g_in.at[k], fc, head3, (v.r1fa, v.r1fb), (v.r2fa, v.r2fb)) for k in range(n)
    ]
    unit_attention = Unit("out", 0, v.g_out.at[0], D, 0, (v.r1oa, v.r1ob), (v.r2oa, v.r2ob))
    units_heads = [
        Unit("in", k, v.g_in.at[k, :, pl.ds(0, head3)], head3, 0, (v.r1qa, v.r1qb), (v.r2qa, v.r2qb)) for k in range(n)
    ]
    units = units_hidden_out + units_hidden_in + [unit_attention] + units_heads
    for u, unit in enumerate(units):
        unit.u = u

    def step_one(unit):
        before = len(me.pending)
        for half, (start, size) in enumerate(unit.halves):
            run = (Y if half == 0 else X) * q
            span = X if half == 0 else Y
            for d in range(1, span):
                peer = me.x_peer(d) if half == 0 else me.y_peer(d)
                place = (me.x + d) % X if half == 0 else (me.y + d) % Y
                me.send(
                    unit.buf.at[rows_at(place * run, run), pl.ds(start, size)],
                    unit.one[half].at[unit.k, span - d - 1],
                    v.s1_send.at[unit.u, half, d - 1], v.s1_recv.at[unit.u, half, span - d - 1], (peer, s),
                )
        unit.sent = me.pending[before:]
        del me.pending[before:]

    def drain_unit(unit):
        for when, wait in unit.sent:
            guarded(when, wait)
        unit.sent = []

    def step_two(unit):
        for half, (start, size) in enumerate(unit.halves):
            run = (Y if half == 0 else X) * q
            span = X if half == 0 else Y
            place = me.x if half == 0 else me.y
            got, k = unit.one[half], unit.k
            for d in range(1, span):
                me.arrived(got.at[k, d - 1], v.s1_recv.at[unit.u, half, d - 1])

            def own(at):
                return unit.buf[shifted(place * run, at), pl.ds(start, size)]

            def store(at, total):
                got[k, 0, at, :] = total.astype(bf16)

            add_rows(store, [own] + [lambda at, d=d: got[k, d - 1, at, :] for d in range(1, span)], run)
            span2 = Y if half == 0 else X
            for d in range(1, span2):
                peer = me.y_peer(d) if half == 0 else me.x_peer(d)
                place2 = (me.y + d) % Y if half == 0 else (me.x + d) % X
                me.send(
                    got.at[k, 0, rows_at(place2 * q, q)], unit.two[half].at[k, span2 - d - 1],
                    v.s2_send.at[unit.u, half, d - 1], v.s2_recv.at[unit.u, half, span2 - d - 1], (peer, s),
                )

    def arrive_sems(unit):
        return unit.u

    def step_three(unit):
        for half, (start, size) in enumerate(unit.halves):
            span2 = Y if half == 0 else X
            place2 = me.y if half == 0 else me.x
            kept, got, k = unit.one[half], unit.two[half], unit.k
            for d in range(1, span2):
                me.arrived(got.at[k, d - 1], v.s2_recv.at[unit.u, half, d - 1])

            def own(at):
                return kept[k, 0, shifted(place2 * q, at), :]

            def store(at, total):
                got[k, 0, at, :] = total.astype(bf16)

            add_rows(store, [own] + [lambda at, d=d: got[k, d - 1, at, :] for d in range(1, span2)], q)
            at = rows_at(quarter(half, r) * q, q)
            cols = pl.ds(unit.col0 + start, size)
            if unit.kind == "in":
                dst = v.fi.at[s, at, cols]
                if k == 0:
                    me.local(got.at[k, 0], dst, v.zi_recv.at[unit.u, half])
                else:
                    me.send(
                        got.at[k, 0], dst, v.zi_send.at[unit.u, half], v.zi_recv.at[unit.u, half], (r, (s + k) % n)
                    )
            else:
                natural = block_of(s, k, n)
                device, i = natural // SLOTS, natural % SLOTS
                dst = v.fo.at[i, at, cols]
                me.local(got.at[k, 0], dst, v.zo_recv.at[i, half], device == s)
                target = jnp.where(device == s, (s + 1) % n, device)
                me.send(got.at[k, 0], dst, v.zo_send.at[k, half], v.zo_recv.at[i, half], (r, target), device != s)

    class Landing:
        def __init__(self, kind, k, index, unit):
            self.kind, self.k, self.index, self.unit = kind, k, index, unit

        def ref(self, half, replica):
            at = rows_at(quarter(half, replica) * q, q)
            start, size = self.unit.halves[half]
            cols = pl.ds(self.unit.col0 + start, size)
            if self.kind == "in":
                return v.fi.at[(s - self.k) % n, at, cols]
            return v.fo.at[self.k, at, cols]

        def spread(self):
            u = self.index
            for half in range(2):
                ref = self.ref(half, r)
                sem = v.zi_recv.at[self.unit.u, half] if self.kind == "in" else v.zo_recv.at[self.k, half]
                me.arrived(ref, sem)
                for d in range(1, X):
                    me.send(ref, ref, v.ax_send.at[u, half, d - 1], v.ax_recv.at[u, half, X - d - 1], (me.x_peer(d), s))
                for d in range(1, Y):
                    me.send(ref, ref, v.ay_send.at[u, half, d - 1], v.ay_recv.at[u, half, Y - d - 1], (me.y_peer(d), s))

        def forward(self):
            u = self.index
            for dx in range(1, X):
                ref = self.ref(0, me.x_peer(dx))
                me.arrived(ref, v.ax_recv.at[u, 0, dx - 1])
                for dy in range(1, Y):
                    me.send(
                        ref, ref, v.af_send.at[u, dy - 1, dx - 1], v.af_recv.at[u, Y - dy - 1, dx - 1], (me.y_peer(dy), s)
                    )
            for dy in range(1, Y):
                ref = self.ref(1, me.y_peer(dy))
                me.arrived(ref, v.ay_recv.at[u, 1, dy - 1])
                for dx in range(1, X):
                    me.send(
                        ref, ref, v.bf_send.at[u, dx - 1, dy - 1], v.bf_recv.at[u, X - dx - 1, dy - 1], (me.x_peer(dx), s)
                    )

        def finish(self):
            u = self.index
            for dy in range(1, Y):
                me.arrived(self.ref(0, me.y_peer(dy)), v.ay_recv.at[u, 0, dy - 1])
            for dx in range(1, X):
                me.arrived(self.ref(1, me.x_peer(dx)), v.ax_recv.at[u, 1, dx - 1])
            for dy in range(1, Y):
                for dx in range(1, X):
                    corner = ((me.y + dy) % Y) * X + (me.x + dx) % X
                    me.arrived(self.ref(0, corner), v.af_recv.at[u, dy - 1, dx - 1])
                    me.arrived(self.ref(1, corner), v.bf_recv.at[u, dx - 1, dy - 1])

    landings_in = [Landing("in", k, k, unit) for k, unit in enumerate(units_hidden_in)]
    landings_out = [Landing("out", i, n + i, unit_attention) for i in range(SLOTS)]
    landings_heads = [Landing("in", k, n + SLOTS + k, unit) for k, unit in enumerate(units_heads)]
    landings = landings_in + landings_out + landings_heads

    line_parts = (v.ct, v.nl)

    def line_begin(a):
        part = line_parts[a]
        for line in range(L):
            me.send(
                chunk(part, 2 * line + 1 - c), v.sbx.at[a, line], v.ls_send.at[a, line], v.ls_recv.at[a, line], me.sibling
            )

    def fetch(src, slot):
        copy = pltpu.make_async_copy(src, v.tmp.at[slot], v.tmp_sem.at[slot])
        copy.start()
        return copy

    def core_sum(a, m):
        part = line_parts[a]
        line = (z + m) % L
        me.arrived(v.sbx.at[a, line], v.ls_recv.at[a, line])
        fetch(v.sbx.at[a, line], m).wait()
        start = (2 * line + c) * rows

        def store(at, total):
            part[shifted(start, at), :] = total.astype(bf16)

        add_rows(store, [lambda at: part[shifted(start, at), :], lambda at: v.tmp[m, at, :]], rows)

    def line_hop(a, e, side):
        part = line_parts[a]
        if side == 0:
            line, inner, nearer = e - (L - 1 - z), has_right, left
            due = jnp.logical_and(line >= 0, line < z)
        else:
            line, inner, nearer = L - 1 - e + z, has_left, right
            due = jnp.logical_and(line > z, line < L)
        line = jnp.clip(line, 0, L - 1)
        start = (2 * line + c) * rows

        @pl.when(both(due, inner))
        def _():
            me.arrived(v.zbx.at[a, side, line], v.lz_recv.at[a, side, line])
            fetch(v.zbx.at[a, side, line], 0).wait()

            def store(at, total):
                part[shifted(start, at), :] = total.astype(bf16)

            add_rows(store, [lambda at: part[shifted(start, at), :], lambda at: v.tmp[0, at, :]], rows)

        me.send(
            part.at[rows_at(start, rows)], v.zbx.at[a, side, line], v.lz_send.at[a, side, e],
            v.lz_recv.at[a, side, line], nearer, due,
        )

    def line_sum(a):
        part = line_parts[a]
        me.arrived(v.sbx.at[a, z], v.ls_recv.at[a, z])
        fetch(v.sbx.at[a, z], 0).wait()
        for side, known in enumerate((has_right, has_left)):
            me.arrived(v.zbx.at[a, side, z], v.lz_recv.at[a, side, z], known)

            @pl.when(known)
            def _():
                fetch(v.zbx.at[a, side, z], 1 + side).wait()

            @pl.when(jnp.logical_not(known))
            def _():
                v.tmp[1 + side] = jnp.zeros((rows, D), bf16)

        def strip(at):
            total = part[shifted(s * rows, at), :].astype(f32)
            for m in range(3):
                total = total + v.tmp[m, at, :].astype(f32)
            return total

        return strip

    def finish_mixed():
        strip = line_sum(0)

        def body(i):
            at = rows_at(i * 16, 16)
            v.block_out[at, :] = (v.tok[at, :].astype(f32) + strip(at) + v.b_out[...]).astype(bf16)

        loop(rows // 16, body)

    def finish_normed():
        strip = line_sum(1)
        v.acc[...] = jnp.zeros(v.acc.shape, f32)

        def body(i):
            at = rows_at(i * 16, 16)
            d_normed = strip(at)
            normed, rstd = normalise(at)
            e = d_normed * v.gain[...]
            back = rstd * (
                e - jnp.mean(e, axis=-1, keepdims=True) - normed * jnp.mean(e * normed, axis=-1, keepdims=True)
            )
            v.grad_tokens[at, :] = (v.cot[at, :].astype(f32) + back).astype(bf16)
            product = d_normed * normed
            v.acc[0] += product[:8] + product[8:]
            v.acc[1] += d_normed[:8] + d_normed[8:]

        loop(rows // 16, body)
        v.v2[:, pl.ds(0, D)] = jnp.sum(v.acc[0], axis=0, keepdims=True)
        v.v2[:, pl.ds(D, D)] = jnp.sum(v.acc[1], axis=0, keepdims=True)

    def to_replicas(vec, got, index):
        for k in range(1, replicas):
            me.send(
                vec, got.at[replicas - k - 1], v.vr_send.at[index, k - 1], v.vr_recv.at[index, replicas - k - 1],
                ((r + k) % replicas, s),
            )

    def from_replicas(vec, got, index):
        for k in range(1, replicas):
            me.arrived(got.at[k - 1], v.vr_recv.at[index, k - 1])
        total = vec[...]
        for k in range(1, replicas):
            total = total + got[k - 1]
        return total

    def biases_begin():
        ones = jnp.ones((8, group), bf16)
        for start in range(0, width, 256):
            size = min(256, width - start)
            v.v1[:, pl.ds(start, size)] = jnp.dot(ones, v.dproj[:, pl.ds(start, size)], preferred_element_type=f32)[:1]
        to_replicas(v.v1, v.got1, 0)

    def bias_out_begin():
        ones = jnp.ones((8, group), bf16)

        def body(i):
            cols = rows_at(i * 256, 256, 256)
            v.v1[:, rows_at(width + i * 256, 256, 256)] = jnp.dot(ones, v.ct[:, cols], preferred_element_type=f32)[:1]

        loop(D // 256, body)

    def biases_share():
        v.v1s[...] = from_replicas(v.v1, v.got1, 0)
        v.gb_out[...] = v.v1s[:, pl.ds(width, D)]
        for part, (src, dst, size) in enumerate(ranges(s)):
            at = rows_at(src, size, 128)
            v.gb_in[:, at] = v.v1s[:, pl.ds(dst, size)]
            for k in range(1, n):
                me.send(
                    v.v1s.at[:, pl.ds(dst, size)], v.gb_in.at[:, at], v.vl_send.at[k - 1, part],
                    v.vl_recv.at[n - k - 1, part], (r, (s + k) % n),
                )

    def biases_end():
        for k in range(1, n):
            for part, (src, _, size) in enumerate(ranges((s + k) % n)):
                me.arrived(v.gb_in.at[:, rows_at(src, size, 128)], v.vl_recv.at[k - 1, part])

    def norms_begin():
        v.v2s[...] = from_replicas(v.v2, v.got2, 1)
        for k in range(1, n):
            me.send(v.v2s, v.got3.at[n - k - 1], v.vn_send.at[k - 1], v.vn_recv.at[n - k - 1], (r, (s + k) % n))

    def norms_end():
        for k in range(1, n):
            me.arrived(v.got3.at[k - 1], v.vn_recv.at[k - 1])
        total = v.v2s[...]
        for k in range(1, n):
            total = total + v.got3[k - 1]
        v.g_gain[...] = total[:, :D]
        v.g_bias[...] = total[:, D:]

    def hop(a, e):
        line_hop(a, e, 0)
        line_hop(a, e, 1)

    events = []
    for unit in units:
        events.append((unit.u, "two", unit, lambda unit=unit: step_two(unit)))
        events.append((unit.u + 1.1, "three", unit, lambda unit=unit: step_three(unit)))
    for landing in landings_in + landings_heads:
        u = landing.unit.u
        events.append((u + 3.2, "four", None, landing.spread))
        events.append((u + 5.3, "five", None, landing.forward))
    for i, landing in enumerate(landings_out):
        u = unit_attention.u + 0.9 * i
        events.append((u + 3.4, "four", None, landing.spread))
        events.append((u + 5.5, "five", None, landing.forward))
    events.sort(key=lambda event: event[0])
    started, doubled = set(), set()

    def begin(unit):
        step_one(unit)
        started.add(unit.u)

    def advance(until):
        while events and events[0][0] <= until:
            _, name, unit, act = events[0]
            if name == "two" and unit.u not in started:
                return
            events.pop(0)
            if name == "two":
                doubled.add(unit.u)
            act()

    ua = unit_attention.u
    for unit in units_hidden_out:
        grad_out(unit)
        begin(unit)
    for k, unit in enumerate(units_hidden_in):
        grad_in(unit)
        begin(unit)
        if k % 4 == 3:
            advance(EAGER[0] * (k // 4 + 1))
    for m in range(tall):
        project_heads(m)
        advance(EAGER[1] + EAGER[2] * (m + 1) * 2 / tall)
    tasks = [(b, pair, side) for b in range(sequences) for pair in range(heads // 2) for side in range(2)]
    for i, (b, pair, side) in enumerate(tasks):
        attend(b, pair, side)
        if side == 1:
            settle_pair(b, pair)
        advance(EAGER[3] + EAGER[4] * (i + 1))
    advance(ua - 2)
    drain_unit(units_hidden_out[0])
    grad_out(unit_attention)
    begin(unit_attention)
    bias_out_begin()
    biases_begin()
    mixed_tiles()
    line_begin(0)
    advance(ua - 1)
    assert all(unit.u in doubled for unit in units_hidden_out + units_hidden_in)
    for unit, past in zip(units_heads, units_hidden_in, strict=True):
        drain_unit(past)
        grad_in(unit)
        begin(unit)
    advance(ua - 0.5)
    for m in range(1, L):
        core_sum(0, m)
    hop(0, 0)
    d_normed_tiles()
    line_begin(1)
    biases_share()
    advance(ua)
    for m in range(1, L):
        core_sum(1, m)
    hop(1, 0)
    for e in range(1, L - 1):
        advance(ua + HOP * e - 0.5)
        hop(0, e)
        advance(ua + HOP * e + 0.5 * HOP - 0.5)
        hop(1, e)
    last = ua + HOP * (L - 1) - 0.5
    advance(last)
    finish_mixed()
    advance(last + 1.5)
    finish_normed()
    to_replicas(v.v2, v.got2, 1)
    advance(last + 2.5)
    norms_begin()
    advance(last + 4)
    norms_end()
    biases_end()
    advance(1000)
    for landing in landings:
        landing.finish()
    for unit in units:
        drain_unit(unit)
    me.drain()


def fused(tokens, ln_gain, ln_bias, w_in, b_own, w_out, b_out, cotangent, cosine, sine):
    n, replicas = lax.axis_size("shard"), lax.axis_size("replica")
    X = max(replicas // 2, 1)
    Y = replicas // X
    L = n // 2
    rows = tokens.shape[0]
    group = rows * n
    depth = D // n
    q = depth // replicas
    head, fc = D // n, FF // n
    head3 = 3 * head
    width = head3 + fc
    both_heads = (group // SEQ_LEN) * (head // HEAD_DIM)
    vmem, dma = pltpu.VMEM, pltpu.SemaphoreType.DMA
    t = n - 2
    most = max(X, Y) - 1
    units = 2 * n + SLOTS
    scratch = {
        "nl": vmem((group, D), bf16), "ct": vmem((group, D), bf16),
        "wi": vmem((D, width), bf16), "wo": vmem((SLOTS * depth, D), bf16),
        "joined": vmem((group, head + fc), bf16), "dproj": vmem((group, width), bf16),
        "flip": vmem((depth, group), bf16),
        "oh": vmem((2, SEQ_LEN, HEAD_DIM), f32), "dq": vmem((2, SEQ_LEN, HEAD_DIM), f32),
        "dk": vmem((2, SEQ_LEN, HEAD_DIM), f32), "dv": vmem((2, SEQ_LEN, HEAD_DIM), f32),
        "g_out": vmem((SLOTS - 1, depth, D), bf16), "g_in": vmem((n, depth, fc), bf16),
        "tmp": vmem((L, rows, D), bf16), "acc": vmem((2, 8, D), f32),
        "v1": vmem((1, width + D), f32), "v1s": vmem((1, width + D), f32), "got1": vmem((replicas - 1, 1, width + D), f32),
        "v2": vmem((1, 2 * D), f32), "v2s": vmem((1, 2 * D), f32), "got2": vmem((replicas - 1, 1, 2 * D), f32),
        "got3": vmem((n - 1, 1, 2 * D), f32),
    }
    for name in ("qh", "kh", "vh", "doh"):
        scratch[name] = vmem((both_heads, SEQ_LEN, HEAD_DIM), bf16)
    for tag, count, wide in (("o", SLOTS, D), ("f", n, fc), ("q", n, head3)):
        a, b = half_of(wide), wide - half_of(wide)
        scratch["r1" + tag + "a"] = vmem((count, X - 1, Y * q, a), bf16)
        scratch["r1" + tag + "b"] = vmem((count, Y - 1, X * q, b), bf16)
        scratch["r2" + tag + "a"] = vmem((count, Y - 1, q, a), bf16)
        scratch["r2" + tag + "b"] = vmem((count, X - 1, q, b), bf16)
    sems = {
        "ag": (2, 2, L), "sib": (2, 2 * L), "ws": (4,), "oz": (SLOTS,),
        "ix": (t, X - 1, 4), "iy": (t, Y - 1, 4), "ia": (t, Y - 1, X - 1, 2), "ib": (t, X - 1, Y - 1, 2),
        "ox": (SLOTS, X - 1, 2), "oy": (SLOTS, Y - 1, 2), "oa": (SLOTS, Y - 1, X - 1, 1), "ob": (SLOTS, X - 1, Y - 1, 1),
        "s1": (units, 2, most), "s2": (units, 2, most), "zi": (units, 2), "zo": (SLOTS, 2),
        "ax": (units, 2, X - 1), "ay": (units, 2, Y - 1),
        "af": (units, Y - 1, X - 1), "bf": (units, X - 1, Y - 1),
        "ls": (2, L), "lz": (2, 2, L), "vr": (2, replicas - 1), "vl": (n - 1, 4), "vn": (n - 1,),
    }
    for name, shape in sems.items():
        scratch[name + "_send"] = dma(shape)
        scratch[name + "_recv"] = dma(shape)
    scratch["wz_send"], scratch["wz_recv"] = dma((t, 4)), dma((t, 2))
    scratch["own_sem"], scratch["tmp_sem"] = dma((5,)), dma((L,))
    any_space, in_vmem = pl.BlockSpec(memory_space=pl.ANY), pl.BlockSpec(memory_space=pltpu.VMEM)
    inputs = {
        "tok": (tokens, in_vmem), "cot": (cotangent, in_vmem), "gain": (ln_gain.reshape(1, D), in_vmem),
        "bias": (ln_bias.reshape(1, D), in_vmem), "b_own": (b_own.reshape(1, width), in_vmem),
        "b_out": (b_out.reshape(1, D), in_vmem), "cosine": (cosine, in_vmem), "sine": (sine, in_vmem),
        "w_in": (w_in, any_space), "w_out": (w_out, any_space),
    }
    shape = jax.ShapeDtypeStruct
    outputs = {
        "fi": (shape((n, depth, width), bf16), any_space), "fo": (shape((SLOTS, depth, D), bf16), any_space),
        "block_out": (shape((rows, D), bf16), in_vmem), "grad_tokens": (shape((rows, D), bf16), in_vmem),
        "gb_in": (shape((1, 3 * D + FF), f32), in_vmem), "gb_out": (shape((1, D), f32), in_vmem),
        "g_gain": (shape((1, D), f32), in_vmem), "g_bias": (shape((1, D), f32), in_vmem),
        "sbx": (shape((2, L, rows, D), bf16), any_space), "zbx": (shape((2, 2, L, rows, D), bf16), any_space),
    }
    return pl.pallas_call(
        functools.partial(fused_kernel, n, replicas, list(inputs) + list(outputs) + list(scratch)),
        out_shape=tuple(out for out, _ in outputs.values()),
        in_specs=[spec for _, spec in inputs.values()],
        out_specs=tuple(spec for _, spec in outputs.values()),
        scratch_shapes=list(scratch.values()),
        compiler_params=pltpu.CompilerParams(collective_id=0, has_side_effects=True, vmem_limit_bytes=63 << 20),
        name="fused",
    )(*[value for value, _ in inputs.values()])


def widen_kernel(n, fi, fo, gi, go, low, wide, in_sem, out_sem):
    depth, width = fi.shape[1], fi.shape[2]
    head, fc = D // n, FF // n
    jobs = [("in", d) for d in range(n)] + [("out", i) for i in range(SLOTS)]

    def load(j):
        kind, i = jobs[j]
        src = fi.at[i] if kind == "in" else fo.at[i]
        return pltpu.make_async_copy(src, low.at[j % 2, :, pl.ds(0, src.shape[1])], in_sem.at[j % 2])

    def stores(j):
        kind, i = jobs[j]
        slot = j % 2
        if kind == "out":
            return [pltpu.make_async_copy(wide.at[slot], go.at[pl.ds(i * depth, depth)], out_sem.at[slot, 0])]
        places = [(part * D + head * i, part * head, head) for part in range(3)] + [(3 * D + fc * i, 3 * head, fc)]
        return [
            pltpu.make_async_copy(wide.at[slot, :, pl.ds(src, size)], gi.at[:, pl.ds(dst, size)], out_sem.at[slot, p])
            for p, (dst, src, size) in enumerate(places)
        ]

    load(0).start()
    for j, (kind, _) in enumerate(jobs):
        if j + 1 < len(jobs):
            load(j + 1).start()
        load(j).wait()
        if j >= 2:
            for copy in stores(j - 2):
                copy.wait()
        size = width if kind == "in" else D

        def body(i, j=j, size=size):
            at = rows_at(i * 16, 16)
            wide[j % 2, at, pl.ds(0, size)] = low[j % 2, at, pl.ds(0, size)].astype(f32)

        loop(depth // 16, body)
        for copy in stores(j):
            copy.start()
    for j in (len(jobs) - 2, len(jobs) - 1):
        for copy in stores(j):
            copy.wait()


def widen(fi, fo):
    n = lax.axis_size("shard")
    depth = fi.shape[1]
    dma = pltpu.SemaphoreType.DMA
    return pl.pallas_call(
        functools.partial(widen_kernel, n),
        out_shape=(
            jax.ShapeDtypeStruct((depth, 3 * D + FF), f32),
            jax.ShapeDtypeStruct((SLOTS * depth, D), f32),
        ),
        in_specs=[pl.BlockSpec(memory_space=pltpu.HBM)] * 2,
        out_specs=(pl.BlockSpec(memory_space=pltpu.HBM),) * 2,
        scratch_shapes=[
            pltpu.VMEM((2, depth, D), bf16), pltpu.VMEM((2, depth, D), f32), dma((2,)), dma((2, 4)),
        ],
        compiler_params=pltpu.CompilerParams(vmem_limit_bytes=60 << 20),
        name="widen",
    )(fi, fo)


def own_columns(vector, s, n):
    head, fc = D // n, FF // n
    parts = [lax.dynamic_slice_in_dim(vector, part * D + s * head, head) for part in range(3)]
    return jnp.concatenate(parts + [lax.dynamic_slice_in_dim(vector, 3 * D + s * fc, fc)])


def local(tokens, ln_gain, ln_bias, w_in, b_in, w_out, b_out, cotangent):
    n = lax.axis_size("shard")
    s = lax.axis_index("shard")
    lane = jnp.arange(128) % HEAD_DIM
    frequency = 10000.0 ** (-(2.0 * (lane % (ROT // 2))).astype(f32) / ROT)
    angle = jnp.arange(SEQ_LEN).astype(f32)[:, None] * frequency[None, :]
    rotary = (lane < ROT)[None, :]
    cosine = jnp.where(rotary, jnp.cos(angle), 1.0)
    sine = jnp.where(rotary, jnp.sin(angle), 0.0)
    fi, fo, block_out, grad_tokens, gb_in, gb_out, g_gain, g_bias, _, _ = fused(
        tokens, ln_gain, ln_bias, w_in, own_columns(b_in, s, n), w_out, b_out, cotangent, cosine, sine
    )
    grad_w_in, grad_w_out = widen(fi, fo)
    return (
        block_out, grad_tokens, g_gain.reshape(D), g_bias.reshape(D),
        grad_w_in, gb_in.reshape(3 * D + FF), grad_w_out, gb_out.reshape(D),
    )


def solution(mesh):
    both_axes = P(("replica", "shard"), None)
    return jax.shard_map(
        local,
        mesh=mesh,
        in_specs=(both_axes, P(), P(), P("shard", None), P(), P("shard", None), P(), both_axes),
        out_specs=(both_axes, both_axes, P(), P(), P("shard", None), P(), P("shard", None), P()),
        check_vma=False,
    )
```

```python
import functools
import jax
import jax.numpy as jnp
import numpy as np
from jax import lax
from jax.experimental import pallas as pl
from jax.experimental.pallas import tpu as pltpu
from jax.sharding import PartitionSpec as P

D = 2048
HEADS = 32
HEAD_DIM = 64
ROT = 32
FF = 8192
SEQ_LEN = 1024
SLOTS = 5

epsilon = 1e-05
masked_score = -1e30
MESH = pl.DeviceIdType.MESH
f32 = jnp.float32
bf16 = jnp.bfloat16


class Place:
    def __init__(self, n, replicas):
        self.n, self.R = n, replicas
        self.X = max(replicas // 2, 1)
        self.Y = replicas // self.X
        self.L = n // 2
        self.r, self.s = lax.axis_index("replica"), lax.axis_index("shard")
        self.x, self.y = self.r % self.X, self.r // self.X
        self.z, self.c = self.s // 2, self.s % 2
        self.sibling = (self.r, self.s + 1 - 2 * self.c)
        self.pool, self.used, self.turn = None, {}, 0

    def x_peer(self, dx):
        return self.y * self.X + (self.x + dx) % self.X

    def y_peer(self, dy):
        return ((self.y + dy) % self.Y) * self.X + self.x

    def send(self, src, dst, recv_sem, device, when=None):
        turn = self.turn % self.pool.shape[0]
        self.turn += 1
        self.sent(turn)
        copy = pltpu.make_async_remote_copy(
            src_ref=src, dst_ref=dst, send_sem=self.pool.at[turn], recv_sem=recv_sem,
            device_id=device, device_id_type=MESH,
        )
        guarded(when, copy.start)
        self.used[turn] = (when, copy.wait_send)
        return turn, copy

    def sent(self, turn, copy=None):
        if turn in self.used and (copy is None or self.used[turn][1].__self__ is copy):
            when, wait = self.used.pop(turn)
            guarded(when, wait)

    def local(self, src, dst, sem, when=None):
        guarded(when, pltpu.make_async_copy(src, dst, sem).start)

    def arrived(self, ref, sem, when=None):
        guarded(when, pltpu.make_async_copy(ref, ref, sem).wait)

    def drain(self):
        for turn in sorted(self.used):
            self.sent(turn)

    def meet(self, line=True, square=True, whole=False):
        barrier = pltpu.get_barrier_semaphore()
        peers = []
        if line:
            peers += [(self.r, (self.s + k) % self.n) for k in range(1, self.n)]
        if whole:
            peers += [((self.r + k) % self.R, self.s) for k in range(1, self.R)]
        elif square:
            peers += [(self.x_peer(dx), self.s) for dx in range(1, self.X)]
            peers += [(self.y_peer(dy), self.s) for dy in range(1, self.Y)]
        for peer in peers:
            pl.semaphore_signal(barrier, inc=1, device_id=peer, device_id_type=MESH)
        pl.semaphore_wait(barrier, len(peers))


def guarded(when, act):
    if when is None:
        act()
    else:
        pl.when(when)(act)


def both(a, b):
    return b if a is None else a if b is None else jnp.logical_and(a, b)


def rows_at(start, size, multiple=16):
    return pl.ds(pl.multiple_of(start, multiple), size)


def half_of(width):
    return -(-width // 256) * 128


def slot_of(block, n):
    past = jnp.maximum(block - n, 0)
    first = block < n
    return jnp.where(first, block, past // 4), jnp.where(first, 0, 1 + past % 4)


def block_of(device, slot, n):
    return device if slot == 0 else n + 4 * device + slot - 1


UP = 0.7978845608028654
NT = (((1,), (1,)), ((), ()))
TALL = 512
EAGER = (1.0, 2.0, 1.0, 4.0, 1.5)
HOP = 2.5


POOL = 96
LOADED = ("tok", "gain", "bias", "b_in", "cot", "b_out", "cosine", "sine")
GIVEN = ("block_out", "grad_tokens", "gb_out", "g_gain", "g_bias")


class Names:
    def __init__(self, names, refs):
        for name, ref in zip(names, refs, strict=True):
            setattr(self, name, ref)


class Unit:
    def __init__(self, kind, k, buf, width, col0, one, two):
        self.kind, self.k, self.buf, self.width, self.col0 = kind, k, buf, width, col0
        cut = half_of(width)
        self.halves = ((0, cut), (cut, width - cut))
        self.one, self.two = one, two
        self.sent = []


def loop(count, body):
    def step(i, carry):
        body(i)
        return carry

    lax.fori_loop(0, count, step, 0)


def add_rows(store, loads, rows, strip=16):
    def step(i):
        at = rows_at(i * strip, strip)
        total = loads[0](at).astype(f32)
        for load in loads[1:]:
            total = total + load(at).astype(f32)
        store(at, total)

    loop(rows // strip, step)


def shifted(start, at):
    return pl.ds(pl.multiple_of(start + at.start, 16), at.size)


def fused_kernel(n, replicas, names, *refs):
    v = Names(names, refs)
    me = Place(n, replicas)
    me.pool = v.pool
    X, Y, L, r, s, z, c = me.X, me.Y, me.L, me.r, me.s, me.z, me.c
    rows = v.tok.shape[0]
    group = rows * n

    def loaded(*picked):
        for name in picked:
            me.arrived(getattr(v, name), v.load_sem.at[LOADED.index(name)])

    def give(name):
        me.local(getattr(v, name), getattr(v, "to_" + name), v.give_sem.at[GIVEN.index(name)])

    for i, name in enumerate(LOADED):
        me.local(getattr(v, "far_" + name), getattr(v, name), v.load_sem.at[i])
    depth = D // n
    q = depth // replicas
    head, fc = D // n, FF // n
    heads = head // HEAD_DIM
    sequences = group // SEQ_LEN
    head3 = 3 * head
    width = head3 + fc
    tall = group // TALL
    me.meet(whole=True)

    def chunk(ref, owner):
        return ref.at[rows_at(owner * rows, rows)]

    def ranges(device):
        return [(part * D + head * device, part * head, head) for part in range(3)] + [
            (3 * D + fc * device, head3, fc)
        ]

    order = list(range(L // 2, L)) + list(range(1, L // 2))

    def far(t):
        chip, m, bit = 0, order[t // 2], 1
        while bit < L:
            chip = chip + ((z // bit + m // bit) % 2) * bit
            bit *= 2
        return 2 * chip + t % 2

    pairs = (v.nl, v.ct)
    has_left, has_right = z > 0, z < L - 1
    left, right = (r, jnp.maximum(s - 2, 0)), (r, jnp.minimum(s + 2, n - 1))

    def spread_own(a, own):
        every = pairs[a]
        me.send(own, chunk(every, s), v.ag_recv.at[a, 0, 1], right, has_right)
        me.send(own, chunk(every, s), v.ag_recv.at[a, 1, 1], left, has_left)
        me.send(own, chunk(every, s), v.sib_recv.at[a, 0], me.sibling)

    me.local(v.far_cot, chunk(v.ct, s), v.own_sem.at[0])

    def send_far(t, which):
        device = far(t)
        back = 2 * (t // 2) + c
        for part, (src, dst, size) in enumerate(ranges(device)):
            if (part == 3) == (which == "fc"):
                me.send(
                    v.w_in.at[rows_at(r * q, q), rows_at(src, size, 128)],
                    v.wi.at[rows_at(s * depth + r * q, q), pl.ds(dst, size)], v.wz_recv.at[back, part // 3], (r, device))

    for t in range(n - 2):
        send_far(t, "fc")

    for i in range(SLOTS):
        device, slot = slot_of(SLOTS * s + i, n)
        mine = device == s
        near = jnp.logical_and(device // 2 == z, device != s)
        away = device // 2 != z
        full = v.wo.at[rows_at(slot * depth, depth)]
        me.local(v.w_out.at[pl.ds(i * depth, depth)], full, v.oz_recv.at[slot], mine)
        me.send(v.w_out.at[pl.ds(i * depth, depth)], full, v.oz_recv.at[slot], me.sibling, near)
        target = jnp.where(away, device, (s + 2) % n)
        me.send(
            v.w_out.at[rows_at(i * depth + r * q, q)], v.wo.at[rows_at(slot * depth + r * q, q)], v.oz_recv.at[slot], (r, target), away)
    for t in range(n - 2):
        send_far(t, "qkv")
    def normalise(at):
        wide = v.tok[at, :].astype(f32)
        centred = wide - jnp.mean(wide, axis=-1, keepdims=True)
        rstd = lax.rsqrt(jnp.mean(centred * centred, axis=-1, keepdims=True) + epsilon)
        return centred * rstd, rstd

    def norm_strip(i):
        at = rows_at(i * 16, 16)
        normed, _ = normalise(at)
        v.nl[rows_at(s * rows + i * 16, 16), :] = (normed * v.gain[...] + v.bias[...]).astype(bf16)

    loaded("tok", "gain", "bias", "b_in")
    loop(rows // 16, norm_strip)
    for src, dst, size in ranges(s):
        v.b_own[:, pl.ds(dst, size)] = v.b_in[:, rows_at(src, size, 128)]

    for part, (src, dst, size) in enumerate(ranges(s)):
        me.local(
            v.w_in.at[:, rows_at(src, size, 128)], v.wi.at[rows_at(s * depth, depth), pl.ds(dst, size)],
            v.own_sem.at[1 + part],
        )
    for part, (src, dst, size) in enumerate(ranges(me.sibling[1])):
        me.send(
            v.w_in.at[:, rows_at(src, size, 128)], v.wi.at[rows_at(s * depth, depth), pl.ds(dst, size)], v.ws_recv.at[0], me.sibling)

    def share(ref_of, halves, index, tag, when=None):
        come, rest = getattr(v, tag + "_come"), getattr(v, tag + "_rest")

        def direct(picked):
            for h in picked:
                ref = ref_of(r, *halves[h])
                for dx in range(1, X):
                    sem = come.at[index, h, X - dx - 1] if h % 2 == 0 else rest.at[index, h]
                    me.send(ref, ref, sem, (me.x_peer(dx), s), when)
                for dy in range(1, Y):
                    sem = rest.at[index, h] if h % 2 == 0 else come.at[index, h, Y - dy - 1]
                    me.send(ref, ref, sem, (me.y_peer(dy), s), when)

        def forward(picked):
            for h in picked:
                for d in range(1, X if h % 2 == 0 else Y):
                    ref = ref_of(me.x_peer(d) if h % 2 == 0 else me.y_peer(d), *halves[h])
                    me.arrived(ref, come.at[index, h, d - 1], when)
                    for e in range(1, Y if h % 2 == 0 else X):
                        peer = me.y_peer(e) if h % 2 == 0 else me.x_peer(e)
                        me.send(ref, ref, rest.at[index, h], (peer, s), when)

        def finish(picked):
            for h in picked:
                count = X * (Y - 1) if h % 2 == 0 else Y * (X - 1)
                me.arrived(ref_of(0, *halves[h], count), rest.at[index, h], when)

        return direct, forward, finish

    fc_half, qkv_half = half_of(fc), half_of(head3)
    halves_in = (
        (head3, fc_half), (head3 + fc_half, fc - fc_half), (0, qkv_half), (qkv_half, head3 - qkv_half),
    )

    def in_piece(t):
        def ref_of(replica, start, size, count=1):
            return v.wi.at[rows_at(far(t) * depth + replica * q, count * q), pl.ds(start, size)]

        return share(ref_of, halves_in, t, "i")

    def in_arrived(t, part):
        base = rows_at(far(t) * depth + r * q, q)
        if part == "fc":
            me.arrived(v.wi.at[base, pl.ds(head3, fc)], v.wz_recv.at[t, 1])
        else:
            me.arrived(v.wi.at[base, pl.ds(0, head3)], v.wz_recv.at[t, 0])

    out_half = half_of(D)
    halves_out = ((0, out_half), (out_half, D - out_half))

    def out_piece(j):
        source = block_of(s, j, n) // SLOTS

        def ref_of(replica, start, size, count=1):
            return v.wo.at[rows_at(j * depth + replica * q, count * q), pl.ds(start, size)]

        return share(ref_of, halves_out, j, "o", source // 2 != z)

    def out_arrived(j):
        source = block_of(s, j, n) // SLOTS
        me.arrived(v.wo.at[rows_at(j * depth + r * q, q)], v.oz_recv.at[j], source // 2 != z)
        me.arrived(v.wo.at[pl.ds(j * depth, depth)], v.oz_recv.at[j], source // 2 == z)

    def pass_on(k, a):
        every = pairs[a]
        for side, (source, there, onward) in enumerate(((s - 2 * k, right, has_right), (s + 2 * k, left, has_left))):
            known = (z - k >= 0) if side == 0 else (z + k < L)
            ref = chunk(every, jnp.clip(source, 0, n - 1))
            me.arrived(ref, v.ag_recv.at[a, side, k], known)
            if k < L - 1:
                me.send(ref, ref, v.ag_recv.at[a, side, k + 1], there, both(known, onward))
            me.send(
                ref, ref, v.sib_recv.at[a, 2 * k - 1 + side], me.sibling, known
            )

    def hidden_rows(chip, when=None):
        at = rows_at(jnp.clip(chip, 0, L - 1) * (2 * rows), 2 * rows)

        def body(j):
            cols = rows_at(head3 + 256 * j, 256, 128)
            x = jnp.dot(v.nl[at, :], v.wi[:, cols], preferred_element_type=f32) + v.b_own[:, cols]
            square = x * x
            t = jnp.tanh(UP * (x + 0.044715 * (square * x)))
            v.joined[at, rows_at(head + 256 * j, 256, 128)] = (0.5 * x * (1.0 + t)).astype(bf16)
            slope = 0.5 * (1.0 + t) + 0.5 * x * (1.0 - t * t) * (UP * (1.0 + (3 * 0.044715) * square))
            d_hidden = lax.dot_general(
                v.ct[at, :], v.wo[rows_at(depth + 256 * j, 256, 128), :], NT, preferred_element_type=f32
            )
            v.dproj[at, cols] = (d_hidden * slope).astype(bf16)

        guarded(when, lambda: loop(fc // 256, body))

    ins = [in_piece(t) for t in range(n - 2)]
    outs = [out_piece(j) for j in range(SLOTS)]
    fc_h, qkv_h = (0, 1), (2, 3)
    arrivals, steps = [], []
    for t in range(n - 2):
        arrivals.append((lambda t=t: (in_arrived(t, "fc"), ins[t][0](fc_h)), lambda t=t: ins[t][1](fc_h)))
    for j in range(SLOTS):
        arrivals.append((lambda j=j: (out_arrived(j), outs[j][0](fc_h)), lambda j=j: outs[j][1](fc_h)))
    for t in range(n - 2):
        arrivals.append((lambda t=t: (in_arrived(t, "qkv"), ins[t][0](qkv_h)), lambda t=t: ins[t][1](qkv_h)))
    for i, (first, then) in enumerate(arrivals):
        steps.append((i, first))
        steps.append((i + 2.5, then))
    steps.append((8.2, lambda: (loaded("cot", "b_out", "cosine", "sine"), spread_own(1, v.cot), spread_own(0, chunk(v.nl, s)))))
    for k in range(1, L - 1):
        steps.append((8.1 + 4 * k, lambda k=k: pass_on(k, 1)))
        steps.append((8.2 + 4 * k, lambda k=k: pass_on(k, 0)))
    for _, step in sorted(steps, key=lambda pair: pair[0]):
        step()
    other = me.sibling[1]

    def rows_there(k):
        for every in (v.nl, v.ct):
            a = 0 if every is v.nl else 1
            if k == 0:
                me.arrived(chunk(every, other), v.sib_recv.at[a, 0])
                continue
            for side in range(2):
                source = other - 2 * k if side == 0 else other + 2 * k
                known = (z - k >= 0) if side == 0 else (z + k < L)
                me.arrived(chunk(every, jnp.clip(source, 0, n - 1)), v.sib_recv.at[a, 2 * k - 1 + side], known)

    me.arrived(chunk(v.ct, s), v.own_sem.at[0])
    for piece in ins:
        piece[2](fc_h)
    for piece in outs:
        piece[2](fc_h)
    for part, (_, dst, size) in enumerate(ranges(s)):
        me.arrived(v.wi.at[rows_at(s * depth, depth), pl.ds(dst, size)], v.own_sem.at[1 + part])
    me.arrived(v.wi.at[rows_at(other * depth, depth), :], v.ws_recv.at[0])
    for k in range(L):
        if k == L - 1:
            pass_on(k, 1)
            pass_on(k, 0)
        rows_there(k)
        if k == 0:
            hidden_rows(z)
        else:
            hidden_rows(z - k, z - k >= 0)
            hidden_rows(z + k, z + k < L)
    for piece in ins:
        piece[2](qkv_h)
    me.drain()

    def tile(i, size=TALL):
        return rows_at(i * size, size)

    def turned_columns(ref, start, size):
        def body(m):
            v.flip[:size, rows_at(m * 256, 256, 256)] = jnp.transpose(ref[tile(m, 256), pl.ds(start, size)])

        loop(group // 256, body)

    def turned_rows(start):
        def body(m):
            v.flip[:depth, rows_at(m * 256, 256, 256)] = jnp.transpose(v.nl[tile(m, 256), rows_at(start, depth, 128)])

        loop(group // 256, body)

    def grad_out(unit):
        turned_columns(v.joined, depth * unit.k, depth)

        def body(m):
            cols = rows_at(m * 512, 512, 512)
            unit.buf[:, cols] = jnp.dot(v.flip[:depth, :], v.ct[:, cols], preferred_element_type=f32).astype(bf16)

        loop(D // 512, body)

    def grad_in(unit):
        turned_rows(((s + unit.k) % n) * depth)
        for start in range(0, unit.width, 256):
            size = min(256, unit.width - start)
            unit.buf[:, pl.ds(start, size)] = jnp.dot(
                v.flip[:depth, :], v.dproj[:, pl.ds(unit.col0 + start, size)], preferred_element_type=f32
            ).astype(bf16)

    def lanes_turn(x, at, sign):
        lane = lax.broadcasted_iota(jnp.int32, x.shape, 1) % HEAD_DIM
        sine = v.sine[at, :] * sign
        swapped = jnp.where(lane < ROT // 2, -pltpu.roll(x, 128 - ROT // 2, 1), pltpu.roll(x, ROT // 2, 1))
        return x * v.cosine[at, :] + swapped * sine

    def project_heads(m):
        at = pl.ds((m % (SEQ_LEN // TALL)) * TALL, TALL)
        for slab in range(head3 // 128):
            cols = pl.ds(128 * slab, 128)
            x = jnp.dot(v.nl[tile(m), :], v.wi[:, cols], preferred_element_type=f32) + v.b_own[:, cols]
            part, first = slab // (head // 128), 2 * (slab % (head // 128))
            if part < 2:
                x = lanes_turn(x, at, 1.0)
            x = x.astype(bf16)
            to = (v.qh, v.kh, v.vh)[part]
            base = (m // (SEQ_LEN // TALL)) * heads + first
            to[base, at, :] = x[:, :HEAD_DIM]
            to[base + 1, at, :] = x[:, HEAD_DIM:]
        for slab in range(head // 128):
            x = lax.dot_general(
                v.ct[tile(m), :], v.wo[pl.ds(128 * slab, 128), :], NT, preferred_element_type=f32
            ).astype(bf16)
            base = (m // (SEQ_LEN // TALL)) * heads + 2 * slab
            v.doh[base, at, :] = x[:, :HEAD_DIM]
            v.doh[base + 1, at, :] = x[:, HEAD_DIM:]

    scale = HEAD_DIM ** (-0.5)
    block = 256

    def attend(b, pair, side):
        hb = b * heads + 2 * pair + side
        key_turned = jnp.transpose(v.kh[hb])
        value_turned = jnp.transpose(v.vh[hb])
        v.dk[side] = jnp.zeros((SEQ_LEN, HEAD_DIM), f32)
        v.dv[side] = jnp.zeros((SEQ_LEN, HEAD_DIM), f32)
        for i in range(SEQ_LEN // block):
            at, past = pl.ds(i * block, block), (i + 1) * block
            query, d_out = v.qh[hb, at, :], v.doh[hb, at, :]
            scores = lax.dot_general(v.kh[hb, :past, :], query, NT, preferred_element_type=f32) * scale
            key_place = lax.broadcasted_iota(jnp.int32, (past, block), 0)
            query_place = lax.broadcasted_iota(jnp.int32, (past, block), 1) + i * block
            scores = jnp.where(key_place <= query_place, scores, masked_score)
            raised = jnp.exp(scores - jnp.max(scores, axis=0, keepdims=True))
            chances = raised * (1.0 / jnp.sum(raised, axis=0, keepdims=True))
            low = chances.astype(bf16)
            out_turned = jnp.dot(value_turned[:, :past], low, preferred_element_type=f32)
            d_out_turned = jnp.transpose(d_out.astype(f32))
            delta = jnp.sum(d_out_turned * out_turned, axis=0, keepdims=True)
            d_chances = lax.dot_general(v.vh[hb, :past, :], d_out, NT, preferred_element_type=f32)
            d_scores = (chances * (d_chances - delta)).astype(bf16)
            v.oh[side, at, :] = jnp.transpose(out_turned)
            d_query_turned = jnp.dot(key_turned[:, :past], d_scores, preferred_element_type=f32) * scale
            v.dq[side, at, :] = jnp.transpose(d_query_turned)
            v.dk[side, :past, :] += jnp.dot(d_scores, query, preferred_element_type=f32) * scale
            v.dv[side, :past, :] += jnp.dot(low, d_out, preferred_element_type=f32)

    def settle_pair(b, pair):
        def settle(m):
            at = tile(m, 256)
            put = rows_at(b * SEQ_LEN + m * 256, 256)

            def slab(ref):
                return jnp.concatenate([ref[0, at, :], ref[1, at, :]], axis=1)

            v.joined[put, pl.ds(128 * pair, 128)] = slab(v.oh).astype(bf16)
            v.dproj[put, pl.ds(128 * pair, 128)] = lanes_turn(slab(v.dq), at, -1.0).astype(bf16)
            v.dproj[put, pl.ds(head + 128 * pair, 128)] = lanes_turn(slab(v.dk), at, -1.0).astype(bf16)
            v.dproj[put, pl.ds(2 * head + 128 * pair, 128)] = slab(v.dv).astype(bf16)

        loop(SEQ_LEN // 256, settle)

    def mixed_tiles():
        def body(i):
            m, cols = i % tall, rows_at((i // tall) * 256, 256, 256)
            v.ct[tile(m), cols] = jnp.dot(v.joined[tile(m), :], v.wo[:, cols], preferred_element_type=f32).astype(bf16)

        loop(tall * (D // 256), body)

    def d_normed_tiles():
        def body(i):
            m, at = i % tall, (i // tall) * 256
            v.nl[tile(m), rows_at(at, 256, 256)] = lax.dot_general(
                v.dproj[tile(m), :], v.wi[rows_at(at, 256, 256), :], NT, preferred_element_type=f32
            ).astype(bf16)

        loop(tall * (D // 256), body)

    def quarter(half, replica):
        x, y = replica % X, replica // X
        return x * Y + y if half == 0 else y * X + x

    units_hidden_out = [
        Unit("out", j, v.g_out.at[j - 1], D, 0, (v.r1oa, v.r1ob), (v.r2oa, v.r2ob)) for j in range(1, SLOTS)
    ]
    units_hidden_in = [
        Unit("in", k, v.g_in.at[k], fc, head3, (v.r1fa, v.r1fb), (v.r2fa, v.r2fb)) for k in range(n)
    ]
    unit_attention = Unit("out", 0, v.g_out.at[0], D, 0, (v.r1oa, v.r1ob), (v.r2oa, v.r2ob))
    units_heads = [
        Unit("in", k, v.g_in.at[k, :, pl.ds(0, head3)], head3, 0, (v.r1qa, v.r1qb), (v.r2qa, v.r2qb)) for k in range(n)
    ]
    units = units_hidden_out + units_hidden_in + [unit_attention] + units_heads
    for u, unit in enumerate(units):
        unit.u = u

    def step_one(unit):
        unit.sent = []
        for half, (start, size) in enumerate(unit.halves):
            run = (Y if half == 0 else X) * q
            span = X if half == 0 else Y
            for d in range(1, span):
                peer = me.x_peer(d) if half == 0 else me.y_peer(d)
                place = (me.x + d) % X if half == 0 else (me.y + d) % Y
                unit.sent.append(me.send(
                    unit.buf.at[rows_at(place * run, run), pl.ds(start, size)],
                    unit.one[half].at[unit.k, span - d - 1], v.s1_recv.at[unit.u, half, span - d - 1], (peer, s)))

    def drain_unit(unit):
        for turn, copy in unit.sent:
            me.sent(turn, copy)

    def step_two(unit):
        for half, (start, size) in enumerate(unit.halves):
            run = (Y if half == 0 else X) * q
            span = X if half == 0 else Y
            place = me.x if half == 0 else me.y
            got, k = unit.one[half], unit.k
            for d in range(1, span):
                me.arrived(got.at[k, d - 1], v.s1_recv.at[unit.u, half, d - 1])

            def own(at):
                return unit.buf[shifted(place * run, at), pl.ds(start, size)]

            def store(at, total):
                got[k, 0, at, :] = total.astype(bf16)

            add_rows(store, [own] + [lambda at, d=d: got[k, d - 1, at, :] for d in range(1, span)], run)
            span2 = Y if half == 0 else X
            for d in range(1, span2):
                peer = me.y_peer(d) if half == 0 else me.x_peer(d)
                place2 = (me.y + d) % Y if half == 0 else (me.x + d) % X
                me.send(
                    got.at[k, 0, rows_at(place2 * q, q)], unit.two[half].at[k, span2 - d - 1], v.s2_recv.at[unit.u, half, span2 - d - 1], (peer, s))

    def arrive_sems(unit):
        return unit.u

    def step_three(unit):
        for half, (start, size) in enumerate(unit.halves):
            span2 = Y if half == 0 else X
            place2 = me.y if half == 0 else me.x
            kept, got, k = unit.one[half], unit.two[half], unit.k
            for d in range(1, span2):
                me.arrived(got.at[k, d - 1], v.s2_recv.at[unit.u, half, d - 1])

            def own(at):
                return kept[k, 0, shifted(place2 * q, at), :]

            def store(at, total):
                got[k, 0, at, :] = total.astype(bf16)

            add_rows(store, [own] + [lambda at, d=d: got[k, d - 1, at, :] for d in range(1, span2)], q)
            at = rows_at(quarter(half, r) * q, q)
            cols = pl.ds(unit.col0 + start, size)
            if unit.kind == "in":
                dst = v.fi.at[s, at, cols]
                if k == 0:
                    me.local(got.at[k, 0], dst, v.zi_recv.at[unit.u])
                else:
                    me.send(
                        got.at[k, 0], dst, v.zi_recv.at[unit.u], (r, (s + k) % n)
                    )
            else:
                natural = block_of(s, k, n)
                device, i = natural // SLOTS, natural % SLOTS
                dst = v.fo.at[i, at, cols]
                me.local(got.at[k, 0], dst, v.zo_recv.at[i], device == s)
                target = jnp.where(device == s, (s + 1) % n, device)
                me.send(got.at[k, 0], dst, v.zo_recv.at[i], (r, target), device != s)

    class Landing:
        def __init__(self, kind, k, index, unit):
            self.kind, self.k, self.index, self.unit = kind, k, index, unit

        def ref(self, half, replica):
            at = rows_at(quarter(half, replica) * q, q)
            start, size = self.unit.halves[half]
            cols = pl.ds(self.unit.col0 + start, size)
            if self.kind == "in":
                return v.fi.at[(s - self.k) % n, at, cols]
            return v.fo.at[self.k, at, cols]

        def rows(self, half, count):
            start, size = self.unit.halves[half] if half is not None else (0, self.unit.width)
            cols = pl.ds(self.unit.col0 + start, size)
            if self.kind == "in":
                return v.fi.at[(s - self.k) % n, pl.ds(0, count * q), cols]
            return v.fo.at[self.k, pl.ds(0, count * q), cols]

        def spread(self):
            u = self.index
            me.arrived(self.rows(None, 1), v.zi_recv.at[self.unit.u] if self.kind == "in" else v.zo_recv.at[self.k])
            for half in range(2):
                ref = self.ref(half, r)
                for d in range(1, X):
                    sem = v.a_come.at[u, 0, X - d - 1] if half == 0 else v.a_rest.at[u, 1]
                    me.send(ref, ref, sem, (me.x_peer(d), s))
                for d in range(1, Y):
                    sem = v.a_rest.at[u, 0] if half == 0 else v.a_come.at[u, 1, Y - d - 1]
                    me.send(ref, ref, sem, (me.y_peer(d), s))

        def forward(self):
            u = self.index
            for half in range(2):
                for d in range(1, X if half == 0 else Y):
                    ref = self.ref(half, me.x_peer(d) if half == 0 else me.y_peer(d))
                    me.arrived(ref, v.a_come.at[u, half, d - 1])
                    for e in range(1, Y if half == 0 else X):
                        peer = me.y_peer(e) if half == 0 else me.x_peer(e)
                        me.send(ref, ref, v.a_rest.at[u, half], (peer, s))

        def finish(self):
            for half in range(2):
                count = X * (Y - 1) if half == 0 else Y * (X - 1)
                me.arrived(self.rows(half, count), v.a_rest.at[self.index, half])

    landings_in = [Landing("in", k, k, unit) for k, unit in enumerate(units_hidden_in)]
    landings_out = [Landing("out", i, n + i, unit_attention) for i in range(SLOTS)]
    landings_heads = [Landing("in", k, n + SLOTS + k, unit) for k, unit in enumerate(units_heads)]
    landings = landings_in + landings_out + landings_heads

    line_parts = (v.ct, v.nl)

    def line_begin(a):
        part = line_parts[a]
        for line in range(L):
            me.send(
                chunk(part, 2 * line + 1 - c), v.sbx.at[a, line], v.ls_recv.at[a, line], me.sibling
            )

    def fetch(src, slot):
        copy = pltpu.make_async_copy(src, v.tmp.at[slot], v.tmp_sem.at[slot])
        copy.start()
        return copy

    def core_sum(a, m):
        part = line_parts[a]
        line = (z + m) % L
        me.arrived(v.sbx.at[a, line], v.ls_recv.at[a, line])
        fetch(v.sbx.at[a, line], m).wait()
        start = (2 * line + c) * rows

        def store(at, total):
            part[shifted(start, at), :] = total.astype(bf16)

        add_rows(store, [lambda at: part[shifted(start, at), :], lambda at: v.tmp[m, at, :]], rows)

    def line_hop(a, e, side):
        part = line_parts[a]
        if side == 0:
            line, inner, nearer = e - (L - 1 - z), has_right, left
            due = jnp.logical_and(line >= 0, line < z)
        else:
            line, inner, nearer = L - 1 - e + z, has_left, right
            due = jnp.logical_and(line > z, line < L)
        line = jnp.clip(line, 0, L - 1)
        start = (2 * line + c) * rows

        @pl.when(both(due, inner))
        def _():
            me.arrived(v.zbx.at[a, side, line], v.lz_recv.at[a, side, line])
            fetch(v.zbx.at[a, side, line], 0).wait()

            def store(at, total):
                part[shifted(start, at), :] = total.astype(bf16)

            add_rows(store, [lambda at: part[shifted(start, at), :], lambda at: v.tmp[0, at, :]], rows)

        me.send(
            part.at[rows_at(start, rows)], v.zbx.at[a, side, line],
            v.lz_recv.at[a, side, line], nearer, due)

    def line_sum(a):
        part = line_parts[a]
        me.arrived(v.sbx.at[a, z], v.ls_recv.at[a, z])
        fetch(v.sbx.at[a, z], 0).wait()
        for side, known in enumerate((has_right, has_left)):
            me.arrived(v.zbx.at[a, side, z], v.lz_recv.at[a, side, z], known)

            @pl.when(known)
            def _():
                fetch(v.zbx.at[a, side, z], 1 + side).wait()

            @pl.when(jnp.logical_not(known))
            def _():
                v.tmp[1 + side] = jnp.zeros((rows, D), bf16)

        def strip(at):
            total = part[shifted(s * rows, at), :].astype(f32)
            for m in range(3):
                total = total + v.tmp[m, at, :].astype(f32)
            return total

        return strip

    def finish_mixed():
        strip = line_sum(0)

        def body(i):
            at = rows_at(i * 16, 16)
            v.block_out[at, :] = (v.tok[at, :].astype(f32) + strip(at) + v.b_out[...]).astype(bf16)

        loop(rows // 16, body)
        give("block_out")

    def finish_normed():
        strip = line_sum(1)
        v.acc[...] = jnp.zeros(v.acc.shape, f32)

        def body(i):
            at = rows_at(i * 16, 16)
            d_normed = strip(at)
            normed, rstd = normalise(at)
            e = d_normed * v.gain[...]
            back = rstd * (
                e - jnp.mean(e, axis=-1, keepdims=True) - normed * jnp.mean(e * normed, axis=-1, keepdims=True)
            )
            v.grad_tokens[at, :] = (v.cot[at, :].astype(f32) + back).astype(bf16)
            product = d_normed * normed
            v.acc[0] += product[:8] + product[8:]
            v.acc[1] += d_normed[:8] + d_normed[8:]

        loop(rows // 16, body)
        give("grad_tokens")
        v.v2[:, pl.ds(0, D)] = jnp.sum(v.acc[0], axis=0, keepdims=True)
        v.v2[:, pl.ds(D, D)] = jnp.sum(v.acc[1], axis=0, keepdims=True)

    def to_replicas(vec, got, index):
        for k in range(1, replicas):
            me.send(
                vec, got.at[replicas - k - 1], v.vr_recv.at[index, replicas - k - 1],
                ((r + k) % replicas, s))

    def from_replicas(vec, got, index):
        for k in range(1, replicas):
            me.arrived(got.at[k - 1], v.vr_recv.at[index, k - 1])
        total = vec[...]
        for k in range(1, replicas):
            total = total + got[k - 1]
        return total

    def biases_begin():
        ones = jnp.ones((8, group), bf16)
        for start in range(0, width, 256):
            size = min(256, width - start)
            v.v1[:, pl.ds(start, size)] = jnp.dot(ones, v.dproj[:, pl.ds(start, size)], preferred_element_type=f32)[:1]
        to_replicas(v.v1, v.got1, 0)

    def bias_out_begin():
        ones = jnp.ones((8, group), bf16)

        def body(i):
            cols = rows_at(i * 256, 256, 256)
            v.v1[:, rows_at(width + i * 256, 256, 256)] = jnp.dot(ones, v.ct[:, cols], preferred_element_type=f32)[:1]

        loop(D // 256, body)

    def biases_share():
        v.v1s[...] = from_replicas(v.v1, v.got1, 0)
        v.gb_out[...] = v.v1s[:, pl.ds(width, D)]
        give("gb_out")
        for part, (src, dst, size) in enumerate(ranges(s)):
            at = rows_at(src, size, 128)
            me.local(v.v1s.at[:, pl.ds(dst, size)], v.gb_in.at[:, at], v.bias_sem.at[part])
            for k in range(1, n):
                me.send(
                    v.v1s.at[:, pl.ds(dst, size)], v.gb_in.at[:, at],
                    v.vl_recv.at[n - k - 1], (r, (s + k) % n))

    def biases_end():
        for part, (src, _, size) in enumerate(ranges(s)):
            me.arrived(v.gb_in.at[:, rows_at(src, size, 128)], v.bias_sem.at[part])
        for k in range(1, n):
            me.arrived(v.gb_in.at[:, pl.ds(0, width)], v.vl_recv.at[k - 1])

    def norms_begin():
        v.v2s[...] = from_replicas(v.v2, v.got2, 1)
        for k in range(1, n):
            me.send(v.v2s, v.got3.at[n - k - 1], v.vn_recv.at[n - k - 1], (r, (s + k) % n))

    def norms_end():
        for k in range(1, n):
            me.arrived(v.got3.at[k - 1], v.vn_recv.at[k - 1])
        total = v.v2s[...]
        for k in range(1, n):
            total = total + v.got3[k - 1]
        v.g_gain[...] = total[:, :D]
        v.g_bias[...] = total[:, D:]
        give("g_gain")
        give("g_bias")

    def hop(a, e):
        line_hop(a, e, 0)
        line_hop(a, e, 1)

    events = []
    for unit in units:
        events.append((unit.u, "two", unit, lambda unit=unit: step_two(unit)))
        events.append((unit.u + 1.1, "three", unit, lambda unit=unit: step_three(unit)))
    for landing in landings_in + landings_heads:
        u = landing.unit.u
        events.append((u + 3.2, "four", None, landing.spread))
        events.append((u + 5.3, "five", None, landing.forward))
    for i, landing in enumerate(landings_out):
        u = unit_attention.u + 0.9 * i
        events.append((u + 3.4, "four", None, landing.spread))
        events.append((u + 5.5, "five", None, landing.forward))
    events.sort(key=lambda event: event[0])
    started, doubled = set(), set()

    def begin(unit):
        step_one(unit)
        started.add(unit.u)

    def advance(until):
        while events and events[0][0] <= until:
            _, name, unit, act = events[0]
            if name == "two" and unit.u not in started:
                return
            events.pop(0)
            if name == "two":
                doubled.add(unit.u)
            act()

    ua = unit_attention.u
    for unit in units_hidden_out:
        grad_out(unit)
        begin(unit)
    for k, unit in enumerate(units_hidden_in):
        grad_in(unit)
        begin(unit)
        if k % 4 == 3:
            advance(EAGER[0] * (k // 4 + 1))
    for m in range(tall):
        project_heads(m)
        advance(EAGER[1] + EAGER[2] * (m + 1) * 2 / tall)
    tasks = [(b, pair, side) for b in range(sequences) for pair in range(heads // 2) for side in range(2)]
    for i, (b, pair, side) in enumerate(tasks):
        attend(b, pair, side)
        if side == 1:
            settle_pair(b, pair)
        advance(EAGER[3] + EAGER[4] * (i + 1))
    advance(ua - 2)
    drain_unit(units_hidden_out[0])
    grad_out(unit_attention)
    begin(unit_attention)
    bias_out_begin()
    biases_begin()
    mixed_tiles()
    line_begin(0)
    advance(ua - 1)
    assert all(unit.u in doubled for unit in units_hidden_out + units_hidden_in)
    for unit, past in zip(units_heads, units_hidden_in, strict=True):
        drain_unit(past)
        grad_in(unit)
        begin(unit)
    advance(ua - 0.5)
    for m in range(1, L):
        core_sum(0, m)
    hop(0, 0)
    d_normed_tiles()
    line_begin(1)
    biases_share()
    advance(ua)
    for m in range(1, L):
        core_sum(1, m)
    hop(1, 0)
    for e in range(1, L - 1):
        advance(ua + HOP * e - 0.5)
        hop(0, e)
        advance(ua + HOP * e + 0.5 * HOP - 0.5)
        hop(1, e)
    last = ua + HOP * (L - 1) - 0.5
    advance(last)
    finish_mixed()
    advance(last + 1.5)
    finish_normed()
    to_replicas(v.v2, v.got2, 1)
    advance(last + 2.5)
    norms_begin()
    advance(last + 4)
    norms_end()
    biases_end()
    advance(1000)
    for landing in landings:
        landing.finish()
    for unit in units:
        drain_unit(unit)
    for i, name in enumerate(GIVEN):
        me.arrived(getattr(v, name), v.give_sem.at[i])
    me.drain()


def fused(tokens, ln_gain, ln_bias, w_in, b_in, w_out, b_out, cotangent, cosine, sine):
    n, replicas = lax.axis_size("shard"), lax.axis_size("replica")
    X = max(replicas // 2, 1)
    Y = replicas // X
    L = n // 2
    rows = tokens.shape[0]
    group = rows * n
    depth = D // n
    q = depth // replicas
    head, fc = D // n, FF // n
    head3 = 3 * head
    width = head3 + fc
    both_heads = (group // SEQ_LEN) * (head // HEAD_DIM)
    vmem, dma = pltpu.VMEM, pltpu.SemaphoreType.DMA
    t = n - 2
    most = max(X, Y) - 1
    units = 2 * n + SLOTS
    scratch = {
        "nl": vmem((group, D), bf16), "ct": vmem((group, D), bf16),
        "wi": vmem((D, width), bf16), "wo": vmem((SLOTS * depth, D), bf16),
        "joined": vmem((group, head + fc), bf16), "dproj": vmem((group, width), bf16),
        "flip": vmem((depth, group), bf16),
        "oh": vmem((2, SEQ_LEN, HEAD_DIM), f32), "dq": vmem((2, SEQ_LEN, HEAD_DIM), f32),
        "dk": vmem((2, SEQ_LEN, HEAD_DIM), f32), "dv": vmem((2, SEQ_LEN, HEAD_DIM), f32),
        "g_out": vmem((SLOTS - 1, depth, D), bf16), "g_in": vmem((n, depth, fc), bf16),
        "b_own": vmem((1, width), f32),
        "tmp": vmem((L, rows, D), bf16), "acc": vmem((2, 8, D), f32),
        "v1": vmem((1, width + D), f32), "v1s": vmem((1, width + D), f32), "got1": vmem((replicas - 1, 1, width + D), f32),
        "v2": vmem((1, 2 * D), f32), "v2s": vmem((1, 2 * D), f32), "got2": vmem((replicas - 1, 1, 2 * D), f32),
        "got3": vmem((n - 1, 1, 2 * D), f32),
    }
    for name in ("qh", "kh", "vh", "doh"):
        scratch[name] = vmem((both_heads, SEQ_LEN, HEAD_DIM), bf16)
    for tag, count, wide in (("o", SLOTS, D), ("f", n, fc), ("q", n, head3)):
        a, b = half_of(wide), wide - half_of(wide)
        scratch["r1" + tag + "a"] = vmem((count, X - 1, Y * q, a), bf16)
        scratch["r1" + tag + "b"] = vmem((count, Y - 1, X * q, b), bf16)
        scratch["r2" + tag + "a"] = vmem((count, Y - 1, q, a), bf16)
        scratch["r2" + tag + "b"] = vmem((count, X - 1, q, b), bf16)
    sems = {
        "ag_recv": (2, 2, L), "sib_recv": (2, 2 * L), "ws_recv": (1,), "oz_recv": (SLOTS,), "wz_recv": (t, 2),
        "i_come": (t, 4, most), "i_rest": (t, 4), "o_come": (SLOTS, 2, most), "o_rest": (SLOTS, 2),
        "s1_recv": (units, 2, most), "s2_recv": (units, 2, most), "zi_recv": (units,), "zo_recv": (SLOTS,),
        "a_come": (units, 2, most), "a_rest": (units, 2),
        "ls_recv": (2, L), "lz_recv": (2, 2, L), "vr_recv": (2, replicas - 1), "vl_recv": (n - 1,), "vn_recv": (n - 1,),
        "pool": (POOL,),
    }
    scratch |= {name: dma(shape) for name, shape in sems.items()}
    scratch["own_sem"], scratch["tmp_sem"] = dma((5,)), dma((L,))
    any_space = pl.BlockSpec(memory_space=pl.ANY)
    loaded = {
        "tok": tokens, "gain": ln_gain.reshape(1, D), "bias": ln_bias.reshape(1, D), "b_in": b_in.reshape(1, 3 * D + FF),
        "cot": cotangent, "b_out": b_out.reshape(1, D), "cosine": cosine, "sine": sine,
    }
    scratch |= {name: vmem(value.shape, value.dtype) for name, value in loaded.items()}
    scratch |= {"block_out": vmem((rows, D), bf16), "grad_tokens": vmem((rows, D), bf16)}
    scratch |= {name: vmem((1, D), f32) for name in ("gb_out", "g_gain", "g_bias")}
    scratch["load_sem"], scratch["give_sem"] = dma((len(loaded),)), dma((len(GIVEN),))
    scratch["bias_sem"] = dma((4,))
    in_hbm = pl.BlockSpec(memory_space=pltpu.HBM)
    inputs = {"far_" + name: (value, in_hbm) for name, value in loaded.items()} | {
        "w_in": (w_in, in_hbm), "w_out": (w_out, in_hbm),
    }
    shape = jax.ShapeDtypeStruct
    outputs = {
        "fi": (shape((n, depth, width), bf16), any_space), "fo": (shape((SLOTS, depth, D), bf16), any_space),
        "to_block_out": (shape((rows, D), bf16), in_hbm), "to_grad_tokens": (shape((rows, D), bf16), in_hbm),
        "gb_in": (shape((1, 3 * D + FF), f32), in_hbm), "to_gb_out": (shape((1, D), f32), in_hbm),
        "to_g_gain": (shape((1, D), f32), in_hbm), "to_g_bias": (shape((1, D), f32), in_hbm),
        "sbx": (shape((2, L, rows, D), bf16), any_space), "zbx": (shape((2, 2, L, rows, D), bf16), any_space),
    }
    done = pl.pallas_call(
        functools.partial(fused_kernel, n, replicas, list(inputs) + list(outputs) + list(scratch)),
        out_shape=tuple(out for out, _ in outputs.values()),
        in_specs=[spec for _, spec in inputs.values()],
        out_specs=tuple(spec for _, spec in outputs.values()),
        scratch_shapes=list(scratch.values()),
        compiler_params=pltpu.CompilerParams(collective_id=0, has_side_effects=True, vmem_limit_bytes=63 << 20),
        name="fused",
    )(*[value for value, _ in inputs.values()])
    return {name.removeprefix("to_"): value for name, value in zip(outputs, done, strict=True)}


def widen_kernel(n, names, *refs):
    v = Names(names, refs)
    depth = D // n
    head, fc = D // n, FF // n
    jobs = [("out", i) for i in range(SLOTS)] + [("in", d) for d in range(n)]
    passed = [
        (
            pltpu.make_async_copy(getattr(v, name), getattr(v, "by_" + name), v.pass_sem.at[p, 0]),
            pltpu.make_async_copy(getattr(v, "by_" + name), getattr(v, "to_" + name), v.pass_sem.at[p, 1]),
        )
        for p, name in enumerate(PASSED)
    ]

    def load(j):
        kind, i = jobs[j]
        src, dst = (v.fi.at[i], v.low_in.at[i]) if kind == "in" else (v.fo.at[i], v.low_out.at[i])
        return pltpu.make_async_copy(src, dst, v.load_sem.at[j])

    def stores(j):
        kind, i = jobs[j]
        if kind == "out":
            return [pltpu.make_async_copy(v.wide_out.at[i], v.go.at[pl.ds(i * depth, depth)], v.store_sem.at[j, 0])]
        places = [(part * D + head * i, part * head, head) for part in range(3)] + [(3 * D + fc * i, 3 * head, fc)]
        return [
            pltpu.make_async_copy(
                v.wide_in.at[i, :, pl.ds(src, size)], v.gi.at[:, pl.ds(dst, size)], v.store_sem.at[j, p]
            )
            for p, (dst, src, size) in enumerate(places)
        ]

    for j in range(len(jobs)):
        load(j).start()
    for first, _ in passed:
        first.start()
    for j, (kind, i) in enumerate(jobs):
        load(j).wait()
        low, wide = (v.low_in, v.wide_in) if kind == "in" else (v.low_out, v.wide_out)

        def body(k, low=low, wide=wide, i=i):
            at = rows_at(k * 16, 16)
            wide[i, at, :] = low[i, at, :].astype(f32)

        loop(depth // 16, body)
        for copy in stores(j):
            copy.start()
    for first, then in passed:
        first.wait()
        then.start()
    for j in range(len(jobs)):
        for copy in stores(j):
            copy.wait()
    for _, then in passed:
        then.wait()


PASSED = ("block_out", "grad_tokens", "gb_in", "gb_out", "g_gain", "g_bias")


def widen(results):
    n = lax.axis_size("shard")
    fi, fo = results["fi"], results["fo"]
    depth, width = fi.shape[1], fi.shape[2]
    dma, vmem, shape = pltpu.SemaphoreType.DMA, pltpu.VMEM, jax.ShapeDtypeStruct
    in_hbm = pl.BlockSpec(memory_space=pltpu.HBM)
    inputs = {"fi": fi, "fo": fo} | {name: results[name] for name in PASSED}
    outputs = {"gi": shape((depth, 3 * D + FF), f32), "go": shape((SLOTS * depth, D), f32)} | {
        "to_" + name: shape(results[name].shape, results[name].dtype) for name in PASSED
    }
    scratch = {
        "low_in": vmem((n, depth, width), bf16), "low_out": vmem((SLOTS, depth, D), bf16),
        "wide_in": vmem((n, depth, width), f32), "wide_out": vmem((SLOTS, depth, D), f32),
        "load_sem": dma((n + SLOTS,)), "store_sem": dma((n + SLOTS, 4)), "pass_sem": dma((len(PASSED), 2)),
    } | {"by_" + name: vmem(results[name].shape, results[name].dtype) for name in PASSED}
    names = list(inputs) + list(outputs) + list(scratch)
    done = pl.pallas_call(
        functools.partial(widen_kernel, n, names),
        out_shape=tuple(outputs.values()),
        in_specs=[in_hbm] * len(inputs),
        out_specs=(in_hbm,) * len(outputs),
        scratch_shapes=list(scratch.values()),
        compiler_params=pltpu.CompilerParams(vmem_limit_bytes=60 << 20),
        name="widen",
    )(*inputs.values())
    return dict(zip(outputs, done, strict=True))


def angle_tables():
    lane = np.arange(128) % HEAD_DIM
    frequency = 10000.0 ** (-2.0 * (lane % (ROT // 2)) / ROT)
    angle = np.arange(SEQ_LEN)[:, None] * frequency[None, :]
    turned = (lane < ROT)[None, :]
    return np.where(turned, np.cos(angle), 1.0).astype(np.float32), np.where(turned, np.sin(angle), 0.0).astype(np.float32)


def local(tokens, ln_gain, ln_bias, w_in, b_in, w_out, b_out, cotangent):
    cosine, sine = angle_tables()
    results = fused(tokens, ln_gain, ln_bias, w_in, b_in, w_out, b_out, cotangent, jnp.asarray(cosine), jnp.asarray(sine))
    done = widen(results)
    return (
        done["to_block_out"], done["to_grad_tokens"], done["to_g_gain"].reshape(D), done["to_g_bias"].reshape(D),
        done["gi"], done["to_gb_in"].reshape(3 * D + FF), done["go"], done["to_gb_out"].reshape(D),
    )


def solution(mesh):
    both_axes = P(("replica", "shard"), None)
    return jax.shard_map(
        local,
        mesh=mesh,
        in_specs=(both_axes, P(), P(), P("shard", None), P(), P("shard", None), P(), both_axes),
        out_specs=(both_axes, both_axes, P(), P(), P("shard", None), P(), P("shard", None), P()),
        check_vma=False,
    )
```

```python
import functools
import jax
import jax.numpy as jnp
import numpy as np
from jax import lax
from jax.experimental import pallas as pl
from jax.experimental.pallas import tpu as pltpu
from jax.sharding import PartitionSpec as P

D = 2048
HEADS = 32
HEAD_DIM = 64
ROT = 32
FF = 8192
SEQ_LEN = 1024
SLOTS = 5

epsilon = 1e-05
masked_score = -1e30
MESH = pl.DeviceIdType.MESH
f32 = jnp.float32
bf16 = jnp.bfloat16


class Place:
    def __init__(self, n, replicas):
        self.n, self.R = n, replicas
        self.X = max(replicas // 2, 1)
        self.Y = replicas // self.X
        self.L = n // 2
        self.r, self.s = lax.axis_index("replica"), lax.axis_index("shard")
        self.x, self.y = self.r % self.X, self.r // self.X
        self.z, self.c = self.s // 2, self.s % 2
        self.sibling = (self.r, self.s + 1 - 2 * self.c)
        self.pool, self.used, self.turn = None, {}, 0

    def x_peer(self, dx):
        return self.y * self.X + (self.x + dx) % self.X

    def y_peer(self, dy):
        return ((self.y + dy) % self.Y) * self.X + self.x

    def send(self, src, dst, recv_sem, device, when=None):
        turn = self.turn % self.pool.shape[0]
        self.turn += 1
        self.sent(turn)
        copy = pltpu.make_async_remote_copy(
            src_ref=src, dst_ref=dst, send_sem=self.pool.at[turn], recv_sem=recv_sem,
            device_id=device, device_id_type=MESH,
        )
        guarded(when, copy.start)
        self.used[turn] = (when, copy.wait_send)
        return turn, copy

    def sent(self, turn, copy=None):
        if turn in self.used and (copy is None or self.used[turn][1].__self__ is copy):
            when, wait = self.used.pop(turn)
            guarded(when, wait)

    def local(self, src, dst, sem, when=None):
        guarded(when, pltpu.make_async_copy(src, dst, sem).start)

    def arrived(self, ref, sem, when=None):
        guarded(when, pltpu.make_async_copy(ref, ref, sem).wait)

    def mark(self):
        return [(turn, wait.__self__) for turn, (_, wait) in sorted(self.used.items())]

    def drain(self):
        for turn in sorted(self.used):
            self.sent(turn)

    def meet(self, line=True, square=True, whole=False):
        barrier = pltpu.get_barrier_semaphore()
        peers = []
        if line:
            peers += [(self.r, (self.s + k) % self.n) for k in range(1, self.n)]
        if whole:
            peers += [((self.r + k) % self.R, self.s) for k in range(1, self.R)]
        elif square:
            peers += [(self.x_peer(dx), self.s) for dx in range(1, self.X)]
            peers += [(self.y_peer(dy), self.s) for dy in range(1, self.Y)]
        for peer in peers:
            pl.semaphore_signal(barrier, inc=1, device_id=peer, device_id_type=MESH)
        pl.semaphore_wait(barrier, len(peers))


def guarded(when, act):
    if when is None:
        act()
    else:
        pl.when(when)(act)


def both(a, b):
    return b if a is None else a if b is None else jnp.logical_and(a, b)


def rows_at(start, size, multiple=16):
    return pl.ds(pl.multiple_of(start, multiple), size)


def half_of(width):
    return -(-width // 256) * 128


def slot_of(block, n):
    past = jnp.maximum(block - n, 0)
    first = block < n
    return jnp.where(first, block, past // 4), jnp.where(first, 0, 1 + past % 4)


def block_of(device, slot, n):
    return device if slot == 0 else n + 4 * device + slot - 1


UP = 0.7978845608028654
NT = (((1,), (1,)), ((), ()))
TALL = 512
PACE = (-13,-11,-9,-7,-4,-0.75,-1,-0.5,-0.4)
HOP = 2.5


POOL = 96
LOADED = ("tok", "gain", "bias", "b_in", "cot", "b_out", "cosine", "sine")
GIVEN = ("block_out", "grad_tokens", "gb_out", "g_gain", "g_bias")


class Names:
    def __init__(self, names, refs):
        for name, ref in zip(names, refs, strict=True):
            setattr(self, name, ref)


class Unit:
    def __init__(self, kind, k, buf, width, col0, one, two):
        self.kind, self.k, self.buf, self.width, self.col0 = kind, k, buf, width, col0
        cut = half_of(width)
        self.halves = ((0, cut), (cut, width - cut))
        self.one, self.two = one, two
        self.sent = []


def loop(count, body):
    def step(i, carry):
        body(i)
        return carry

    lax.fori_loop(0, count, step, 0)


def add_rows(store, loads, rows, strip=16):
    def step(i):
        at = rows_at(i * strip, strip)
        total = loads[0](at).astype(f32)
        for load in loads[1:]:
            total = total + load(at).astype(f32)
        store(at, total)

    loop(rows // strip, step)


def shifted(start, at):
    return pl.ds(pl.multiple_of(start + at.start, 16), at.size)


def fused_kernel(n, replicas, names, *refs):
    v = Names(names, refs)
    me = Place(n, replicas)
    me.pool = v.pool
    X, Y, L, r, s, z, c = me.X, me.Y, me.L, me.r, me.s, me.z, me.c
    rows = v.tok.shape[0]
    group = rows * n

    def loaded(*picked):
        for name in picked:
            me.arrived(getattr(v, name), v.load_sem.at[LOADED.index(name)])

    def give(name):
        me.local(getattr(v, name), getattr(v, "to_" + name), v.give_sem.at[GIVEN.index(name)])

    for i, name in enumerate(LOADED):
        me.local(getattr(v, "far_" + name), getattr(v, name), v.load_sem.at[i])
    depth = D // n
    q = depth // replicas
    head, fc = D // n, FF // n
    heads = head // HEAD_DIM
    sequences = group // SEQ_LEN
    head3 = 3 * head
    width = head3 + fc
    tall = group // TALL
    me.meet(whole=True)

    def chunk(ref, owner):
        return ref.at[rows_at(owner * rows, rows)]

    def ranges(device):
        return [(part * D + head * device, part * head, head) for part in range(3)] + [
            (3 * D + fc * device, head3, fc)
        ]

    order = list(range(L // 2, L)) + list(range(1, L // 2))

    def far(t):
        chip, m, bit = 0, order[t // 2], 1
        while bit < L:
            chip = chip + ((z // bit + m // bit) % 2) * bit
            bit *= 2
        return 2 * chip + t % 2

    pairs = (v.nl, v.ct)
    has_left, has_right = z > 0, z < L - 1
    left, right = (r, jnp.maximum(s - 2, 0)), (r, jnp.minimum(s + 2, n - 1))

    def spread_own(a, own):
        every = pairs[a]
        me.send(own, chunk(every, s), v.ag_recv.at[a, 0, 1], right, has_right)
        me.send(own, chunk(every, s), v.ag_recv.at[a, 1, 1], left, has_left)
        me.send(own, chunk(every, s), v.sib_recv.at[a, 0], me.sibling)

    me.local(v.far_cot, chunk(v.ct, s), v.own_sem.at[0])

    def send_far(t, which):
        device = far(t)
        back = 2 * (t // 2) + c
        for part, (src, dst, size) in enumerate(ranges(device)):
            if (part == 3) == (which == "fc"):
                me.send(
                    v.w_in.at[rows_at(r * q, q), rows_at(src, size, 128)],
                    v.wi.at[rows_at(s * depth + r * q, q), pl.ds(dst, size)], v.wz_recv.at[back, part // 3], (r, device))

    for t in range(n - 2):
        send_far(t, "fc")

    for i in range(SLOTS):
        device, slot = slot_of(SLOTS * s + i, n)
        mine = device == s
        near = jnp.logical_and(device // 2 == z, device != s)
        away = device // 2 != z
        full = v.wo.at[rows_at(slot * depth, depth)]
        me.local(v.w_out.at[pl.ds(i * depth, depth)], full, v.oz_recv.at[slot], mine)
        me.send(v.w_out.at[pl.ds(i * depth, depth)], full, v.oz_recv.at[slot], me.sibling, near)
        target = jnp.where(away, device, (s + 2) % n)
        me.send(
            v.w_out.at[rows_at(i * depth + r * q, q)], v.wo.at[rows_at(slot * depth + r * q, q)], v.oz_recv.at[slot], (r, target), away)
    for t in range(n - 2):
        send_far(t, "qkv")
    def normalise(at):
        wide = v.tok[at, :].astype(f32)
        centred = wide - jnp.mean(wide, axis=-1, keepdims=True)
        rstd = lax.rsqrt(jnp.mean(centred * centred, axis=-1, keepdims=True) + epsilon)
        return centred * rstd, rstd

    def norm_strip(i):
        at = rows_at(i * 16, 16)
        normed, _ = normalise(at)
        v.nl[rows_at(s * rows + i * 16, 16), :] = (normed * v.gain[...] + v.bias[...]).astype(bf16)

    loaded("tok", "gain", "bias", "b_in")
    loop(rows // 16, norm_strip)
    for src, dst, size in ranges(s):
        v.b_own[:, pl.ds(dst, size)] = v.b_in[:, rows_at(src, size, 128)]

    for part, (src, dst, size) in enumerate(ranges(s)):
        me.local(
            v.w_in.at[:, rows_at(src, size, 128)], v.wi.at[rows_at(s * depth, depth), pl.ds(dst, size)],
            v.own_sem.at[1 + part],
        )
    for part, (src, dst, size) in enumerate(ranges(me.sibling[1])):
        me.send(
            v.w_in.at[:, rows_at(src, size, 128)], v.wi.at[rows_at(s * depth, depth), pl.ds(dst, size)], v.ws_recv.at[0], me.sibling)

    def share(ref_of, halves, index, tag, when=None):
        come, rest = getattr(v, tag + "_come"), getattr(v, tag + "_rest")

        def direct(picked):
            for h in picked:
                ref = ref_of(r, *halves[h])
                for dx in range(1, X):
                    sem = come.at[index, h, X - dx - 1] if h % 2 == 0 else rest.at[index, h]
                    me.send(ref, ref, sem, (me.x_peer(dx), s), when)
                for dy in range(1, Y):
                    sem = rest.at[index, h] if h % 2 == 0 else come.at[index, h, Y - dy - 1]
                    me.send(ref, ref, sem, (me.y_peer(dy), s), when)

        def forward(picked):
            for h in picked:
                for d in range(1, X if h % 2 == 0 else Y):
                    ref = ref_of(me.x_peer(d) if h % 2 == 0 else me.y_peer(d), *halves[h])
                    me.arrived(ref, come.at[index, h, d - 1], when)
                    for e in range(1, Y if h % 2 == 0 else X):
                        peer = me.y_peer(e) if h % 2 == 0 else me.x_peer(e)
                        me.send(ref, ref, rest.at[index, h], (peer, s), when)

        def finish(picked):
            for h in picked:
                count = X * (Y - 1) if h % 2 == 0 else Y * (X - 1)
                me.arrived(ref_of(0, *halves[h], count), rest.at[index, h], when)

        return direct, forward, finish

    fc_half, qkv_half = half_of(fc), half_of(head3)
    halves_in = (
        (head3, fc_half), (head3 + fc_half, fc - fc_half), (0, qkv_half), (qkv_half, head3 - qkv_half),
    )

    def in_piece(t):
        def ref_of(replica, start, size, count=1):
            return v.wi.at[rows_at(far(t) * depth + replica * q, count * q), pl.ds(start, size)]

        return share(ref_of, halves_in, t, "i")

    def in_arrived(t, part):
        base = rows_at(far(t) * depth + r * q, q)
        if part == "fc":
            me.arrived(v.wi.at[base, pl.ds(head3, fc)], v.wz_recv.at[t, 1])
        else:
            me.arrived(v.wi.at[base, pl.ds(0, head3)], v.wz_recv.at[t, 0])

    out_half = half_of(D)
    halves_out = ((0, out_half), (out_half, D - out_half))

    def out_piece(j):
        source = block_of(s, j, n) // SLOTS

        def ref_of(replica, start, size, count=1):
            return v.wo.at[rows_at(j * depth + replica * q, count * q), pl.ds(start, size)]

        return share(ref_of, halves_out, j, "o", source // 2 != z)

    def out_arrived(j):
        source = block_of(s, j, n) // SLOTS
        me.arrived(v.wo.at[rows_at(j * depth + r * q, q)], v.oz_recv.at[j], source // 2 != z)
        me.arrived(v.wo.at[pl.ds(j * depth, depth)], v.oz_recv.at[j], source // 2 == z)

    def pass_on(k, a):
        every = pairs[a]
        for side, (source, there, onward) in enumerate(((s - 2 * k, right, has_right), (s + 2 * k, left, has_left))):
            known = (z - k >= 0) if side == 0 else (z + k < L)
            ref = chunk(every, jnp.clip(source, 0, n - 1))
            me.arrived(ref, v.ag_recv.at[a, side, k], known)
            if k < L - 1:
                me.send(ref, ref, v.ag_recv.at[a, side, k + 1], there, both(known, onward))
            me.send(
                ref, ref, v.sib_recv.at[a, 2 * k - 1 + side], me.sibling, known
            )

    def hidden_rows(chip, when=None, tiles=None):
        at = rows_at(jnp.clip(chip, 0, L - 1) * (2 * rows), 2 * rows)

        def body(j):
            cols = rows_at(head3 + depth * j, depth, 128)
            x = jnp.dot(v.nl[at, :], v.wi[:, cols], preferred_element_type=f32) + v.b_own[:, cols]
            square = x * x
            t = jnp.tanh(UP * (x + 0.044715 * (square * x)))
            v.joined[at, rows_at(head + depth * j, depth, 128)] = (0.5 * x * (1.0 + t)).astype(bf16)
            slope = 0.5 * (1.0 + t) + 0.5 * x * (1.0 - t * t) * (UP * (1.0 + (3 * 0.044715) * square))
            d_hidden = lax.dot_general(
                v.ct[at, :], v.wo[rows_at(depth + depth * j, depth, 128), :], NT, preferred_element_type=f32
            )
            v.dproj[at, cols] = (d_hidden * slope).astype(bf16)

        def work():
            if tiles is None:
                loop(fc // depth, body)
            else:
                body(tiles)

        guarded(when, work)

    ins = [in_piece(t) for t in range(n - 2)]
    outs = [out_piece(j) for j in range(SLOTS)]
    fc_h, qkv_h = (0, 1), (2, 3)
    def lanes_turn(x, at, sign):
        lane = lax.broadcasted_iota(jnp.int32, x.shape, 1) % HEAD_DIM
        sine = v.sine[at, :] * sign
        swapped = jnp.where(lane < ROT // 2, -pltpu.roll(x, 128 - ROT // 2, 1), pltpu.roll(x, ROT // 2, 1))
        return x * v.cosine[at, :] + swapped * sine

    def project_rows(chip, when=None):
        chip = jnp.clip(chip, 0, L - 1)
        tall = 2 * rows
        at = rows_at(chip * tall, tall)
        inside = rows_at(chip % (SEQ_LEN // tall) * tall, tall)
        base = chip // (SEQ_LEN // tall) * heads

        def part_of(part):
            if part == 3:
                return lax.dot_general(v.ct[at, :], v.wo[:depth, :], NT, preferred_element_type=f32)
            cols = pl.ds(head * part, head)
            return jnp.dot(v.nl[at, :], v.wi[:, cols], preferred_element_type=f32) + v.b_own[:, cols]

        def work():
            for part, to in enumerate((v.qh, v.kh, v.vh, v.doh)):
                wide = part_of(part)
                for slab in range(head // 128):
                    x = wide[:, 128 * slab : 128 * (slab + 1)]
                    if part < 2:
                        x = lanes_turn(x, inside, 1.0)
                    x = x.astype(bf16)
                    to[base + 2 * slab, inside, :] = x[:, :HEAD_DIM]
                    to[base + 2 * slab + 1, inside, :] = x[:, HEAD_DIM:]

        guarded(when, work)

    arrivals, steps = [], []
    for t in range(n - 2):
        arrivals.append((lambda t=t: (in_arrived(t, "fc"), ins[t][0](fc_h)), lambda t=t: ins[t][1](fc_h)))
    for j in range(SLOTS):
        arrivals.append((lambda j=j: (out_arrived(j), outs[j][0](fc_h)), lambda j=j: outs[j][1](fc_h)))
    for t in range(n - 2):
        arrivals.append((lambda t=t: (in_arrived(t, "qkv"), ins[t][0](qkv_h)), lambda t=t: ins[t][1](qkv_h)))
    for i, (first, then) in enumerate(arrivals):
        steps.append((i, first))
        steps.append((i + 2.5, then))
    steps.append((8.2, lambda: (loaded("cot", "b_out", "cosine", "sine"), spread_own(1, v.cot), spread_own(0, chunk(v.nl, s)))))
    for k in range(1, L - 1):
        steps.append((8.1 + 4 * k, lambda k=k: pass_on(k, 1)))
        steps.append((8.2 + 4 * k, lambda k=k: pass_on(k, 0)))
    for _, step in sorted(steps, key=lambda pair: pair[0]):
        step()
    other = me.sibling[1]

    def rows_there(k):
        for every in (v.nl, v.ct):
            a = 0 if every is v.nl else 1
            if k == 0:
                me.arrived(chunk(every, other), v.sib_recv.at[a, 0])
                continue
            for side in range(2):
                source = other - 2 * k if side == 0 else other + 2 * k
                known = (z - k >= 0) if side == 0 else (z + k < L)
                me.arrived(chunk(every, jnp.clip(source, 0, n - 1)), v.sib_recv.at[a, 2 * k - 1 + side], known)

    me.arrived(chunk(v.ct, s), v.own_sem.at[0])
    for piece in ins:
        piece[2](fc_h)
    for piece in outs:
        piece[2](fc_h)
    for part, (_, dst, size) in enumerate(ranges(s)):
        me.arrived(v.wi.at[rows_at(s * depth, depth), pl.ds(dst, size)], v.own_sem.at[1 + part])
    me.arrived(v.wi.at[rows_at(other * depth, depth), :], v.ws_recv.at[0])
    for k in range(L - 1):
        rows_there(k)
        if k == 0:
            hidden_rows(z)
        else:
            hidden_rows(z - k, z - k >= 0)
            hidden_rows(z + k, z + k < L)
    for piece in ins:
        piece[2](qkv_h)
    for k in range(L - 1):
        project_rows(z - k, z - k >= 0 if k else None)
        if k:
            project_rows(z + k, z + k < L)

    def last_rows():
        pass_on(L - 1, 1)
        pass_on(L - 1, 0)
        rows_there(L - 1)
        for j, unit in enumerate(units_hidden_out):
            hidden_rows(0, z == L - 1, j)
            hidden_rows(L - 1, z == 0, j)
            grad_out(unit)
            begin(unit)

    def tile(i, size=TALL):
        return rows_at(i * size, size)

    def turned_columns(ref, start, size):
        def body(m):
            v.flip[:size, rows_at(m * 256, 256, 256)] = jnp.transpose(ref[tile(m, 256), pl.ds(start, size)])

        loop(group // 256, body)

    def turned_rows(start):
        def body(m):
            v.flip[:depth, rows_at(m * 256, 256, 256)] = jnp.transpose(v.nl[tile(m, 256), rows_at(start, depth, 128)])

        loop(group // 256, body)

    def grad_out(unit):
        turned_columns(v.joined, depth * unit.k, depth)

        def body(m):
            cols = rows_at(m * 512, 512, 512)
            unit.buf[:, cols] = jnp.dot(v.flip[:depth, :], v.ct[:, cols], preferred_element_type=f32).astype(bf16)

        loop(D // 512, body)

    def grad_in(unit):
        turned_rows(((s + unit.k) % n) * depth)
        for start in range(0, unit.width, 256):
            size = min(256, unit.width - start)
            unit.buf[:, pl.ds(start, size)] = jnp.dot(
                v.flip[:depth, :], v.dproj[:, pl.ds(unit.col0 + start, size)], preferred_element_type=f32
            ).astype(bf16)

    scale = HEAD_DIM ** (-0.5)
    block = 256

    def attend(b, pair, side):
        hb = b * heads + 2 * pair + side
        key_turned = jnp.transpose(v.kh[hb])
        value_turned = jnp.transpose(v.vh[hb])
        v.dk[side] = jnp.zeros((SEQ_LEN, HEAD_DIM), f32)
        v.dv[side] = jnp.zeros((SEQ_LEN, HEAD_DIM), f32)
        for i in range(SEQ_LEN // block):
            at, past = pl.ds(i * block, block), (i + 1) * block
            query, d_out = v.qh[hb, at, :], v.doh[hb, at, :]
            scores = lax.dot_general(v.kh[hb, :past, :], query, NT, preferred_element_type=f32) * scale
            key_place = lax.broadcasted_iota(jnp.int32, (past, block), 0)
            query_place = lax.broadcasted_iota(jnp.int32, (past, block), 1) + i * block
            scores = jnp.where(key_place <= query_place, scores, masked_score)
            raised = jnp.exp(scores - jnp.max(scores, axis=0, keepdims=True))
            chances = raised * (1.0 / jnp.sum(raised, axis=0, keepdims=True))
            low = chances.astype(bf16)
            out_turned = jnp.dot(value_turned[:, :past], low, preferred_element_type=f32)
            d_out_turned = jnp.transpose(d_out.astype(f32))
            delta = jnp.sum(d_out_turned * out_turned, axis=0, keepdims=True)
            d_chances = lax.dot_general(v.vh[hb, :past, :], d_out, NT, preferred_element_type=f32)
            d_scores = (chances * (d_chances - delta)).astype(bf16)
            v.oh[side, at, :] = jnp.transpose(out_turned)
            d_query_turned = jnp.dot(key_turned[:, :past], d_scores, preferred_element_type=f32) * scale
            v.dq[side, at, :] = jnp.transpose(d_query_turned)
            v.dk[side, :past, :] += jnp.dot(d_scores, query, preferred_element_type=f32) * scale
            v.dv[side, :past, :] += jnp.dot(low, d_out, preferred_element_type=f32)

    def settle_pair(b, pair):
        def settle(m):
            at = tile(m, 256)
            put = rows_at(b * SEQ_LEN + m * 256, 256)

            def slab(ref):
                return jnp.concatenate([ref[0, at, :], ref[1, at, :]], axis=1)

            v.joined[put, pl.ds(128 * pair, 128)] = slab(v.oh).astype(bf16)
            v.dproj[put, pl.ds(128 * pair, 128)] = lanes_turn(slab(v.dq), at, -1.0).astype(bf16)
            v.dproj[put, pl.ds(head + 128 * pair, 128)] = lanes_turn(slab(v.dk), at, -1.0).astype(bf16)
            v.dproj[put, pl.ds(2 * head + 128 * pair, 128)] = slab(v.dv).astype(bf16)

        loop(SEQ_LEN // 256, settle)

    def mixed_tiles():
        def body(i):
            m, cols = i % tall, rows_at((i // tall) * 256, 256, 256)
            v.ct[tile(m), cols] = jnp.dot(v.joined[tile(m), :], v.wo[:, cols], preferred_element_type=f32).astype(bf16)

        loop(tall * (D // 256), body)

    def d_normed_tiles():
        def body(i):
            m, at = i % tall, (i // tall) * 256
            v.nl[tile(m), rows_at(at, 256, 256)] = lax.dot_general(
                v.dproj[tile(m), :], v.wi[rows_at(at, 256, 256), :], NT, preferred_element_type=f32
            ).astype(bf16)

        loop(tall * (D // 256), body)

    def quarter(half, replica):
        x, y = replica % X, replica // X
        return x * Y + y if half == 0 else y * X + x

    units_hidden_out = [
        Unit("out", j, v.g_out.at[j - 1], D, 0, (v.r1oa, v.r1ob), (v.r2oa, v.r2ob)) for j in range(1, SLOTS)
    ]
    units_hidden_in = [
        Unit("in", k, v.g_in.at[k], fc, head3, (v.r1fa, v.r1fb), (v.r2fa, v.r2fb)) for k in range(n)
    ]
    unit_attention = Unit("out", 0, v.g_out.at[0], D, 0, (v.r1oa, v.r1ob), (v.r2oa, v.r2ob))
    units_heads = [
        Unit("in", k, v.g_in.at[k, :, pl.ds(0, head3)], head3, 0, (v.r1qa, v.r1qb), (v.r2qa, v.r2qb))
        for k in range(n)
    ]
    units = units_hidden_out + units_hidden_in + [unit_attention] + units_heads
    for u, unit in enumerate(units):
        unit.u = u

    def step_one(unit):
        unit.sent = []
        for half, (start, size) in enumerate(unit.halves):
            run = (Y if half == 0 else X) * q
            span = X if half == 0 else Y
            for d in range(1, span):
                peer = me.x_peer(d) if half == 0 else me.y_peer(d)
                place = (me.x + d) % X if half == 0 else (me.y + d) % Y
                unit.sent.append(me.send(
                    unit.buf.at[rows_at(place * run, run), pl.ds(start, size)],
                    unit.one[half].at[unit.k, span - d - 1], v.s1_recv.at[unit.u, half, span - d - 1], (peer, s)))

    def drain_unit(unit):
        for turn, copy in unit.sent:
            me.sent(turn, copy)

    def step_two(unit):
        for half, (start, size) in enumerate(unit.halves):
            run = (Y if half == 0 else X) * q
            span = X if half == 0 else Y
            place = me.x if half == 0 else me.y
            got, k = unit.one[half], unit.k
            for d in range(1, span):
                me.arrived(got.at[k, d - 1], v.s1_recv.at[unit.u, half, d - 1])

            def own(at):
                return unit.buf[shifted(place * run, at), pl.ds(start, size)]

            def store(at, total):
                got[k, 0, at, :] = total.astype(bf16)

            add_rows(store, [own] + [lambda at, d=d: got[k, d - 1, at, :] for d in range(1, span)], run)
            span2 = Y if half == 0 else X
            for d in range(1, span2):
                peer = me.y_peer(d) if half == 0 else me.x_peer(d)
                place2 = (me.y + d) % Y if half == 0 else (me.x + d) % X
                me.send(
                    got.at[k, 0, rows_at(place2 * q, q)], unit.two[half].at[k, span2 - d - 1], v.s2_recv.at[unit.u, half, span2 - d - 1], (peer, s))

    def arrive_sems(unit):
        return unit.u

    def step_three(unit):
        for half, (start, size) in enumerate(unit.halves):
            span2 = Y if half == 0 else X
            place2 = me.y if half == 0 else me.x
            kept, got, k = unit.one[half], unit.two[half], unit.k
            for d in range(1, span2):
                me.arrived(got.at[k, d - 1], v.s2_recv.at[unit.u, half, d - 1])

            def own(at):
                return kept[k, 0, shifted(place2 * q, at), :]

            def store(at, total):
                got[k, 0, at, :] = total.astype(bf16)

            add_rows(store, [own] + [lambda at, d=d: got[k, d - 1, at, :] for d in range(1, span2)], q)
            at = rows_at(quarter(half, r) * q, q)
            cols = pl.ds(unit.col0 + start, size)
            if unit.kind == "in":
                dst = v.fi.at[s, at, cols]
                if k == 0:
                    me.local(got.at[k, 0], dst, v.zi_recv.at[unit.u])
                else:
                    me.send(
                        got.at[k, 0], dst, v.zi_recv.at[unit.u], (r, (s + k) % n)
                    )
            else:
                natural = block_of(s, k, n)
                device, i = natural // SLOTS, natural % SLOTS
                dst = v.fo.at[i, at, cols]
                me.local(got.at[k, 0], dst, v.zo_recv.at[i], device == s)
                target = jnp.where(device == s, (s + 1) % n, device)
                me.send(got.at[k, 0], dst, v.zo_recv.at[i], (r, target), device != s)

    class Landing:
        def __init__(self, kind, k, index, unit):
            self.kind, self.k, self.index, self.unit = kind, k, index, unit

        def ref(self, half, replica):
            at = rows_at(quarter(half, replica) * q, q)
            start, size = self.unit.halves[half]
            cols = pl.ds(self.unit.col0 + start, size)
            if self.kind == "in":
                return v.fi.at[(s - self.k) % n, at, cols]
            return v.fo.at[self.k, at, cols]

        def rows(self, half, count):
            start, size = self.unit.halves[half] if half is not None else (0, self.unit.width)
            cols = pl.ds(self.unit.col0 + start, size)
            if self.kind == "in":
                return v.fi.at[(s - self.k) % n, pl.ds(0, count * q), cols]
            return v.fo.at[self.k, pl.ds(0, count * q), cols]

        def spread(self):
            u = self.index
            me.arrived(self.rows(None, 1), v.zi_recv.at[self.unit.u] if self.kind == "in" else v.zo_recv.at[self.k])
            for half in range(2):
                ref = self.ref(half, r)
                for d in range(1, X):
                    sem = v.a_come.at[u, 0, X - d - 1] if half == 0 else v.a_rest.at[u, 1]
                    me.send(ref, ref, sem, (me.x_peer(d), s))
                for d in range(1, Y):
                    sem = v.a_rest.at[u, 0] if half == 0 else v.a_come.at[u, 1, Y - d - 1]
                    me.send(ref, ref, sem, (me.y_peer(d), s))

        def forward(self):
            u = self.index
            for half in range(2):
                for d in range(1, X if half == 0 else Y):
                    ref = self.ref(half, me.x_peer(d) if half == 0 else me.y_peer(d))
                    me.arrived(ref, v.a_come.at[u, half, d - 1])
                    for e in range(1, Y if half == 0 else X):
                        peer = me.y_peer(e) if half == 0 else me.x_peer(e)
                        me.send(ref, ref, v.a_rest.at[u, half], (peer, s))

        def finish(self):
            for half in range(2):
                count = X * (Y - 1) if half == 0 else Y * (X - 1)
                me.arrived(self.rows(half, count), v.a_rest.at[self.index, half])

    landings_in = [Landing("in", k, k, unit) for k, unit in enumerate(units_hidden_in)]
    landings_out = [Landing("out", i, n + i, unit_attention) for i in range(SLOTS)]
    landings_heads = [Landing("in", unit.k, n + SLOTS + unit.k, unit) for unit in units_heads]
    landings = landings_in + landings_out + landings_heads

    line_parts = (v.ct, v.nl)

    def line_begin(a):
        part = line_parts[a]
        for line in range(L):
            me.send(
                chunk(part, 2 * line + 1 - c), v.sbx.at[a, line], v.ls_recv.at[a, line], me.sibling
            )

    def fetch(src, slot):
        copy = pltpu.make_async_copy(src, v.tmp.at[slot], v.tmp_sem.at[slot])
        copy.start()
        return copy

    def core_sum(a, m):
        part = line_parts[a]
        line = (z + m) % L
        me.arrived(v.sbx.at[a, line], v.ls_recv.at[a, line])
        fetch(v.sbx.at[a, line], m).wait()
        start = (2 * line + c) * rows

        def store(at, total):
            part[shifted(start, at), :] = total.astype(bf16)

        add_rows(store, [lambda at: part[shifted(start, at), :], lambda at: v.tmp[m, at, :]], rows)

    def line_hop(a, e, side):
        part = line_parts[a]
        if side == 0:
            line, inner, nearer = e - (L - 1 - z), has_right, left
            due = jnp.logical_and(line >= 0, line < z)
        else:
            line, inner, nearer = L - 1 - e + z, has_left, right
            due = jnp.logical_and(line > z, line < L)
        line = jnp.clip(line, 0, L - 1)
        start = (2 * line + c) * rows

        @pl.when(both(due, inner))
        def _():
            me.arrived(v.zbx.at[a, side, line], v.lz_recv.at[a, side, line])
            fetch(v.zbx.at[a, side, line], 0).wait()

            def store(at, total):
                part[shifted(start, at), :] = total.astype(bf16)

            add_rows(store, [lambda at: part[shifted(start, at), :], lambda at: v.tmp[0, at, :]], rows)

        me.send(
            part.at[rows_at(start, rows)], v.zbx.at[a, side, line],
            v.lz_recv.at[a, side, line], nearer, due)

    def line_sum(a):
        part = line_parts[a]
        me.arrived(v.sbx.at[a, z], v.ls_recv.at[a, z])
        fetch(v.sbx.at[a, z], 0).wait()
        for side, known in enumerate((has_right, has_left)):
            me.arrived(v.zbx.at[a, side, z], v.lz_recv.at[a, side, z], known)

            @pl.when(known)
            def _():
                fetch(v.zbx.at[a, side, z], 1 + side).wait()

            @pl.when(jnp.logical_not(known))
            def _():
                v.tmp[1 + side] = jnp.zeros((rows, D), bf16)

        def strip(at):
            total = part[shifted(s * rows, at), :].astype(f32)
            for m in range(3):
                total = total + v.tmp[m, at, :].astype(f32)
            return total

        return strip

    def finish_mixed():
        strip = line_sum(0)

        def body(i):
            at = rows_at(i * 16, 16)
            v.block_out[at, :] = (v.tok[at, :].astype(f32) + strip(at) + v.b_out[...]).astype(bf16)

        loop(rows // 16, body)
        give("block_out")

    def finish_normed():
        strip = line_sum(1)
        v.acc[...] = jnp.zeros(v.acc.shape, f32)

        def body(i):
            at = rows_at(i * 16, 16)
            d_normed = strip(at)
            normed, rstd = normalise(at)
            e = d_normed * v.gain[...]
            back = rstd * (
                e - jnp.mean(e, axis=-1, keepdims=True) - normed * jnp.mean(e * normed, axis=-1, keepdims=True)
            )
            v.grad_tokens[at, :] = (v.cot[at, :].astype(f32) + back).astype(bf16)
            product = d_normed * normed
            v.acc[0] += product[:8] + product[8:]
            v.acc[1] += d_normed[:8] + d_normed[8:]

        loop(rows // 16, body)
        give("grad_tokens")
        v.v2[:, pl.ds(0, D)] = jnp.sum(v.acc[0], axis=0, keepdims=True)
        v.v2[:, pl.ds(D, D)] = jnp.sum(v.acc[1], axis=0, keepdims=True)

    def to_replicas(vec, got, index):
        for k in range(1, replicas):
            me.send(
                vec, got.at[replicas - k - 1], v.vr_recv.at[index, replicas - k - 1],
                ((r + k) % replicas, s))

    def from_replicas(vec, got, index):
        for k in range(1, replicas):
            me.arrived(got.at[k - 1], v.vr_recv.at[index, k - 1])
        total = vec[...]
        for k in range(1, replicas):
            total = total + got[k - 1]
        return total

    def biases_begin():
        ones = jnp.ones((8, group), bf16)
        for start in range(0, width, 256):
            size = min(256, width - start)
            v.v1[:, pl.ds(start, size)] = jnp.dot(ones, v.dproj[:, pl.ds(start, size)], preferred_element_type=f32)[:1]
        to_replicas(v.v1, v.got1, 0)

    def bias_out_begin():
        ones = jnp.ones((8, group), bf16)

        def body(i):
            cols = rows_at(i * 256, 256, 256)
            v.v1[:, rows_at(width + i * 256, 256, 256)] = jnp.dot(ones, v.ct[:, cols], preferred_element_type=f32)[:1]

        loop(D // 256, body)

    def biases_share():
        v.v1s[...] = from_replicas(v.v1, v.got1, 0)
        v.gb_out[...] = v.v1s[:, pl.ds(width, D)]
        give("gb_out")
        for part, (src, dst, size) in enumerate(ranges(s)):
            at = rows_at(src, size, 128)
            me.local(v.v1s.at[:, pl.ds(dst, size)], v.gb_in.at[:, at], v.bias_sem.at[part])
            for k in range(1, n):
                me.send(
                    v.v1s.at[:, pl.ds(dst, size)], v.gb_in.at[:, at],
                    v.vl_recv.at[n - k - 1], (r, (s + k) % n))

    def biases_end():
        for part, (src, _, size) in enumerate(ranges(s)):
            me.arrived(v.gb_in.at[:, rows_at(src, size, 128)], v.bias_sem.at[part])
        for k in range(1, n):
            me.arrived(v.gb_in.at[:, pl.ds(0, width)], v.vl_recv.at[k - 1])

    def norms_begin():
        v.v2s[...] = from_replicas(v.v2, v.got2, 1)
        for k in range(1, n):
            me.send(v.v2s, v.got3.at[n - k - 1], v.vn_recv.at[n - k - 1], (r, (s + k) % n))

    def norms_end():
        for k in range(1, n):
            me.arrived(v.got3.at[k - 1], v.vn_recv.at[k - 1])
        total = v.v2s[...]
        for k in range(1, n):
            total = total + v.got3[k - 1]
        v.g_gain[...] = total[:, :D]
        v.g_bias[...] = total[:, D:]
        give("g_gain")
        give("g_bias")

    def hop(a, e):
        line_hop(a, e, 0)
        line_hop(a, e, 1)

    events = []
    for unit in units:
        events.append((unit.u, "two", unit, lambda unit=unit: step_two(unit)))
        late = unit.u + 1.1 if unit.u >= n + SLOTS - 1 else n + SLOTS - 1.9 + 0.05 * unit.u
        events.append((late, "three", unit, lambda unit=unit: step_three(unit)))
    for landing in landings_in + landings_heads:
        u = landing.unit.u
        after = n + SLOTS - 0.8 + 0.05 * u
        events.append((max(u + 3.2, after), "four", None, landing.spread))
        events.append((max(u + 5.3, after + 0.4), "five", None, landing.forward))
    for i, landing in enumerate(landings_out):
        u = unit_attention.u + 0.9 * i
        events.append((u + 3.4, "four", None, landing.spread))
        events.append((u + 5.5, "five", None, landing.forward))
    events.sort(key=lambda event: event[0])
    started, doubled = set(), set()

    def begin(unit):
        step_one(unit)
        started.add(unit.u)

    def advance(until):
        while events and events[0][0] <= until:
            _, name, unit, act = events[0]
            if name == "two" and unit.u not in started:
                return
            events.pop(0)
            if name == "two":
                doubled.add(unit.u)
            act()

    ua = unit_attention.u
    gathering = me.mark()
    last_rows()
    gathering += me.mark()
    for unit in units_hidden_in:
        grad_in(unit)
        begin(unit)
    project_rows(0, z == L - 1)
    project_rows(L - 1, z == 0)
    advance(ua + PACE[0])
    tasks = [(b, pair, side) for b in range(sequences) for pair in range(heads // 2) for side in range(2)]
    for i, (b, pair, side) in enumerate(tasks):
        attend(b, pair, side)
        if side == 1:
            settle_pair(b, pair)
        advance(ua + PACE[1 + 4 * i // len(tasks)])
    drain_unit(units_hidden_out[0])
    grad_out(unit_attention)
    begin(unit_attention)
    bias_out_begin()
    biases_begin()
    advance(ua + PACE[6])
    assert all(unit.u in doubled for unit in units_hidden_out + units_hidden_in)
    for unit in units_heads:
        drain_unit(units_hidden_in[unit.k])
        grad_in(unit)
        begin(unit)
    advance(ua + PACE[5])
    for turn, copy in gathering:
        me.sent(turn, copy)
    mixed_tiles()
    line_begin(0)
    advance(ua + PACE[7])
    for m in range(1, L):
        core_sum(0, m)
    hop(0, 0)
    advance(ua + PACE[8])
    d_normed_tiles()
    line_begin(1)
    biases_share()
    advance(ua)
    for m in range(1, L):
        core_sum(1, m)
    hop(1, 0)
    for e in range(1, L - 1):
        advance(ua + HOP * e - 0.5)
        hop(0, e)
        advance(ua + HOP * e + 0.5 * HOP - 0.5)
        hop(1, e)
    last = ua + HOP * (L - 1) - 0.5
    advance(last)
    finish_mixed()
    advance(last + 1.5)
    finish_normed()
    to_replicas(v.v2, v.got2, 1)
    advance(last + 2.5)
    norms_begin()
    advance(last + 4)
    norms_end()
    biases_end()
    advance(1000)
    for landing in landings:
        landing.finish()
    for unit in units:
        drain_unit(unit)
    for i, name in enumerate(GIVEN):
        me.arrived(getattr(v, name), v.give_sem.at[i])
    me.drain()


def fused(tokens, ln_gain, ln_bias, w_in, b_in, w_out, b_out, cotangent, cosine, sine):
    n, replicas = lax.axis_size("shard"), lax.axis_size("replica")
    X = max(replicas // 2, 1)
    Y = replicas // X
    L = n // 2
    rows = tokens.shape[0]
    group = rows * n
    depth = D // n
    q = depth // replicas
    head, fc = D // n, FF // n
    head3 = 3 * head
    width = head3 + fc
    both_heads = (group // SEQ_LEN) * (head // HEAD_DIM)
    vmem, dma = pltpu.VMEM, pltpu.SemaphoreType.DMA
    t = n - 2
    most = max(X, Y) - 1
    units = 2 * n + SLOTS
    scratch = {
        "nl": vmem((group, D), bf16), "ct": vmem((group, D), bf16),
        "wi": vmem((D, width), bf16), "wo": vmem((SLOTS * depth, D), bf16),
        "joined": vmem((group, head + fc), bf16), "dproj": vmem((group, width), bf16),
        "flip": vmem((depth, group), bf16),
        "oh": vmem((2, SEQ_LEN, HEAD_DIM), f32), "dq": vmem((2, SEQ_LEN, HEAD_DIM), f32),
        "dk": vmem((2, SEQ_LEN, HEAD_DIM), f32), "dv": vmem((2, SEQ_LEN, HEAD_DIM), f32),
        "g_out": vmem((SLOTS - 1, depth, D), bf16), "g_in": vmem((n, depth, fc), bf16),
        "b_own": vmem((1, width), f32),
        "tmp": vmem((L, rows, D), bf16), "acc": vmem((2, 8, D), f32),
        "v1": vmem((1, width + D), f32), "v1s": vmem((1, width + D), f32), "got1": vmem((replicas - 1, 1, width + D), f32),
        "v2": vmem((1, 2 * D), f32), "v2s": vmem((1, 2 * D), f32), "got2": vmem((replicas - 1, 1, 2 * D), f32),
        "got3": vmem((n - 1, 1, 2 * D), f32),
    }
    for name in ("qh", "kh", "vh", "doh"):
        scratch[name] = vmem((both_heads, SEQ_LEN, HEAD_DIM), bf16)
    for tag, count, wide in (("o", SLOTS, D), ("f", n, fc), ("q", n, head3)):
        a, b = half_of(wide), wide - half_of(wide)
        scratch["r1" + tag + "a"] = vmem((count, X - 1, Y * q, a), bf16)
        scratch["r1" + tag + "b"] = vmem((count, Y - 1, X * q, b), bf16)
        scratch["r2" + tag + "a"] = vmem((count, Y - 1, q, a), bf16)
        scratch["r2" + tag + "b"] = vmem((count, X - 1, q, b), bf16)
    sems = {
        "ag_recv": (2, 2, L), "sib_recv": (2, 2 * L), "ws_recv": (1,), "oz_recv": (SLOTS,), "wz_recv": (t, 2),
        "i_come": (t, 4, most), "i_rest": (t, 4), "o_come": (SLOTS, 2, most), "o_rest": (SLOTS, 2),
        "s1_recv": (units, 2, most), "s2_recv": (units, 2, most), "zi_recv": (units,), "zo_recv": (SLOTS,),
        "a_come": (units, 2, most), "a_rest": (units, 2),
        "ls_recv": (2, L), "lz_recv": (2, 2, L), "vr_recv": (2, replicas - 1), "vl_recv": (n - 1,), "vn_recv": (n - 1,),
        "pool": (POOL,),
    }
    scratch |= {name: dma(shape) for name, shape in sems.items()}
    scratch["own_sem"], scratch["tmp_sem"] = dma((5,)), dma((L,))
    any_space = pl.BlockSpec(memory_space=pl.ANY)
    loaded = {
        "tok": tokens, "gain": ln_gain.reshape(1, D), "bias": ln_bias.reshape(1, D), "b_in": b_in.reshape(1, 3 * D + FF),
        "cot": cotangent, "b_out": b_out.reshape(1, D), "cosine": cosine, "sine": sine,
    }
    scratch |= {name: vmem(value.shape, value.dtype) for name, value in loaded.items()}
    scratch |= {"block_out": vmem((rows, D), bf16), "grad_tokens": vmem((rows, D), bf16)}
    scratch |= {name: vmem((1, D), f32) for name in ("gb_out", "g_gain", "g_bias")}
    scratch["load_sem"], scratch["give_sem"] = dma((len(loaded),)), dma((len(GIVEN),))
    scratch["bias_sem"] = dma((4,))
    in_hbm = pl.BlockSpec(memory_space=pltpu.HBM)
    inputs = {"far_" + name: (value, in_hbm) for name, value in loaded.items()} | {
        "w_in": (w_in, in_hbm), "w_out": (w_out, in_hbm),
    }
    shape = jax.ShapeDtypeStruct
    outputs = {
        "fi": (shape((n, depth, width), bf16), any_space), "fo": (shape((SLOTS, depth, D), bf16), any_space),
        "to_block_out": (shape((rows, D), bf16), in_hbm), "to_grad_tokens": (shape((rows, D), bf16), in_hbm),
        "gb_in": (shape((1, 3 * D + FF), f32), in_hbm), "to_gb_out": (shape((1, D), f32), in_hbm),
        "to_g_gain": (shape((1, D), f32), in_hbm), "to_g_bias": (shape((1, D), f32), in_hbm),
        "sbx": (shape((2, L, rows, D), bf16), any_space), "zbx": (shape((2, 2, L, rows, D), bf16), any_space),
    }
    done = pl.pallas_call(
        functools.partial(fused_kernel, n, replicas, list(inputs) + list(outputs) + list(scratch)),
        out_shape=tuple(out for out, _ in outputs.values()),
        in_specs=[spec for _, spec in inputs.values()],
        out_specs=tuple(spec for _, spec in outputs.values()),
        scratch_shapes=list(scratch.values()),
        compiler_params=pltpu.CompilerParams(collective_id=0, has_side_effects=True, vmem_limit_bytes=63 << 20),
        name="fused",
    )(*[value for value, _ in inputs.values()])
    return {name.removeprefix("to_"): value for name, value in zip(outputs, done, strict=True)}


def widen_kernel(n, names, *refs):
    v = Names(names, refs)
    depth = D // n
    head, fc = D // n, FF // n
    jobs = [("out", i) for i in range(SLOTS)] + [("in", d) for d in range(n)]
    passed = [
        (
            pltpu.make_async_copy(getattr(v, name), getattr(v, "by_" + name), v.pass_sem.at[p, 0]),
            pltpu.make_async_copy(getattr(v, "by_" + name), getattr(v, "to_" + name), v.pass_sem.at[p, 1]),
        )
        for p, name in enumerate(PASSED)
    ]

    def load(j):
        kind, i = jobs[j]
        src, dst = (v.fi.at[i], v.low_in.at[i]) if kind == "in" else (v.fo.at[i], v.low_out.at[i])
        return pltpu.make_async_copy(src, dst, v.load_sem.at[j])

    def stores(j):
        kind, i = jobs[j]
        if kind == "out":
            return [pltpu.make_async_copy(v.wide_out.at[i], v.go.at[pl.ds(i * depth, depth)], v.store_sem.at[j, 0])]
        places = [(part * D + head * i, part * head, head) for part in range(3)] + [(3 * D + fc * i, 3 * head, fc)]
        return [
            pltpu.make_async_copy(
                v.wide_in.at[i, :, pl.ds(src, size)], v.gi.at[:, pl.ds(dst, size)], v.store_sem.at[j, p]
            )
            for p, (dst, src, size) in enumerate(places)
        ]

    for j in range(len(jobs)):
        load(j).start()
    for first, _ in passed:
        first.start()
    for j, (kind, i) in enumerate(jobs):
        load(j).wait()
        low, wide = (v.low_in, v.wide_in) if kind == "in" else (v.low_out, v.wide_out)

        def body(k, low=low, wide=wide, i=i):
            at = rows_at(k * 16, 16)
            wide[i, at, :] = low[i, at, :].astype(f32)

        loop(depth // 16, body)
        for copy in stores(j):
            copy.start()
    for first, then in passed:
        first.wait()
        then.start()
    for j in range(len(jobs)):
        for copy in stores(j):
            copy.wait()
    for _, then in passed:
        then.wait()


PASSED = ("block_out", "grad_tokens", "gb_in", "gb_out", "g_gain", "g_bias")


def widen(results):
    n = lax.axis_size("shard")
    fi, fo = results["fi"], results["fo"]
    depth, width = fi.shape[1], fi.shape[2]
    dma, vmem, shape = pltpu.SemaphoreType.DMA, pltpu.VMEM, jax.ShapeDtypeStruct
    in_hbm = pl.BlockSpec(memory_space=pltpu.HBM)
    inputs = {"fi": fi, "fo": fo} | {name: results[name] for name in PASSED}
    outputs = {"gi": shape((depth, 3 * D + FF), f32), "go": shape((SLOTS * depth, D), f32)} | {
        "to_" + name: shape(results[name].shape, results[name].dtype) for name in PASSED
    }
    scratch = {
        "low_in": vmem((n, depth, width), bf16), "low_out": vmem((SLOTS, depth, D), bf16),
        "wide_in": vmem((n, depth, width), f32), "wide_out": vmem((SLOTS, depth, D), f32),
        "load_sem": dma((n + SLOTS,)), "store_sem": dma((n + SLOTS, 4)), "pass_sem": dma((len(PASSED), 2)),
    } | {"by_" + name: vmem(results[name].shape, results[name].dtype) for name in PASSED}
    names = list(inputs) + list(outputs) + list(scratch)
    done = pl.pallas_call(
        functools.partial(widen_kernel, n, names),
        out_shape=tuple(outputs.values()),
        in_specs=[in_hbm] * len(inputs),
        out_specs=(in_hbm,) * len(outputs),
        scratch_shapes=list(scratch.values()),
        compiler_params=pltpu.CompilerParams(vmem_limit_bytes=60 << 20),
        name="widen",
    )(*inputs.values())
    return dict(zip(outputs, done, strict=True))


def angle_tables():
    lane = np.arange(128) % HEAD_DIM
    frequency = 10000.0 ** (-2.0 * (lane % (ROT // 2)) / ROT)
    angle = np.arange(SEQ_LEN)[:, None] * frequency[None, :]
    turned = (lane < ROT)[None, :]
    return np.where(turned, np.cos(angle), 1.0).astype(np.float32), np.where(turned, np.sin(angle), 0.0).astype(np.float32)


def local(tokens, ln_gain, ln_bias, w_in, b_in, w_out, b_out, cotangent):
    cosine, sine = angle_tables()
    results = fused(tokens, ln_gain, ln_bias, w_in, b_in, w_out, b_out, cotangent, jnp.asarray(cosine), jnp.asarray(sine))
    done = widen(results)
    return (
        done["to_block_out"], done["to_grad_tokens"], done["to_g_gain"].reshape(D), done["to_g_bias"].reshape(D),
        done["gi"], done["to_gb_in"].reshape(3 * D + FF), done["go"], done["to_gb_out"].reshape(D),
    )


def solution(mesh):
    both_axes = P(("replica", "shard"), None)
    return jax.shard_map(
        local,
        mesh=mesh,
        in_specs=(both_axes, P(), P(), P("shard", None), P(), P("shard", None), P(), both_axes),
        out_specs=(both_axes, both_axes, P(), P(), P("shard", None), P(), P("shard", None), P()),
        check_vma=False,
    )
```

```python
import functools
import jax
import jax.numpy as jnp
import numpy as np
from jax import lax
from jax.experimental import pallas as pl
from jax.experimental.pallas import tpu as pltpu
from jax.sharding import PartitionSpec as P

D = 2048
HEADS = 32
HEAD_DIM = 64
ROT = 32
FF = 8192
SEQ_LEN = 1024
SLOTS = 5

epsilon = 1e-05
masked_score = -1e30
MESH = pl.DeviceIdType.MESH
f32 = jnp.float32
bf16 = jnp.bfloat16


class Place:
    def __init__(self, n, replicas):
        self.n, self.R = n, replicas
        self.X = max(replicas // 2, 1)
        self.Y = replicas // self.X
        self.L = n // 2
        self.r, self.s = lax.axis_index("replica"), lax.axis_index("shard")
        self.x, self.y = self.r % self.X, self.r // self.X
        self.z, self.c = self.s // 2, self.s % 2
        self.sibling = (self.r, self.s + 1 - 2 * self.c)
        self.pool, self.used, self.turn = None, {}, 0

    def x_peer(self, dx):
        return self.y * self.X + (self.x + dx) % self.X

    def y_peer(self, dy):
        return ((self.y + dy) % self.Y) * self.X + self.x

    def send(self, src, dst, recv_sem, device, when=None):
        turn = self.turn % self.pool.shape[0]
        self.turn += 1
        self.sent(turn)
        copy = pltpu.make_async_remote_copy(
            src_ref=src, dst_ref=dst, send_sem=self.pool.at[turn], recv_sem=recv_sem,
            device_id=device, device_id_type=MESH,
        )
        guarded(when, copy.start)
        self.used[turn] = (when, copy.wait_send)
        return turn, copy

    def sent(self, turn, copy=None):
        if turn in self.used and (copy is None or self.used[turn][1].__self__ is copy):
            when, wait = self.used.pop(turn)
            guarded(when, wait)

    def local(self, src, dst, sem, when=None):
        guarded(when, pltpu.make_async_copy(src, dst, sem).start)

    def arrived(self, ref, sem, when=None):
        guarded(when, pltpu.make_async_copy(ref, ref, sem).wait)

    def mark(self):
        return [(turn, wait.__self__) for turn, (_, wait) in sorted(self.used.items())]

    def drain(self):
        for turn in sorted(self.used):
            self.sent(turn)

    def meet(self, line=True, square=True, whole=False):
        barrier = pltpu.get_barrier_semaphore()
        peers = []
        if line:
            peers += [(self.r, (self.s + k) % self.n) for k in range(1, self.n)]
        if whole:
            peers += [((self.r + k) % self.R, self.s) for k in range(1, self.R)]
        elif square:
            peers += [(self.x_peer(dx), self.s) for dx in range(1, self.X)]
            peers += [(self.y_peer(dy), self.s) for dy in range(1, self.Y)]
        for peer in peers:
            pl.semaphore_signal(barrier, inc=1, device_id=peer, device_id_type=MESH)
        pl.semaphore_wait(barrier, len(peers))


def guarded(when, act):
    if when is None:
        act()
    else:
        pl.when(when)(act)


def both(a, b):
    return b if a is None else a if b is None else jnp.logical_and(a, b)


def rows_at(start, size, multiple=16):
    return pl.ds(pl.multiple_of(start, multiple), size)


def half_of(width):
    return -(-width // 256) * 128


def slot_of(block, n):
    past = jnp.maximum(block - n, 0)
    first = block < n
    return jnp.where(first, block, past // 4), jnp.where(first, 0, 1 + past % 4)


def block_of(device, slot, n):
    return device if slot == 0 else n + 4 * device + slot - 1


UP = 0.7978845608028654
NT = (((1,), (1,)), ((), ()))
TALL = 512
PACE = (-13,-11,-9,-7,-4,-0.75,-1,-0.5,-0.4)
HOP = 2.5


POOL = 96
LOADED = ("tok", "gain", "bias", "b_in", "cot", "b_out", "cosine", "sine")
GIVEN = ("block_out", "grad_tokens", "gb_out", "g_gain", "g_bias")


class Names:
    def __init__(self, names, refs):
        for name, ref in zip(names, refs, strict=True):
            setattr(self, name, ref)


class Unit:
    def __init__(self, kind, k, buf, width, col0, one, two):
        self.kind, self.k, self.buf, self.width, self.col0 = kind, k, buf, width, col0
        cut = half_of(width)
        self.halves = ((0, cut), (cut, width - cut))
        self.one, self.two = one, two
        self.sent = []


def loop(count, body):
    def step(i, carry):
        body(i)
        return carry

    lax.fori_loop(0, count, step, 0)


def add_rows(store, loads, rows, strip=16):
    def step(i):
        at = rows_at(i * strip, strip)
        total = loads[0](at).astype(f32)
        for load in loads[1:]:
            total = total + load(at).astype(f32)
        store(at, total)

    loop(rows // strip, step)


def shifted(start, at):
    return pl.ds(pl.multiple_of(start + at.start, 16), at.size)


def fused_kernel(n, replicas, names, *refs):
    v = Names(names, refs)
    me = Place(n, replicas)
    me.pool = v.pool
    X, Y, L, r, s, z, c = me.X, me.Y, me.L, me.r, me.s, me.z, me.c
    rows = v.tok.shape[0]
    group = rows * n

    def loaded(*picked):
        for name in picked:
            me.arrived(getattr(v, name), v.load_sem.at[LOADED.index(name)])

    def give(name):
        me.local(getattr(v, name), getattr(v, "to_" + name), v.give_sem.at[GIVEN.index(name)])

    for i, name in enumerate(LOADED):
        me.local(getattr(v, "far_" + name), getattr(v, name), v.load_sem.at[i])
    depth = D // n
    q = depth // replicas
    head, fc = D // n, FF // n
    heads = head // HEAD_DIM
    sequences = group // SEQ_LEN
    head3 = 3 * head
    width = head3 + fc
    tall = group // TALL
    me.meet(whole=True)

    def chunk(ref, owner):
        return ref.at[rows_at(owner * rows, rows)]

    def ranges(device):
        return [(part * D + head * device, part * head, head) for part in range(3)] + [
            (3 * D + fc * device, head3, fc)
        ]

    order = list(range(L // 2, L)) + list(range(1, L // 2))

    def far(t):
        chip, m, bit = 0, order[t // 2], 1
        while bit < L:
            chip = chip + ((z // bit + m // bit) % 2) * bit
            bit *= 2
        return 2 * chip + t % 2

    pairs = (v.nl, v.ct)
    has_left, has_right = z > 0, z < L - 1
    left, right = (r, jnp.maximum(s - 2, 0)), (r, jnp.minimum(s + 2, n - 1))

    def spread_own(a, own):
        every = pairs[a]
        me.send(own, chunk(every, s), v.ag_recv.at[a, 0, 1], right, has_right)
        me.send(own, chunk(every, s), v.ag_recv.at[a, 1, 1], left, has_left)
        me.send(own, chunk(every, s), v.sib_recv.at[a, 0], me.sibling)

    me.local(v.far_cot, chunk(v.ct, s), v.own_sem.at[0])

    def send_far(t, which):
        device = far(t)
        back = 2 * (t // 2) + c
        for part, (src, dst, size) in enumerate(ranges(device)):
            if (part == 3) == (which == "fc"):
                me.send(
                    v.w_in.at[rows_at(r * q, q), rows_at(src, size, 128)],
                    v.wi.at[rows_at(s * depth + r * q, q), pl.ds(dst, size)], v.wz_recv.at[back, part // 3], (r, device))

    for t in range(n - 2):
        send_far(t, "fc")

    for i in range(SLOTS):
        device, slot = slot_of(SLOTS * s + i, n)
        mine = device == s
        near = jnp.logical_and(device // 2 == z, device != s)
        away = device // 2 != z
        full = v.wo.at[rows_at(slot * depth, depth)]
        me.local(v.w_out.at[pl.ds(i * depth, depth)], full, v.oz_recv.at[slot], mine)
        me.send(v.w_out.at[pl.ds(i * depth, depth)], full, v.oz_recv.at[slot], me.sibling, near)
        target = jnp.where(away, device, (s + 2) % n)
        me.send(
            v.w_out.at[rows_at(i * depth + r * q, q)], v.wo.at[rows_at(slot * depth + r * q, q)], v.oz_recv.at[slot], (r, target), away)
    for t in range(n - 2):
        send_far(t, "qkv")
    def normalise(at):
        wide = v.tok[at, :].astype(f32)
        centred = wide - jnp.mean(wide, axis=-1, keepdims=True)
        rstd = lax.rsqrt(jnp.mean(centred * centred, axis=-1, keepdims=True) + epsilon)
        return centred * rstd, rstd

    def norm_strip(i):
        at = rows_at(i * 16, 16)
        normed, _ = normalise(at)
        v.nl[rows_at(s * rows + i * 16, 16), :] = (normed * v.gain[...] + v.bias[...]).astype(bf16)

    loaded("tok", "gain", "bias", "b_in")
    loop(rows // 16, norm_strip)
    for src, dst, size in ranges(s):
        v.b_own[:, pl.ds(dst, size)] = v.b_in[:, rows_at(src, size, 128)]

    for part, (src, dst, size) in enumerate(ranges(s)):
        me.local(
            v.w_in.at[:, rows_at(src, size, 128)], v.wi.at[rows_at(s * depth, depth), pl.ds(dst, size)],
            v.own_sem.at[1 + part],
        )
    for part, (src, dst, size) in enumerate(ranges(me.sibling[1])):
        me.send(
            v.w_in.at[:, rows_at(src, size, 128)], v.wi.at[rows_at(s * depth, depth), pl.ds(dst, size)], v.ws_recv.at[0], me.sibling)

    def share(ref_of, halves, index, tag, when=None):
        come, rest = getattr(v, tag + "_come"), getattr(v, tag + "_rest")

        def direct(picked):
            for h in picked:
                ref = ref_of(r, *halves[h])
                for dx in range(1, X):
                    sem = come.at[index, h, X - dx - 1] if h % 2 == 0 else rest.at[index, h]
                    me.send(ref, ref, sem, (me.x_peer(dx), s), when)
                for dy in range(1, Y):
                    sem = rest.at[index, h] if h % 2 == 0 else come.at[index, h, Y - dy - 1]
                    me.send(ref, ref, sem, (me.y_peer(dy), s), when)

        def forward(picked):
            for h in picked:
                for d in range(1, X if h % 2 == 0 else Y):
                    ref = ref_of(me.x_peer(d) if h % 2 == 0 else me.y_peer(d), *halves[h])
                    me.arrived(ref, come.at[index, h, d - 1], when)
                    for e in range(1, Y if h % 2 == 0 else X):
                        peer = me.y_peer(e) if h % 2 == 0 else me.x_peer(e)
                        me.send(ref, ref, rest.at[index, h], (peer, s), when)

        def finish(picked):
            for h in picked:
                count = X * (Y - 1) if h % 2 == 0 else Y * (X - 1)
                me.arrived(ref_of(0, *halves[h], count), rest.at[index, h], when)

        return direct, forward, finish

    fc_half, qkv_half = half_of(fc), half_of(head3)
    halves_in = (
        (head3, fc_half), (head3 + fc_half, fc - fc_half), (0, qkv_half), (qkv_half, head3 - qkv_half),
    )

    def in_piece(t):
        def ref_of(replica, start, size, count=1):
            return v.wi.at[rows_at(far(t) * depth + replica * q, count * q), pl.ds(start, size)]

        return share(ref_of, halves_in, t, "i")

    def in_arrived(t, part):
        base = rows_at(far(t) * depth + r * q, q)
        if part == "fc":
            me.arrived(v.wi.at[base, pl.ds(head3, fc)], v.wz_recv.at[t, 1])
        else:
            me.arrived(v.wi.at[base, pl.ds(0, head3)], v.wz_recv.at[t, 0])

    out_half = half_of(D)
    halves_out = ((0, out_half), (out_half, D - out_half))

    def out_piece(j):
        source = block_of(s, j, n) // SLOTS

        def ref_of(replica, start, size, count=1):
            return v.wo.at[rows_at(j * depth + replica * q, count * q), pl.ds(start, size)]

        return share(ref_of, halves_out, j, "o", source // 2 != z)

    def out_arrived(j):
        source = block_of(s, j, n) // SLOTS
        me.arrived(v.wo.at[rows_at(j * depth + r * q, q)], v.oz_recv.at[j], source // 2 != z)
        me.arrived(v.wo.at[pl.ds(j * depth, depth)], v.oz_recv.at[j], source // 2 == z)

    def pass_on(k, a):
        every = pairs[a]
        for side, (source, there, onward) in enumerate(((s - 2 * k, right, has_right), (s + 2 * k, left, has_left))):
            known = (z - k >= 0) if side == 0 else (z + k < L)
            ref = chunk(every, jnp.clip(source, 0, n - 1))
            me.arrived(ref, v.ag_recv.at[a, side, k], known)
            if k < L - 1:
                me.send(ref, ref, v.ag_recv.at[a, side, k + 1], there, both(known, onward))
            me.send(
                ref, ref, v.sib_recv.at[a, 2 * k - 1 + side], me.sibling, known
            )

    def hidden_rows(chip, when=None, tiles=None):
        at = rows_at(jnp.clip(chip, 0, L - 1) * (2 * rows), 2 * rows)

        def body(j):
            cols = rows_at(head3 + depth * j, depth, 128)
            x = jnp.dot(v.nl[at, :], v.wi[:, cols], preferred_element_type=f32) + v.b_own[:, cols]
            square = x * x
            t = jnp.tanh(UP * (x + 0.044715 * (square * x)))
            v.joined[at, rows_at(head + depth * j, depth, 128)] = (0.5 * x * (1.0 + t)).astype(bf16)
            slope = 0.5 * (1.0 + t) + 0.5 * x * (1.0 - t * t) * (UP * (1.0 + (3 * 0.044715) * square))
            d_hidden = lax.dot_general(
                v.ct[at, :], v.wo[rows_at(depth + depth * j, depth, 128), :], NT, preferred_element_type=f32
            )
            v.dproj[at, cols] = (d_hidden * slope).astype(bf16)

        def work():
            if tiles is None:
                loop(fc // depth, body)
            else:
                body(tiles)

        guarded(when, work)

    ins = [in_piece(t) for t in range(n - 2)]
    outs = [out_piece(j) for j in range(SLOTS)]
    fc_h, qkv_h = (0, 1), (2, 3)
    def lanes_turn(x, at, sign):
        lane = lax.broadcasted_iota(jnp.int32, x.shape, 1) % HEAD_DIM
        sine = v.sine[at, :] * sign
        swapped = jnp.where(lane < ROT // 2, -pltpu.roll(x, 128 - ROT // 2, 1), pltpu.roll(x, ROT // 2, 1))
        return x * v.cosine[at, :] + swapped * sine

    def project_rows(chip, when=None):
        chip = jnp.clip(chip, 0, L - 1)
        tall = 2 * rows
        at = rows_at(chip * tall, tall)
        inside = rows_at(chip % (SEQ_LEN // tall) * tall, tall)
        base = chip // (SEQ_LEN // tall) * heads

        def part_of(part):
            if part == 3:
                return lax.dot_general(v.ct[at, :], v.wo[:depth, :], NT, preferred_element_type=f32)
            cols = pl.ds(head * part, head)
            return jnp.dot(v.nl[at, :], v.wi[:, cols], preferred_element_type=f32) + v.b_own[:, cols]

        def work():
            for part, to in enumerate((v.qh, v.kh, v.vh, v.doh)):
                wide = part_of(part)
                for slab in range(head // 128):
                    x = wide[:, 128 * slab : 128 * (slab + 1)]
                    if part < 2:
                        x = lanes_turn(x, inside, 1.0)
                    x = x.astype(bf16)
                    to[base + 2 * slab, inside, :] = x[:, :HEAD_DIM]
                    to[base + 2 * slab + 1, inside, :] = x[:, HEAD_DIM:]

        guarded(when, work)

    arrivals, steps = [], []
    for t in range(n - 2):
        arrivals.append((lambda t=t: (in_arrived(t, "fc"), ins[t][0](fc_h)), lambda t=t: ins[t][1](fc_h)))
    for j in range(SLOTS):
        arrivals.append((lambda j=j: (out_arrived(j), outs[j][0](fc_h)), lambda j=j: outs[j][1](fc_h)))
    for t in range(n - 2):
        arrivals.append((lambda t=t: (in_arrived(t, "qkv"), ins[t][0](qkv_h)), lambda t=t: ins[t][1](qkv_h)))
    for i, (first, then) in enumerate(arrivals):
        steps.append((i, first))
        steps.append((i + 2.5, then))
    steps.append((7.7, lambda: (loaded("cot", "b_out", "cosine", "sine"), spread_own(1, v.cot), spread_own(0, chunk(v.nl, s)))))
    for k in range(1, L - 1):
        steps.append((8.1 + 4.4 * k, lambda k=k: pass_on(k, 1)))
        steps.append((8.2 + 4.4 * k, lambda k=k: pass_on(k, 0)))
    for _, step in sorted(steps, key=lambda pair: pair[0]):
        step()
    other = me.sibling[1]

    def rows_there(k):
        for every in (v.nl, v.ct):
            a = 0 if every is v.nl else 1
            if k == 0:
                me.arrived(chunk(every, other), v.sib_recv.at[a, 0])
                continue
            for side in range(2):
                source = other - 2 * k if side == 0 else other + 2 * k
                known = (z - k >= 0) if side == 0 else (z + k < L)
                me.arrived(chunk(every, jnp.clip(source, 0, n - 1)), v.sib_recv.at[a, 2 * k - 1 + side], known)

    me.arrived(chunk(v.ct, s), v.own_sem.at[0])
    for piece in ins:
        piece[2](fc_h)
    for piece in outs:
        piece[2](fc_h)
    for part, (_, dst, size) in enumerate(ranges(s)):
        me.arrived(v.wi.at[rows_at(s * depth, depth), pl.ds(dst, size)], v.own_sem.at[1 + part])
    me.arrived(v.wi.at[rows_at(other * depth, depth), :], v.ws_recv.at[0])
    for k in range(L - 1):
        rows_there(k)
        if k == 0:
            hidden_rows(z)
        else:
            hidden_rows(z - k, z - k >= 0)
            hidden_rows(z + k, z + k < L)
    for piece in ins:
        piece[2](qkv_h)
    for k in range(L - 1):
        project_rows(z - k, z - k >= 0 if k else None)
        if k:
            project_rows(z + k, z + k < L)

    def last_rows():
        pass_on(L - 1, 1)
        pass_on(L - 1, 0)
        rows_there(L - 1)
        for j, unit in enumerate(units_hidden_out):
            hidden_rows(0, z == L - 1, j)
            hidden_rows(L - 1, z == 0, j)
            grad_out(unit)
            begin(unit)

    def tile(i, size=TALL):
        return rows_at(i * size, size)

    def turned_columns(ref, start, size):
        def body(m):
            v.flip[:size, rows_at(m * 256, 256, 256)] = jnp.transpose(ref[tile(m, 256), pl.ds(start, size)])

        loop(group // 256, body)

    def turned_rows(start):
        def body(m):
            v.flip[:depth, rows_at(m * 256, 256, 256)] = jnp.transpose(v.nl[tile(m, 256), rows_at(start, depth, 128)])

        loop(group // 256, body)

    def grad_out(unit):
        turned_columns(v.joined, depth * unit.k, depth)

        def body(m):
            cols = rows_at(m * 512, 512, 512)
            unit.buf[:, cols] = jnp.dot(v.flip[:depth, :], v.ct[:, cols], preferred_element_type=f32).astype(bf16)

        loop(D // 512, body)

    def grad_in(unit):
        turned_rows(((s + unit.k) % n) * depth)
        for start in range(0, unit.width, 256):
            size = min(256, unit.width - start)
            unit.buf[:, pl.ds(start, size)] = jnp.dot(
                v.flip[:depth, :], v.dproj[:, pl.ds(unit.col0 + start, size)], preferred_element_type=f32
            ).astype(bf16)

    scale = HEAD_DIM ** (-0.5)
    block = 256

    def attend(b, pair, side):
        hb = b * heads + 2 * pair + side
        key_turned = jnp.transpose(v.kh[hb])
        value_turned = jnp.transpose(v.vh[hb])
        v.dk[side] = jnp.zeros((SEQ_LEN, HEAD_DIM), f32)
        v.dv[side] = jnp.zeros((SEQ_LEN, HEAD_DIM), f32)
        for i in range(SEQ_LEN // block):
            at, past = pl.ds(i * block, block), (i + 1) * block
            query, d_out = v.qh[hb, at, :], v.doh[hb, at, :]
            scores = lax.dot_general(v.kh[hb, :past, :], query, NT, preferred_element_type=f32) * scale
            key_place = lax.broadcasted_iota(jnp.int32, (past, block), 0)
            query_place = lax.broadcasted_iota(jnp.int32, (past, block), 1) + i * block
            scores = jnp.where(key_place <= query_place, scores, masked_score)
            raised = jnp.exp(scores - jnp.max(scores, axis=0, keepdims=True))
            chances = raised * (1.0 / jnp.sum(raised, axis=0, keepdims=True))
            low = chances.astype(bf16)
            out_turned = jnp.dot(value_turned[:, :past], low, preferred_element_type=f32)
            d_out_turned = jnp.transpose(d_out.astype(f32))
            delta = jnp.sum(d_out_turned * out_turned, axis=0, keepdims=True)
            d_chances = lax.dot_general(v.vh[hb, :past, :], d_out, NT, preferred_element_type=f32)
            d_scores = (chances * (d_chances - delta)).astype(bf16)
            v.oh[side, at, :] = jnp.transpose(out_turned)
            d_query_turned = jnp.dot(key_turned[:, :past], d_scores, preferred_element_type=f32) * scale
            v.dq[side, at, :] = jnp.transpose(d_query_turned)
            v.dk[side, :past, :] += jnp.dot(d_scores, query, preferred_element_type=f32) * scale
            v.dv[side, :past, :] += jnp.dot(low, d_out, preferred_element_type=f32)

    def settle_pair(b, pair):
        def settle(m):
            at = tile(m, 256)
            put = rows_at(b * SEQ_LEN + m * 256, 256)

            def slab(ref):
                return jnp.concatenate([ref[0, at, :], ref[1, at, :]], axis=1)

            v.joined[put, pl.ds(128 * pair, 128)] = slab(v.oh).astype(bf16)
            v.dproj[put, pl.ds(128 * pair, 128)] = lanes_turn(slab(v.dq), at, -1.0).astype(bf16)
            v.dproj[put, pl.ds(head + 128 * pair, 128)] = lanes_turn(slab(v.dk), at, -1.0).astype(bf16)
            v.dproj[put, pl.ds(2 * head + 128 * pair, 128)] = slab(v.dv).astype(bf16)

        loop(SEQ_LEN // 256, settle)

    def mixed_tiles():
        def body(i):
            m, cols = i % tall, rows_at((i // tall) * 256, 256, 256)
            v.ct[tile(m), cols] = jnp.dot(v.joined[tile(m), :], v.wo[:, cols], preferred_element_type=f32).astype(bf16)

        loop(tall * (D // 256), body)

    def d_normed_tiles():
        def body(i):
            m, at = i % tall, (i // tall) * 256
            v.nl[tile(m), rows_at(at, 256, 256)] = lax.dot_general(
                v.dproj[tile(m), :], v.wi[rows_at(at, 256, 256), :], NT, preferred_element_type=f32
            ).astype(bf16)

        loop(tall * (D // 256), body)

    def quarter(half, replica):
        x, y = replica % X, replica // X
        return x * Y + y if half == 0 else y * X + x

    units_hidden_out = [
        Unit("out", j, v.g_out.at[j - 1], D, 0, (v.r1oa, v.r1ob), (v.r2oa, v.r2ob)) for j in range(1, SLOTS)
    ]
    units_hidden_in = [
        Unit("in", k, v.g_in.at[k], fc, head3, (v.r1fa, v.r1fb), (v.r2fa, v.r2fb)) for k in range(n)
    ]
    unit_attention = Unit("out", 0, v.g_out.at[0], D, 0, (v.r1oa, v.r1ob), (v.r2oa, v.r2ob))
    units_heads = [
        Unit("in", k, v.g_in.at[k, :, pl.ds(0, head3)], head3, 0, (v.r1qa, v.r1qb), (v.r2qa, v.r2qb))
        for k in range(n)
    ]
    units = units_hidden_out + units_hidden_in + [unit_attention] + units_heads
    for u, unit in enumerate(units):
        unit.u = u

    def step_one(unit):
        unit.sent = []
        for half, (start, size) in enumerate(unit.halves):
            run = (Y if half == 0 else X) * q
            span = X if half == 0 else Y
            for d in range(1, span):
                peer = me.x_peer(d) if half == 0 else me.y_peer(d)
                place = (me.x + d) % X if half == 0 else (me.y + d) % Y
                unit.sent.append(me.send(
                    unit.buf.at[rows_at(place * run, run), pl.ds(start, size)],
                    unit.one[half].at[unit.k, span - d - 1], v.s1_recv.at[unit.u, half, span - d - 1], (peer, s)))

    def drain_unit(unit):
        for turn, copy in unit.sent:
            me.sent(turn, copy)

    def step_two(unit):
        for half, (start, size) in enumerate(unit.halves):
            run = (Y if half == 0 else X) * q
            span = X if half == 0 else Y
            place = me.x if half == 0 else me.y
            got, k = unit.one[half], unit.k
            for d in range(1, span):
                me.arrived(got.at[k, d - 1], v.s1_recv.at[unit.u, half, d - 1])

            def own(at):
                return unit.buf[shifted(place * run, at), pl.ds(start, size)]

            def store(at, total):
                got[k, 0, at, :] = total.astype(bf16)

            add_rows(store, [own] + [lambda at, d=d: got[k, d - 1, at, :] for d in range(1, span)], run)
            span2 = Y if half == 0 else X
            for d in range(1, span2):
                peer = me.y_peer(d) if half == 0 else me.x_peer(d)
                place2 = (me.y + d) % Y if half == 0 else (me.x + d) % X
                me.send(
                    got.at[k, 0, rows_at(place2 * q, q)], unit.two[half].at[k, span2 - d - 1], v.s2_recv.at[unit.u, half, span2 - d - 1], (peer, s))

    def arrive_sems(unit):
        return unit.u

    def step_three(unit):
        for half, (start, size) in enumerate(unit.halves):
            span2 = Y if half == 0 else X
            place2 = me.y if half == 0 else me.x
            kept, got, k = unit.one[half], unit.two[half], unit.k
            for d in range(1, span2):
                me.arrived(got.at[k, d - 1], v.s2_recv.at[unit.u, half, d - 1])

            def own(at):
                return kept[k, 0, shifted(place2 * q, at), :]

            def store(at, total):
                got[k, 0, at, :] = total.astype(bf16)

            add_rows(store, [own] + [lambda at, d=d: got[k, d - 1, at, :] for d in range(1, span2)], q)
            at = rows_at(quarter(half, r) * q, q)
            cols = pl.ds(unit.col0 + start, size)
            if unit.kind == "in":
                dst = v.fi.at[s, at, cols]
                if k == 0:
                    me.local(got.at[k, 0], dst, v.zi_recv.at[unit.u])
                else:
                    me.send(
                        got.at[k, 0], dst, v.zi_recv.at[unit.u], (r, (s + k) % n)
                    )
            else:
                natural = block_of(s, k, n)
                device, i = natural // SLOTS, natural % SLOTS
                dst = v.fo.at[i, at, cols]
                me.local(got.at[k, 0], dst, v.zo_recv.at[i], device == s)
                target = jnp.where(device == s, (s + 1) % n, device)
                me.send(got.at[k, 0], dst, v.zo_recv.at[i], (r, target), device != s)

    apart = 0 if X == Y else 1

    class Landing:
        def __init__(self, kind, k, index, unit):
            self.kind, self.k, self.index, self.unit = kind, k, index, unit

        def ref(self, half, replica):
            at = rows_at(quarter(half, replica) * q, q)
            start, size = self.unit.halves[half]
            cols = pl.ds(self.unit.col0 + start, size)
            if self.kind == "in":
                return v.fi.at[(s - self.k) % n, at, cols]
            return v.fo.at[self.k, at, cols]

        def rows(self, half, count):
            start, size = self.unit.halves[half] if half is not None else (0, self.unit.width)
            cols = pl.ds(self.unit.col0 + start, size)
            if self.kind == "in":
                return v.fi.at[(s - self.k) % n, pl.ds(0, count * q), cols]
            return v.fo.at[self.k, pl.ds(0, count * q), cols]

        def spread(self):
            u = self.index
            me.arrived(self.rows(None, 1), v.zi_recv.at[self.unit.u] if self.kind == "in" else v.zo_recv.at[self.k])
            for half in range(2):
                ref = self.ref(half, r)
                for d in range(1, X):
                    sem = v.a_come.at[u, 0, X - d - 1] if half == 0 else v.a_rest.at[u, apart]
                    me.send(ref, ref, sem, (me.x_peer(d), s))
                for d in range(1, Y):
                    sem = v.a_rest.at[u, 0] if half == 0 else v.a_come.at[u, apart, Y - d - 1]
                    me.send(ref, ref, sem, (me.y_peer(d), s))

        def forward(self):
            u = self.index
            if not apart:
                for d in range(1, X):
                    me.arrived(self.rows(None, 1), v.a_come.at[u, 0, d - 1])
            for half in range(2):
                for d in range(1, X if half == 0 else Y):
                    ref = self.ref(half, me.x_peer(d) if half == 0 else me.y_peer(d))
                    if apart:
                        me.arrived(ref, v.a_come.at[u, half, d - 1])
                    for e in range(1, Y if half == 0 else X):
                        peer = me.y_peer(e) if half == 0 else me.x_peer(e)
                        me.send(ref, ref, v.a_rest.at[u, half * apart], (peer, s))

        def finish(self):
            if not apart:
                me.arrived(self.rows(None, X * (Y - 1)), v.a_rest.at[self.index, 0])
                return
            for half in range(2):
                count = X * (Y - 1) if half == 0 else Y * (X - 1)
                me.arrived(self.rows(half, count), v.a_rest.at[self.index, half])

    landings_in = [Landing("in", k, k, unit) for k, unit in enumerate(units_hidden_in)]
    landings_out = [Landing("out", i, n + i, unit_attention) for i in range(SLOTS)]
    landings_heads = [Landing("in", unit.k, n + SLOTS + unit.k, unit) for unit in units_heads]
    landings = landings_in + landings_out + landings_heads

    line_parts = (v.ct, v.nl)

    def line_begin(a):
        part = line_parts[a]
        for line in range(L):
            me.send(
                chunk(part, 2 * line + 1 - c), v.sbx.at[a, line], v.ls_recv.at[a, line], me.sibling
            )

    def fetch(src, slot):
        copy = pltpu.make_async_copy(src, v.tmp.at[slot], v.tmp_sem.at[slot])
        copy.start()
        return copy

    def core_sum(a, m):
        part = line_parts[a]
        line = (z + m) % L
        me.arrived(v.sbx.at[a, line], v.ls_recv.at[a, line])
        fetch(v.sbx.at[a, line], m).wait()
        start = (2 * line + c) * rows

        def store(at, total):
            part[shifted(start, at), :] = total.astype(bf16)

        add_rows(store, [lambda at: part[shifted(start, at), :], lambda at: v.tmp[m, at, :]], rows)

    def line_hop(a, e, side):
        part = line_parts[a]
        if side == 0:
            line, inner, nearer = e - (L - 1 - z), has_right, left
            due = jnp.logical_and(line >= 0, line < z)
        else:
            line, inner, nearer = L - 1 - e + z, has_left, right
            due = jnp.logical_and(line > z, line < L)
        line = jnp.clip(line, 0, L - 1)
        start = (2 * line + c) * rows

        @pl.when(both(due, inner))
        def _():
            me.arrived(v.zbx.at[a, side, line], v.lz_recv.at[a, side, line])
            fetch(v.zbx.at[a, side, line], 0).wait()

            def store(at, total):
                part[shifted(start, at), :] = total.astype(bf16)

            add_rows(store, [lambda at: part[shifted(start, at), :], lambda at: v.tmp[0, at, :]], rows)

        me.send(
            part.at[rows_at(start, rows)], v.zbx.at[a, side, line],
            v.lz_recv.at[a, side, line], nearer, due)

    def line_sum(a):
        part = line_parts[a]
        me.arrived(v.sbx.at[a, z], v.ls_recv.at[a, z])
        fetch(v.sbx.at[a, z], 0).wait()
        for side, known in enumerate((has_right, has_left)):
            me.arrived(v.zbx.at[a, side, z], v.lz_recv.at[a, side, z], known)

            @pl.when(known)
            def _():
                fetch(v.zbx.at[a, side, z], 1 + side).wait()

            @pl.when(jnp.logical_not(known))
            def _():
                v.tmp[1 + side] = jnp.zeros((rows, D), bf16)

        def strip(at):
            total = part[shifted(s * rows, at), :].astype(f32)
            for m in range(3):
                total = total + v.tmp[m, at, :].astype(f32)
            return total

        return strip

    def finish_mixed():
        strip = line_sum(0)

        def body(i):
            at = rows_at(i * 16, 16)
            v.block_out[at, :] = (v.tok[at, :].astype(f32) + strip(at) + v.b_out[...]).astype(bf16)

        loop(rows // 16, body)
        give("block_out")

    def finish_normed():
        strip = line_sum(1)
        v.acc[...] = jnp.zeros(v.acc.shape, f32)

        def body(i):
            at = rows_at(i * 16, 16)
            d_normed = strip(at)
            normed, rstd = normalise(at)
            e = d_normed * v.gain[...]
            back = rstd * (
                e - jnp.mean(e, axis=-1, keepdims=True) - normed * jnp.mean(e * normed, axis=-1, keepdims=True)
            )
            v.grad_tokens[at, :] = (v.cot[at, :].astype(f32) + back).astype(bf16)
            product = d_normed * normed
            v.acc[0] += product[:8] + product[8:]
            v.acc[1] += d_normed[:8] + d_normed[8:]

        loop(rows // 16, body)
        give("grad_tokens")
        v.v2[:, pl.ds(0, D)] = jnp.sum(v.acc[0], axis=0, keepdims=True)
        v.v2[:, pl.ds(D, D)] = jnp.sum(v.acc[1], axis=0, keepdims=True)

    def to_replicas(vec, got, index):
        for k in range(1, replicas):
            me.send(
                vec, got.at[replicas - k - 1], v.vr_recv.at[index, replicas - k - 1],
                ((r + k) % replicas, s))

    def from_replicas(vec, got, index):
        for k in range(1, replicas):
            me.arrived(got.at[k - 1], v.vr_recv.at[index, k - 1])
        total = vec[...]
        for k in range(1, replicas):
            total = total + got[k - 1]
        return total

    def biases_begin():
        ones = jnp.ones((8, group), bf16)
        for start in range(0, width, 256):
            size = min(256, width - start)
            v.v1[:, pl.ds(start, size)] = jnp.dot(ones, v.dproj[:, pl.ds(start, size)], preferred_element_type=f32)[:1]
        to_replicas(v.v1, v.got1, 0)

    def bias_out_begin():
        ones = jnp.ones((8, group), bf16)

        def body(i):
            cols = rows_at(i * 256, 256, 256)
            v.v1[:, rows_at(width + i * 256, 256, 256)] = jnp.dot(ones, v.ct[:, cols], preferred_element_type=f32)[:1]

        loop(D // 256, body)

    def biases_share():
        v.v1s[...] = from_replicas(v.v1, v.got1, 0)
        v.gb_out[...] = v.v1s[:, pl.ds(width, D)]
        give("gb_out")
        for part, (src, dst, size) in enumerate(ranges(s)):
            at = rows_at(src, size, 128)
            me.local(v.v1s.at[:, pl.ds(dst, size)], v.gb_in.at[:, at], v.bias_sem.at[part])
            for k in range(1, n):
                me.send(
                    v.v1s.at[:, pl.ds(dst, size)], v.gb_in.at[:, at],
                    v.vl_recv.at[n - k - 1], (r, (s + k) % n))

    def biases_end():
        for part, (src, _, size) in enumerate(ranges(s)):
            me.arrived(v.gb_in.at[:, rows_at(src, size, 128)], v.bias_sem.at[part])
        for k in range(1, n):
            me.arrived(v.gb_in.at[:, pl.ds(0, width)], v.vl_recv.at[k - 1])

    def norms_begin():
        v.v2s[...] = from_replicas(v.v2, v.got2, 1)
        for k in range(1, n):
            me.send(v.v2s, v.got3.at[n - k - 1], v.vn_recv.at[n - k - 1], (r, (s + k) % n))

    def norms_end():
        for k in range(1, n):
            me.arrived(v.got3.at[k - 1], v.vn_recv.at[k - 1])
        total = v.v2s[...]
        for k in range(1, n):
            total = total + v.got3[k - 1]
        v.g_gain[...] = total[:, :D]
        v.g_bias[...] = total[:, D:]
        give("g_gain")
        give("g_bias")

    def hop(a, e):
        line_hop(a, e, 0)
        line_hop(a, e, 1)

    events = []
    for unit in units:
        events.append((unit.u, "two", unit, lambda unit=unit: step_two(unit)))
        late = unit.u + 1.1 if unit.u >= n + SLOTS - 1 else n + SLOTS - 1.9 + 0.05 * unit.u
        events.append((late, "three", unit, lambda unit=unit: step_three(unit)))
    for landing in landings_in + landings_heads:
        u = landing.unit.u
        after = n + SLOTS - 0.8 + 0.05 * u
        events.append((max(u + 3.2, after), "four", None, landing.spread))
        events.append((max(u + 5.3, after + 0.4), "five", None, landing.forward))
    for i, landing in enumerate(landings_out):
        u = unit_attention.u + 0.9 * i
        events.append((u + 3.4, "four", None, landing.spread))
        events.append((u + 5.5, "five", None, landing.forward))
    events.sort(key=lambda event: event[0])
    started, doubled = set(), set()

    def begin(unit):
        step_one(unit)
        started.add(unit.u)

    def advance(until):
        while events and events[0][0] <= until:
            _, name, unit, act = events[0]
            if name == "two" and unit.u not in started:
                return
            events.pop(0)
            if name == "two":
                doubled.add(unit.u)
            act()

    ua = unit_attention.u
    gathering = me.mark()
    last_rows()
    gathering += me.mark()
    for unit in units_hidden_in:
        grad_in(unit)
        begin(unit)
    project_rows(0, z == L - 1)
    project_rows(L - 1, z == 0)
    advance(ua + PACE[0])
    tasks = [(b, pair, side) for b in range(sequences) for pair in range(heads // 2) for side in range(2)]
    for i, (b, pair, side) in enumerate(tasks):
        attend(b, pair, side)
        if side == 1:
            settle_pair(b, pair)
        advance(ua + PACE[1 + 4 * i // len(tasks)])
    drain_unit(units_hidden_out[0])
    grad_out(unit_attention)
    begin(unit_attention)
    bias_out_begin()
    biases_begin()
    advance(ua + PACE[6])
    assert all(unit.u in doubled for unit in units_hidden_out + units_hidden_in)
    for unit in units_heads:
        drain_unit(units_hidden_in[unit.k])
        grad_in(unit)
        begin(unit)
    advance(ua + PACE[5])
    for turn, copy in gathering:
        me.sent(turn, copy)
    mixed_tiles()
    line_begin(0)
    advance(ua + PACE[7])
    for m in range(1, L):
        core_sum(0, m)
    hop(0, 0)
    advance(ua + PACE[8])
    d_normed_tiles()
    line_begin(1)
    biases_share()
    advance(ua)
    for m in range(1, L):
        core_sum(1, m)
    hop(1, 0)
    for e in range(1, L - 1):
        advance(ua + HOP * e - 0.5)
        hop(0, e)
        advance(ua + HOP * e + 0.5 * HOP - 0.5)
        hop(1, e)
    last = ua + HOP * (L - 1) - 0.5
    advance(last)
    finish_mixed()
    advance(last + 1.5)
    finish_normed()
    to_replicas(v.v2, v.got2, 1)
    advance(last + 2.5)
    norms_begin()
    advance(last + 4)
    norms_end()
    biases_end()
    advance(1000)
    for landing in landings:
        landing.finish()
    for unit in units:
        drain_unit(unit)
    for i, name in enumerate(GIVEN):
        me.arrived(getattr(v, name), v.give_sem.at[i])
    me.drain()


def fused(tokens, ln_gain, ln_bias, w_in, b_in, w_out, b_out, cotangent, cosine, sine):
    n, replicas = lax.axis_size("shard"), lax.axis_size("replica")
    X = max(replicas // 2, 1)
    Y = replicas // X
    L = n // 2
    rows = tokens.shape[0]
    group = rows * n
    depth = D // n
    q = depth // replicas
    head, fc = D // n, FF // n
    head3 = 3 * head
    width = head3 + fc
    both_heads = (group // SEQ_LEN) * (head // HEAD_DIM)
    vmem, dma = pltpu.VMEM, pltpu.SemaphoreType.DMA
    t = n - 2
    most = max(X, Y) - 1
    units = 2 * n + SLOTS
    scratch = {
        "nl": vmem((group, D), bf16), "ct": vmem((group, D), bf16),
        "wi": vmem((D, width), bf16), "wo": vmem((SLOTS * depth, D), bf16),
        "joined": vmem((group, head + fc), bf16), "dproj": vmem((group, width), bf16),
        "flip": vmem((depth, group), bf16),
        "oh": vmem((2, SEQ_LEN, HEAD_DIM), f32), "dq": vmem((2, SEQ_LEN, HEAD_DIM), f32),
        "dk": vmem((2, SEQ_LEN, HEAD_DIM), f32), "dv": vmem((2, SEQ_LEN, HEAD_DIM), f32),
        "g_out": vmem((SLOTS - 1, depth, D), bf16), "g_in": vmem((n, depth, fc), bf16),
        "b_own": vmem((1, width), f32),
        "tmp": vmem((L, rows, D), bf16), "acc": vmem((2, 8, D), f32),
        "v1": vmem((1, width + D), f32), "v1s": vmem((1, width + D), f32), "got1": vmem((replicas - 1, 1, width + D), f32),
        "v2": vmem((1, 2 * D), f32), "v2s": vmem((1, 2 * D), f32), "got2": vmem((replicas - 1, 1, 2 * D), f32),
        "got3": vmem((n - 1, 1, 2 * D), f32),
    }
    for name in ("qh", "kh", "vh", "doh"):
        scratch[name] = vmem((both_heads, SEQ_LEN, HEAD_DIM), bf16)
    for tag, count, wide in (("o", SLOTS, D), ("f", n, fc), ("q", n, head3)):
        a, b = half_of(wide), wide - half_of(wide)
        scratch["r1" + tag + "a"] = vmem((count, X - 1, Y * q, a), bf16)
        scratch["r1" + tag + "b"] = vmem((count, Y - 1, X * q, b), bf16)
        scratch["r2" + tag + "a"] = vmem((count, Y - 1, q, a), bf16)
        scratch["r2" + tag + "b"] = vmem((count, X - 1, q, b), bf16)
    sems = {
        "ag_recv": (2, 2, L), "sib_recv": (2, 2 * L), "ws_recv": (1,), "oz_recv": (SLOTS,), "wz_recv": (t, 2),
        "i_come": (t, 4, most), "i_rest": (t, 4), "o_come": (SLOTS, 2, most), "o_rest": (SLOTS, 2),
        "s1_recv": (units, 2, most), "s2_recv": (units, 2, most), "zi_recv": (units,), "zo_recv": (SLOTS,),
        "a_come": (units, 1 if X == Y else 2, most), "a_rest": (units, 1 if X == Y else 2),
        "ls_recv": (2, L), "lz_recv": (2, 2, L), "vr_recv": (2, replicas - 1), "vl_recv": (n - 1,), "vn_recv": (n - 1,),
        "pool": (POOL,),
    }
    scratch |= {name: dma(shape) for name, shape in sems.items()}
    scratch["own_sem"], scratch["tmp_sem"] = dma((5,)), dma((L,))
    any_space = pl.BlockSpec(memory_space=pl.ANY)
    loaded = {
        "tok": tokens, "gain": ln_gain.reshape(1, D), "bias": ln_bias.reshape(1, D), "b_in": b_in.reshape(1, 3 * D + FF),
        "cot": cotangent, "b_out": b_out.reshape(1, D), "cosine": cosine, "sine": sine,
    }
    scratch |= {name: vmem(value.shape, value.dtype) for name, value in loaded.items()}
    scratch |= {"block_out": vmem((rows, D), bf16), "grad_tokens": vmem((rows, D), bf16)}
    scratch |= {name: vmem((1, D), f32) for name in ("gb_out", "g_gain", "g_bias")}
    scratch["load_sem"], scratch["give_sem"] = dma((len(loaded),)), dma((len(GIVEN),))
    scratch["bias_sem"] = dma((4,))
    in_hbm = pl.BlockSpec(memory_space=pltpu.HBM)
    inputs = {"far_" + name: (value, in_hbm) for name, value in loaded.items()} | {
        "w_in": (w_in, in_hbm), "w_out": (w_out, in_hbm),
    }
    shape = jax.ShapeDtypeStruct
    outputs = {
        "fi": (shape((n, depth, width), bf16), any_space), "fo": (shape((SLOTS, depth, D), bf16), any_space),
        "to_block_out": (shape((rows, D), bf16), in_hbm), "to_grad_tokens": (shape((rows, D), bf16), in_hbm),
        "gb_in": (shape((1, 3 * D + FF), f32), in_hbm), "to_gb_out": (shape((1, D), f32), in_hbm),
        "to_g_gain": (shape((1, D), f32), in_hbm), "to_g_bias": (shape((1, D), f32), in_hbm),
        "sbx": (shape((2, L, rows, D), bf16), any_space), "zbx": (shape((2, 2, L, rows, D), bf16), any_space),
    }
    done = pl.pallas_call(
        functools.partial(fused_kernel, n, replicas, list(inputs) + list(outputs) + list(scratch)),
        out_shape=tuple(out for out, _ in outputs.values()),
        in_specs=[spec for _, spec in inputs.values()],
        out_specs=tuple(spec for _, spec in outputs.values()),
        scratch_shapes=list(scratch.values()),
        compiler_params=pltpu.CompilerParams(collective_id=0, has_side_effects=True, vmem_limit_bytes=63 << 20),
        name="fused",
    )(*[value for value, _ in inputs.values()])
    return {name.removeprefix("to_"): value for name, value in zip(outputs, done, strict=True)}


def widen_kernel(n, names, *refs):
    v = Names(names, refs)
    depth = D // n
    head, fc = D // n, FF // n
    jobs = [("out", i) for i in range(SLOTS)] + [("in", d) for d in range(n)]
    passed = [
        (
            pltpu.make_async_copy(getattr(v, name), getattr(v, "by_" + name), v.pass_sem.at[p, 0]),
            pltpu.make_async_copy(getattr(v, "by_" + name), getattr(v, "to_" + name), v.pass_sem.at[p, 1]),
        )
        for p, name in enumerate(PASSED)
    ]

    def load(j):
        kind, i = jobs[j]
        src, dst = (v.fi.at[i], v.low_in.at[i]) if kind == "in" else (v.fo.at[i], v.low_out.at[i])
        return pltpu.make_async_copy(src, dst, v.load_sem.at[j])

    def stores(j):
        kind, i = jobs[j]
        if kind == "out":
            return [pltpu.make_async_copy(v.wide_out.at[i], v.go.at[pl.ds(i * depth, depth)], v.store_sem.at[j, 0])]
        places = [(part * D + head * i, part * head, head) for part in range(3)] + [(3 * D + fc * i, 3 * head, fc)]
        return [
            pltpu.make_async_copy(
                v.wide_in.at[i, :, pl.ds(src, size)], v.gi.at[:, pl.ds(dst, size)], v.store_sem.at[j, p]
            )
            for p, (dst, src, size) in enumerate(places)
        ]

    for j in range(len(jobs)):
        load(j).start()
    for first, _ in passed:
        first.start()
    for j, (kind, i) in enumerate(jobs):
        load(j).wait()
        low, wide = (v.low_in, v.wide_in) if kind == "in" else (v.low_out, v.wide_out)

        def body(k, low=low, wide=wide, i=i):
            at = rows_at(k * 16, 16)
            wide[i, at, :] = low[i, at, :].astype(f32)

        loop(depth // 16, body)
        for copy in stores(j):
            copy.start()
    for first, then in passed:
        first.wait()
        then.start()
    for j in range(len(jobs)):
        for copy in stores(j):
            copy.wait()
    for _, then in passed:
        then.wait()


PASSED = ("block_out", "grad_tokens", "gb_in", "gb_out", "g_gain", "g_bias")


def widen(results):
    n = lax.axis_size("shard")
    fi, fo = results["fi"], results["fo"]
    depth, width = fi.shape[1], fi.shape[2]
    dma, vmem, shape = pltpu.SemaphoreType.DMA, pltpu.VMEM, jax.ShapeDtypeStruct
    in_hbm = pl.BlockSpec(memory_space=pltpu.HBM)
    inputs = {"fi": fi, "fo": fo} | {name: results[name] for name in PASSED}
    outputs = {"gi": shape((depth, 3 * D + FF), f32), "go": shape((SLOTS * depth, D), f32)} | {
        "to_" + name: shape(results[name].shape, results[name].dtype) for name in PASSED
    }
    scratch = {
        "low_in": vmem((n, depth, width), bf16), "low_out": vmem((SLOTS, depth, D), bf16),
        "wide_in": vmem((n, depth, width), f32), "wide_out": vmem((SLOTS, depth, D), f32),
        "load_sem": dma((n + SLOTS,)), "store_sem": dma((n + SLOTS, 4)), "pass_sem": dma((len(PASSED), 2)),
    } | {"by_" + name: vmem(results[name].shape, results[name].dtype) for name in PASSED}
    names = list(inputs) + list(outputs) + list(scratch)
    done = pl.pallas_call(
        functools.partial(widen_kernel, n, names),
        out_shape=tuple(outputs.values()),
        in_specs=[in_hbm] * len(inputs),
        out_specs=(in_hbm,) * len(outputs),
        scratch_shapes=list(scratch.values()),
        compiler_params=pltpu.CompilerParams(vmem_limit_bytes=60 << 20),
        name="widen",
    )(*inputs.values())
    return dict(zip(outputs, done, strict=True))


def angle_tables():
    lane = np.arange(128) % HEAD_DIM
    frequency = 10000.0 ** (-2.0 * (lane % (ROT // 2)) / ROT)
    angle = np.arange(SEQ_LEN)[:, None] * frequency[None, :]
    turned = (lane < ROT)[None, :]
    return np.where(turned, np.cos(angle), 1.0).astype(np.float32), np.where(turned, np.sin(angle), 0.0).astype(np.float32)


def local(tokens, ln_gain, ln_bias, w_in, b_in, w_out, b_out, cotangent):
    cosine, sine = angle_tables()
    results = fused(tokens, ln_gain, ln_bias, w_in, b_in, w_out, b_out, cotangent, jnp.asarray(cosine), jnp.asarray(sine))
    done = widen(results)
    return (
        done["to_block_out"], done["to_grad_tokens"], done["to_g_gain"].reshape(D), done["to_g_bias"].reshape(D),
        done["gi"], done["to_gb_in"].reshape(3 * D + FF), done["go"], done["to_gb_out"].reshape(D),
    )


def solution(mesh):
    both_axes = P(("replica", "shard"), None)
    return jax.shard_map(
        local,
        mesh=mesh,
        in_specs=(both_axes, P(), P(), P("shard", None), P(), P("shard", None), P(), both_axes),
        out_specs=(both_axes, both_axes, P(), P(), P("shard", None), P(), P("shard", None), P()),
        check_vma=False,
    )
```
